32 devices in a mesh: narrow: 4 (over y, x), wide: 8 (over z, core).
Axes of the slice: x: 2, y: 2, z: 4, core: 2. Of those that a mesh axis runs over, the one named last changes fastest.
Arguments:
- tokens: bfloat16 [8192, 1024], P(('narrow', 'wide')), may hold values from -6 to 6
- attn_gain: float32 [1024], replicated, may hold values from 0.5 to 1.5
- qkv_weights: float32 [3, 1024, 1024], P(None, 'narrow', 'wide'), may hold values from -0.1875 to 0.1875
- out_weight: float32 [1024, 1024], P('narrow', 'wide'), may hold values from -1.75 to 1.75
- rel_bias: float32 [32, 16], replicated, may hold values from -6 to 6
- moe_gain: float32 [1024], replicated, may hold values from 0.5 to 1.5
- router: float32 [1024, 8], P('narrow', 'wide'), may hold values from -0.125 to 0.125
- gate_weight: float32 [4, 8, 1024, 704], P('narrow', 'wide'), may hold values from -0.1875 to 0.1875
- up_weight: float32 [4, 8, 1024, 704], P('narrow', 'wide'), may hold values from -0.1875 to 0.1875
- down_weight: float32 [4, 8, 704, 1024], P('narrow', 'wide'), may hold values from -0.21875 to 0.21875
- expert_ids: int32 [8192, 2], P(('narrow', 'wide')), may hold values from 0 to 7, as said below
- expert_slots: int32 [8192, 2], P(('narrow', 'wide')), may hold values from -1 to 79, as said below
- buckets: int32 [511], replicated, may hold values from 0 to 31, as said below
- upstream: bfloat16 [8192, 1024], P(('narrow', 'wide')), may hold values from -6 to 6
Outputs:
- block_out: bfloat16 [8192, 1024], P(('narrow', 'wide'))
- tokens_grad: bfloat16 [8192, 1024], P(('narrow', 'wide'))
- attn_gain_grad: float32 [1024], replicated
- qkv_grad: float32 [3, 1024, 1024], replicated
- out_weight_grad: float32 [1024, 1024], replicated
- rel_bias_grad: float32 [32, 16], replicated
- moe_gain_grad: float32 [1024], replicated
- router_grad: float32 [1024, 8], replicated
- gate_grad: float32 [4, 8, 1024, 704], P('narrow', 'wide')
- up_grad: float32 [4, 8, 1024, 704], P('narrow', 'wide')
- down_grad: float32 [4, 8, 704, 1024], P('narrow', 'wide')
- qkv_new: float32 [3, 1024, 1024], P(None, 'narrow', 'wide')
- out_weight_step: float32 [1024, 1024], P('narrow', 'wide')
- router_new: float32 [1024, 8], P('narrow', 'wide')
- gate_new: float32 [4, 8, 1024, 704], P('narrow', 'wide')
- up_new: float32 [4, 8, 1024, 704], P('narrow', 'wide')
- down_new: float32 [4, 8, 704, 1024], P('narrow', 'wide')
- qkv_stats: float32 [2, 3, 1024], replicated
- out_stats: float32 [2, 1024], replicated
- router_rows: float32 [1024], replicated
- router_cols: float32 [8], replicated
- expert_sum_stats: float32 [4, 8, 3, 1024], P('narrow', 'wide')
- expert_part_stats: float32 [4, 8, 3, 704], P('narrow', 'wide')
The draws below stay inside these ranges and needn't reach their ends.
Inputs may be any that keep to these rules, and one draw needn't show every extreme that they name: `expert_ids`: each token names two different experts. `expert_slots`: among the pairs of one device's 256 tokens, taken in order of token and then choice, those naming the same expert hold slots 0, 1, 2 and so on; a pair whose slot would be 80 or more holds -1. `buckets`: entry j - i + 255 is the bucket of offset j - i: 0 at offset 0, never falling with the offset's size on either side, under 32 // 2 for offsets of 0 or less and 16 or more for positive ones.
All inputs are finite; a program needn't handle non-finite values.
Results may differ from the reference program's by a relative error of at most 0.02.
Values may be sent and summed in bfloat16 or wider, within the bound.
No kernel may reach another device: no remote copies, remote signals or barrier semaphores. Data moves between devices by JAX's collectives and lax.ppermute only.
A program may use at most 256 MiB of HBM per device.

```python
import math
import jax
import jax.numpy as jnp
from jax import lax

D = 1024
HEADS = 16
HEAD = 64
FF = 2816
BUCKETS = 32
SPLIT = 4
TOK_DEV = 256
GROUPS = 4
PLACES = 2
SPECIALIST_TOTAL = 8
FFP = 704
CAP = 80
ROWS = 2560
TOKENS = 8192


def routing_pairs(key):
    base_key = jax.random.fold_in(key, 7)
    ordered_priority_list = jax.random.permutation(jax.random.fold_in(base_key, 1), SPECIALIST_TOTAL)
    added_logit_shift = 160 // (ordered_priority_list + 1)
    jitter_perturbation = jax.random.randint(jax.random.fold_in(base_key, 2), (TOKENS, SPECIALIST_TOTAL), 0, 1024)
    distinct_elements = (jitter_perturbation + added_logit_shift[None, :]) * SPECIALIST_TOTAL + jnp.arange(SPECIALIST_TOTAL)[None, :]
    top_values, chosen = lax.top_k(distinct_elements, 2)
    return chosen.astype(jnp.int32)


def draw_expert_ids(key, part):
    return routing_pairs(key)


def draw_expert_slots(key, part):
    chosen = routing_pairs(key)
    per_device = chosen.reshape(TOKENS // TOK_DEV, TOK_DEV * 2)
    hit_table = (per_device[:, :, None] == jnp.arange(SPECIALIST_TOTAL)[None, None, :]).astype(jnp.int32)
    before = jnp.cumsum(hit_table, axis=1) - hit_table
    slot_ids = jnp.sum(before * hit_table, axis=2)
    slot_ids = jnp.where(slot_ids < CAP, slot_ids, -1)
    return slot_ids.reshape(TOKENS, 2).astype(jnp.int32)


def draw_buckets(key, part):
    half_count = BUCKETS // 2
    boundaries = jnp.sort(jax.random.randint(jax.random.fold_in(key, 3), (half_count - 1,), 1, TOK_DEV))
    offset_ids = jnp.arange(2 * TOK_DEV - 1) - (TOK_DEV - 1)
    distance = jnp.abs(offset_ids)
    level_ids = jnp.sum((boundaries[None, :] <= distance[:, None]).astype(jnp.int32), axis=1)
    return (level_ids + half_count * (offset_ids > 0).astype(jnp.int32)).astype(jnp.int32)


def level_of(own_key, extent, cuts, least, top_value):
    factor_of = 1.0
    for axis_at, blocks in cuts:
        draws = jax.random.uniform(jax.random.fold_in(jax.random.fold_in(own_key, 6), axis_at), (blocks,), jnp.float32, least / len(cuts), top_value / len(cuts))
        factor_of = factor_of * jnp.repeat(jnp.exp(draws), extent[axis_at] // blocks).reshape((-1,) + (1,) * (len(extent) - 1 - axis_at))
    return factor_of


def normal_values(stream_key, extent, deviation, bound, split=(), kind=jnp.bfloat16):
    entries = jax.random.normal(stream_key, extent, jnp.float32) * deviation
    if len(split) > 0:
        entries = level_of(stream_key, extent, split, -0.22, 0.18) * entries
    return jnp.clip(entries, min=-bound, max=bound).astype(kind)


def setup_inputs(seed: int = 0) -> dict:
    splits = jax.random.split(jax.random.key(seed), 15)
    tokens = normal_values(splits[0], (TOKENS, D), 1.0, 6.0, ((0, 32),))
    attn_gain = jnp.clip(1.0 + 0.1 * jax.random.normal(splits[1], (D,), jnp.float32), 0.5, 1.5)
    qkv_weights = normal_values(splits[2], (3, D, D), D ** -0.5, 0.1875, ((1, 4), (2, 8)), jnp.float32)
    out_weight = normal_values(splits[3], (D, D), (max(1, 3 * D // TOK_DEV)) ** -0.5, 1.75, ((0, 4), (1, 8)), jnp.float32)
    rel_bias = normal_values(splits[4], (BUCKETS, HEADS), 1.0, 6.0, (), jnp.float32)
    moe_gain = jnp.clip(1.0 + 0.1 * jax.random.normal(splits[5], (D,), jnp.float32), 0.5, 1.5)
    router = normal_values(splits[6], (D, SPECIALIST_TOTAL), (2 * D) ** -0.5, 0.125, ((0, 4), (1, 8)), jnp.float32)
    gate_weight = normal_values(splits[7], (GROUPS, PLACES * SPLIT, D, FFP), D ** -0.5, 0.1875, ((0, 4), (1, 8)), jnp.float32)
    up_weight = normal_values(splits[8], (GROUPS, PLACES * SPLIT, D, FFP), D ** -0.5, 0.1875, ((0, 4), (1, 8)), jnp.float32)
    down_weight = normal_values(splits[9], (GROUPS, PLACES * SPLIT, FFP, D), (FF // 4) ** -0.5, 0.21875, ((0, 4), (1, 8)), jnp.float32)
    expert_ids = draw_expert_ids(jax.random.fold_in(splits[14], 71), 0)
    expert_slots = draw_expert_slots(jax.random.fold_in(splits[14], 71), 0)
    buckets = draw_buckets(jax.random.fold_in(splits[14], 71), 0)
    upstream = normal_values(splits[13], (TOKENS, D), 1.0, 6.0, ((0, 32),))
    return dict(tokens=tokens, attn_gain=attn_gain, qkv_weights=qkv_weights, out_weight=out_weight, rel_bias=rel_bias, moe_gain=moe_gain, router=router, gate_weight=gate_weight, up_weight=up_weight, down_weight=down_weight, expert_ids=expert_ids, expert_slots=expert_slots, buckets=buckets, upstream=upstream)


@jax.custom_vjp
def low(v):
    return lax.optimization_barrier(v.astype(jnp.bfloat16)).astype(jnp.float32)

@jax.custom_vjp
def low_back(v):
    return v

def low_keep(v):
    return (low(v), None)

def low_pass(kept, grad):
    return (grad,)

def back_keep(v):
    return (v, None)

def back_low(kept, grad):
    return (low(grad),)
low.defvjp(low_keep, low_pass)
low_back.defvjp(back_keep, back_low)
NORM_EPS = 1e-06
STAT_EPS = 1e-06
STEP_RATE = 0.01

def round_both(values):
    return low_back(low(values))

def norm_apply(values, gain):
    factor = lax.rsqrt(lax.optimization_barrier(jnp.mean(values * values, axis=-1, keepdims=True)) + NORM_EPS)
    return values * factor * gain

def adafactor_step(gradient, row_stats, col_stats, mean_rows):
    return STEP_RATE * gradient / jnp.sqrt(row_stats[..., :, None] * col_stats[..., None, :] / mean_rows[..., None, None])

def factored(weight, gradient, row_stats, col_stats, mean_rows):
    return weight - adafactor_step(gradient, row_stats, col_stats, mean_rows)

def per_expert(weights):
    shaped = weights.reshape((GROUPS, PLACES, SPLIT) + weights.shape[2:])
    return jnp.transpose(shaped, (1, 0, 2, 3, 4)).reshape((SPECIALIST_TOTAL, SPLIT) + weights.shape[2:])

def reference(tokens, attn_gain, qkv_weights, out_weight, rel_bias, moe_gain, router, gate_weight, up_weight, down_weight, expert_ids, expert_slots, buckets, upstream):
    length = TOK_DEV
    score_scale = HEAD ** (-0.5)
    sequences = TOKENS // length
    per_step = math.gcd(sequences, max(1, 4096 // length))
    steps_count = sequences // per_step
    positions = jnp.arange(length, dtype=jnp.int32)
    offsets = positions[None, :] - positions[:, None] + length - 1
    bias_index = buckets[offsets]
    token_ids = jnp.arange(TOKENS, dtype=jnp.int32)
    source = token_ids // length
    kept_pairs = expert_slots >= 0
    flat_rows = jnp.where(kept_pairs, expert_ids * ROWS + source[:, None] * CAP + expert_slots, SPECIALIST_TOTAL * ROWS).astype(jnp.int32)
    inverse = jnp.full((SPECIALIST_TOTAL * ROWS + 1,), TOKENS, jnp.int32).at[flat_rows.reshape(-1)].set(jnp.repeat(token_ids, 2).astype(jnp.int32))
    inverse = inverse[:-1].reshape(SPECIALIST_TOTAL, ROWS)
    safe_rows = jnp.minimum(flat_rows, SPECIALIST_TOTAL * ROWS - 1).astype(jnp.int32)
    keep_float = kept_pairs.astype(jnp.float32)

    def forward(inputs, gain_a, qkv_w, out_w, bias_w, gain_m, router_w, gate_w, up_w, down_w):
        normed_in = low(norm_apply(inputs, gain_a))
        projected = round_both(jnp.einsum('td,kde->kte', normed_in, low(qkv_w), precision=lax.Precision.HIGHEST))
        shaped = projected.reshape(3, steps_count, per_step, length, HEADS, HEAD)
        bias_full = jnp.transpose(bias_w[bias_index], (2, 0, 1))

        def attend(pieces):
            query_heads, key_heads, value_heads = pieces
            raw_scores = jnp.einsum('gqhd,gkhd->ghqk', query_heads, key_heads, precision=lax.Precision.HIGHEST)
            scores = low_back(raw_scores * score_scale + bias_full[None])
            attn_probs = low(jax.nn.softmax(scores, axis=-1))
            return jnp.einsum('ghqk,gkhd->gqhd', attn_probs, value_heads, precision=lax.Precision.HIGHEST)
        attended = lax.map(jax.checkpoint(attend), (shaped[0], shaped[1], shaped[2]))
        attended = round_both(attended.reshape(TOKENS, D))
        hidden_x1 = inputs + low_back(jnp.dot(attended, low(out_w), precision=lax.Precision.HIGHEST))
        moe_input = low(norm_apply(hidden_x1, gain_m))
        logits = low_back(jnp.dot(moe_input, low(router_w), precision=lax.Precision.HIGHEST))
        picked = jnp.take_along_axis(logits, expert_ids, axis=1)
        gate_values = jax.nn.softmax(picked, axis=1)
        moe_pad = jnp.concatenate([moe_input, jnp.zeros((1, D), jnp.float32)], axis=0)

        def expert_apply(pieces):
            index_rows, gate_e, up_e, down_e = pieces
            expert_rows = moe_pad[index_rows]
            running = jnp.zeros((ROWS, D), jnp.float32)
            for portion in range(SPLIT):
                part_rows = low_back(expert_rows)
                gate_pre = low_back(jnp.dot(part_rows, low(gate_e[portion]), precision=lax.Precision.HIGHEST))
                up_pre = low_back(jnp.dot(part_rows, low(up_e[portion]), precision=lax.Precision.HIGHEST))
                hidden = low(jax.nn.gelu(gate_pre, approximate=True) * up_pre)
                running = running + round_both(jnp.dot(hidden, low(down_e[portion]), precision=lax.Precision.HIGHEST))
            return running
        produced = lax.map(jax.checkpoint(expert_apply), (inverse, per_expert(gate_w), per_expert(up_w), per_expert(down_w)))
        flat_out = produced.reshape(SPECIALIST_TOTAL * ROWS, D)
        moe_sum = jnp.zeros((TOKENS, D), jnp.float32)
        for choice_index in range(2):
            weight_col = (gate_values[:, choice_index] * keep_float[:, choice_index])[:, None]
            moe_sum = moe_sum + weight_col * flat_out[safe_rows[:, choice_index]]
        return hidden_x1 + moe_sum
    primals = (tokens.astype(jnp.float32), attn_gain, qkv_weights, out_weight, rel_bias, moe_gain, router, gate_weight, up_weight, down_weight)
    result, pullback = jax.vjp(forward, *primals)
    grads = pullback(upstream.astype(jnp.float32))
    input_g, gain_a_g, qkv_g, out_g, bias_g, gain_m_g, router_g, gate_g, up_g, down_g = grads
    attn_all = jnp.concatenate([qkv_g, out_g[None]], axis=0)
    focus_squared_mean = attn_all * attn_all
    attn_rows = lax.optimization_barrier(jnp.mean(focus_squared_mean, axis=2)) + STAT_EPS
    attn_cols = lax.optimization_barrier(jnp.mean(focus_squared_mean, axis=1)) + STAT_EPS
    attn_means = lax.optimization_barrier(jnp.mean(attn_rows, axis=1))
    qkv_new = factored(qkv_weights, qkv_g, attn_rows[:3], attn_cols[:3], attn_means[:3])
    out_step = adafactor_step(out_g, attn_rows[3], attn_cols[3], attn_means[3])
    qkv_stats = jnp.stack([attn_rows[:3], attn_cols[:3]], axis=0)
    out_stats = jnp.stack([attn_rows[3], attn_cols[3]], axis=0)
    router_sq = router_g * router_g
    router_rows = lax.optimization_barrier(jnp.mean(router_sq, axis=1)) + STAT_EPS
    router_cols = lax.optimization_barrier(jnp.mean(router_sq, axis=0)) + STAT_EPS
    router_new = factored(router, router_g, router_rows, router_cols, jnp.mean(router_rows))

    def wide_matrix(weight, gradient):
        shaped_g = gradient.reshape(GROUPS, PLACES, SPLIT, D, FFP)
        shaped_w = weight.reshape(GROUPS, PLACES, SPLIT, D, FFP)
        squares = shaped_g * shaped_g
        row_stats = lax.optimization_barrier(jnp.sum(squares, axis=(2, 4))) / FF + STAT_EPS
        col_stats = lax.optimization_barrier(jnp.mean(squares, axis=3)) + STAT_EPS
        mean_rows = lax.optimization_barrier(jnp.mean(row_stats, axis=2))
        denom = jnp.sqrt(row_stats[:, :, None, :, None] * col_stats[:, :, :, None, :] / mean_rows[:, :, None, None, None])
        updated = shaped_w - STEP_RATE * shaped_g / denom
        return (updated.reshape(weight.shape), row_stats, col_stats)
    gate_new, gate_rows, gate_cols = wide_matrix(gate_weight, gate_g)
    up_new, up_rows, up_cols = wide_matrix(up_weight, up_g)
    down_shaped = down_g.reshape(GROUPS, PLACES, SPLIT, FFP, D)
    down_sq = down_shaped * down_shaped
    down_rows = lax.optimization_barrier(jnp.mean(down_sq, axis=4)) + STAT_EPS
    down_cols = lax.optimization_barrier(jnp.sum(down_sq, axis=(2, 3))) / FF + STAT_EPS
    down_mean = lax.optimization_barrier(jnp.mean(down_rows, axis=(2, 3)))
    down_denom = jnp.sqrt(down_rows[:, :, :, :, None] * down_cols[:, :, None, None, :] / down_mean[:, :, None, None, None])
    down_new = (down_weight.reshape(GROUPS, PLACES, SPLIT, FFP, D) - STEP_RATE * down_shaped / down_denom).reshape(down_weight.shape)
    sum_stats = jnp.stack([gate_rows, up_rows, down_cols], axis=2)
    sum_stats = jnp.broadcast_to(sum_stats[:, :, None], (GROUPS, PLACES, SPLIT, 3, D)).reshape(GROUPS, PLACES * SPLIT, 3, D)
    part_stats = jnp.stack([gate_cols, up_cols, down_rows], axis=3).reshape(GROUPS, PLACES * SPLIT, 3, FFP)
    return (result.astype(jnp.bfloat16), input_g.astype(jnp.bfloat16), gain_a_g, qkv_g, out_g, bias_g, gain_m_g, router_g, gate_g, up_g, down_g, qkv_new, out_step, router_new, gate_new, up_new, down_new, qkv_stats, out_stats, router_rows, router_cols, sum_stats, part_stats)
```

```python
import functools

import jax
import jax.numpy as jnp
from jax import lax
from jax.experimental import pallas as pl
from jax.experimental.pallas import tpu as pltpu
from jax.sharding import PartitionSpec as P

NORM_EPS = 1e-06
STAT_EPS = 1e-06
STEP_RATE = 0.01
LANES = 128
GELU_C = 0.7978845608028654
GELU_A = 0.044715
BF = jnp.bfloat16
F32 = jnp.float32
VMEM_LIMIT = 60 * 1024 * 1024
NN = (((1,), (0,)), ((), ()))
NT = (((1,), (1,)), ((), ()))
TN = (((0,), (0,)), ((), ()))


def mm(a, b, dims=NN):
    return lax.dot_general(a, b, dims, preferred_element_type=F32)


def from_partner(value, hop):
    axis, bit = hop
    mask = 2**bit
    pairs = [(source, source ^ mask) for source in range(lax.axis_size(axis))]
    return lax.ppermute(value, axis, pairs)


def hop_orders(groups, wide_count):
    narrow = [("narrow", b) for b in range(groups.bit_length() - 1)]
    wide = [("wide", b) for b in range(1, wide_count.bit_length() - 1)]
    far, near = wide[1:][::-1], wide[:1]
    core = [("wide", 0)]
    return (
        far + narrow + near + core,
        far + near + narrow + core,
        far + narrow[1:] + near + narrow[:1] + core,
    )


def block_slots(order, groups, wide_count):
    n_ids = jnp.arange(groups, dtype=jnp.int32)[:, None]
    w_ids = 2 * jnp.arange(wide_count // 2, dtype=jnp.int32)[None, :]
    slots = jnp.zeros((groups, wide_count // 2), jnp.int32)
    for stage, (axis, bit) in enumerate(order[:-1]):
        ids = n_ids if axis == "narrow" else w_ids
        differs = ((ids ^ lax.axis_index(axis)) >> bit) & 1
        slots = slots | (differs << stage)
    return slots


def gather_blocks(block, order):
    blocks = block[None]
    for hop in order[:-1]:
        blocks = jnp.concatenate([blocks, from_partner(blocks, hop)], axis=0)
    return blocks, from_partner(blocks, order[-1])


def scatter_sum(keep, send, order):
    total = keep + from_partner(send, order[-1]).astype(F32)
    for hop in order[:-1][::-1]:
        half = total.shape[0] // 2
        total = total[:half] + from_partner(total[half:].astype(BF), hop).astype(F32)
    return total[0]


def cube_sum(value, hops):
    for hop in hops:
        value = value + from_partner(value, hop)
    return value


def as_matrix(own, other, slots, my_core):
    groups, half_wide = slots.shape
    both = jnp.stack([jnp.where(my_core == 0, own, other), jnp.where(my_core == 0, other, own)], 1)
    picked = jnp.take(both, slots.reshape(-1), axis=0)
    rows, cols = own.shape[1:]
    picked = picked.reshape(groups, half_wide, 2, rows, cols)
    return jnp.transpose(picked, (0, 3, 1, 2, 4)).reshape(groups * rows, half_wide * 2 * cols)


def from_matrix(matrix, groups, half_wide):
    lead = matrix.shape[:-2]
    rows, cols = matrix.shape[-2] // groups, matrix.shape[-1] // (2 * half_wide)
    shaped = matrix.reshape(lead + (groups, rows, half_wide, 2, cols))
    k = len(lead)
    order = tuple(range(k)) + (k, k + 2, k + 3, k + 1, k + 4)
    return jnp.transpose(shaped, order)


def gelu_tanh(values):
    return jax.nn.gelu(values, approximate=True)


def adafactor_step(gradient, row_stats, col_stats, mean_rows):
    return (
        STEP_RATE
        * gradient
        / jnp.sqrt(row_stats[..., :, None] * col_stats[..., None, :] / mean_rows[..., None, None])
    )


def factored(weight, gradient, row_stats, col_stats, mean_rows):
    return weight - adafactor_step(gradient, row_stats, col_stats, mean_rows)


def vmem():
    return pl.BlockSpec(memory_space=pltpu.VMEM)


def smem():
    return pl.BlockSpec(memory_space=pltpu.SMEM)


def params():
    return pltpu.CompilerParams(vmem_limit_bytes=VMEM_LIMIT)


def lane_masks(head_dim):
    heads = LANES // head_dim
    ids = lax.broadcasted_iota(jnp.int32, (1, LANES), 1) // head_dim
    return [ids == i for i in range(heads)]


def attend_body(
    table_ref, tokens_ref, gain_ref, bias_ref,
    own_q, own_k, own_v, far_q, far_k, far_v,
    normed_ref, heads_ref, probs_ref, attended_ref,
    *, groups, pairs, head_dim,
):
    length, features = tokens_ref.shape
    rows = features // groups
    x = tokens_ref[...].astype(F32)
    factor = lax.rsqrt(jnp.mean(x * x, axis=-1, keepdims=True) + NORM_EPS)
    normed_ref[...] = (x * factor * gain_ref[...]).astype(BF)
    core = table_ref[0]

    def project(w2, carry):
        for m, (own, far) in enumerate(((own_q, far_q), (own_k, far_k), (own_v, far_v))):
            total = None
            for n in range(groups):
                at = table_ref[1 + (m * groups + n) * pairs + w2]
                block = jnp.concatenate([own[at], far[at]], axis=1)
                part = mm(normed_ref[:, n * rows : (n + 1) * rows], block)
                total = part if total is None else total + part
            total = total.astype(BF)
            heads_ref[m, 2 * w2 + core] = total[:, :LANES]
            heads_ref[m, 2 * w2 + 1 - core] = total[:, LANES:]
        return carry

    lax.fori_loop(0, pairs, project, 0)
    masks = lane_masks(head_dim)
    scale = head_dim**-0.5

    def attend(w, carry):
        q, k, v = heads_ref[0, w], heads_ref[1, w], heads_ref[2, w]
        mixed = jnp.zeros((length, LANES), F32)
        for i, mask in enumerate(masks):
            head = w * len(masks) + i
            raw = mm(jnp.where(mask, q, jnp.zeros_like(q)), k, NT)
            line = jnp.broadcast_to(bias_ref[pl.ds(head, 1), :], (length, 2 * length))
            bias = pltpu.roll(line, length + 1, 1, stride=1, stride_axis=0)[:, :length]
            scores = raw * scale + bias
            top = jnp.max(scores, axis=-1, keepdims=True)
            grown = jnp.exp(scores - top)
            probs = grown / jnp.sum(grown, axis=-1, keepdims=True)
            probs_ref[head] = probs
            mixed = jnp.where(mask, mm(probs.astype(BF), v), mixed)
        attended_ref[w] = mixed.astype(BF)
        return carry

    lax.fori_loop(0, 2 * pairs, attend, 0)


def attend_call(table, tokens, gain, bias_table, gathered, groups, head_dim):
    length, features = tokens.shape
    pairs = features // (2 * LANES)
    head_count = features // head_dim
    owns = [g[0] for g in gathered]
    fars = [g[1] for g in gathered]
    body = functools.partial(attend_body, groups=groups, pairs=pairs, head_dim=head_dim)
    return pl.pallas_call(
        body,
        in_specs=[smem()] + [vmem()] * 9,
        out_specs=[vmem()] * 4,
        out_shape=[
            jax.ShapeDtypeStruct((length, features), BF),
            jax.ShapeDtypeStruct((3, 2 * pairs, length, LANES), BF),
            jax.ShapeDtypeStruct((head_count, length, length), F32),
            jax.ShapeDtypeStruct((2 * pairs, length, LANES), BF),
        ],
        compiler_params=params(),
        name="attend",
    )(table, tokens, gain.reshape(1, features), bias_table, *owns, *fars)


def attend_back_body(
    table_ref, normed_ref, heads_ref, probs_ref, grad_ref,
    keep_ref, send_ref, dheads_ref, diag_ref,
    *, groups, pairs, head_dim,
):
    length, features = normed_ref.shape
    rows = features // groups
    masks = lane_masks(head_dim)
    scale = head_dim**-0.5

    def back(w, carry):
        q, k, v = heads_ref[0, w], heads_ref[1, w], heads_ref[2, w]
        da = grad_ref[w]
        dq = jnp.zeros((length, LANES), F32)
        dk, dv = dq, dq
        for i, mask in enumerate(masks):
            head = w * len(masks) + i
            probs = probs_ref[head]
            dp = mm(jnp.where(mask, da, jnp.zeros_like(da)), v, NT)
            spread = jnp.sum(probs * dp, axis=-1, keepdims=True)
            ds = (probs * (dp - spread)).astype(BF)
            dq = jnp.where(mask, mm(ds, k), dq)
            dk = jnp.where(mask, mm(ds, q, TN), dk)
            dv = jnp.where(mask, mm(probs.astype(BF), da, TN), dv)
            wide_ds = jnp.concatenate([ds.astype(F32), jnp.zeros((length, length), F32)], axis=1)
            diag = jnp.zeros((8, 2 * length), F32)
            for g in range(length // 8):
                diag = diag + pltpu.roll(wide_ds[8 * g : 8 * g + 8], length - 1 - 8 * g, 1)
            diag_ref[head] = diag
        dheads_ref[0, w] = (dq * scale).astype(BF)
        dheads_ref[1, w] = (dk * scale).astype(BF)
        dheads_ref[2, w] = dv.astype(BF)
        return carry

    lax.fori_loop(0, 2 * pairs, back, 0)
    core = table_ref[0]

    def weigh(w2, carry):
        for m in range(3):
            both = jnp.concatenate(
                [dheads_ref[m, 2 * w2 + core], dheads_ref[m, 2 * w2 + 1 - core]], axis=1
            )
            for n in range(groups):
                at = table_ref[1 + (m * groups + n) * pairs + w2]
                block = mm(normed_ref[:, n * rows : (n + 1) * rows], both, TN)
                keep_ref[m, at] = block[:, :LANES]
                send_ref[m, at] = block[:, LANES:].astype(BF)
        return carry

    lax.fori_loop(0, pairs, weigh, 0)


def attend_back_call(table, normed, heads, probs, attended_grad, groups, head_dim):
    length, features = normed.shape
    pairs = features // (2 * LANES)
    head_count = features // head_dim
    rows = features // groups
    body = functools.partial(attend_back_body, groups=groups, pairs=pairs, head_dim=head_dim)
    return pl.pallas_call(
        body,
        in_specs=[smem()] + [vmem()] * 4,
        out_specs=[vmem()] * 4,
        out_shape=[
            jax.ShapeDtypeStruct((3, groups * pairs, rows, LANES), F32),
            jax.ShapeDtypeStruct((3, groups * pairs, rows, LANES), BF),
            jax.ShapeDtypeStruct((3, 2 * pairs, length, LANES), BF),
            jax.ShapeDtypeStruct((head_count, 8, 2 * length), F32),
        ],
        compiler_params=params(),
        name="attend_back",
    )(table, normed, heads, probs, attended_grad)


def tokens_back_body(
    table_ref, tokens_ref, gain_ref, x1_grad_ref, dheads_ref,
    own_q, own_k, own_v, far_q, far_k, far_v,
    out_ref, gain_out_ref, acc_ref,
    *, groups, pairs,
):
    length, features = tokens_ref.shape
    rows = features // groups
    core = table_ref[0]
    for n in range(groups):

        def step(w2, total):
            for m, (own, far) in enumerate(((own_q, far_q), (own_k, far_k), (own_v, far_v))):
                at = table_ref[1 + (m * groups + n) * pairs + w2]
                both = jnp.concatenate(
                    [dheads_ref[m, 2 * w2 + core], dheads_ref[m, 2 * w2 + 1 - core]], axis=1
                )
                total = total + mm(both, jnp.concatenate([own[at], far[at]], axis=1), NT)
            return total

        total = lax.fori_loop(0, pairs, step, jnp.zeros((length, rows), F32))
        acc_ref[:, n * rows : (n + 1) * rows] = total
    x = tokens_ref[...].astype(F32)
    factor = lax.rsqrt(jnp.mean(x * x, axis=-1, keepdims=True) + NORM_EPS)
    hat = x * factor
    grad = acc_ref[...]
    gain_out_ref[...] = jnp.sum(grad * hat, axis=0, keepdims=True)
    scaled = grad * gain_ref[...]
    inner = jnp.mean(scaled * hat, axis=-1, keepdims=True)
    out_ref[...] = (x1_grad_ref[...] + factor * (scaled - hat * inner)).astype(BF)


def tokens_back_call(table, tokens, gain, x1_grad, dheads, gathered, groups):
    length, features = tokens.shape
    pairs = features // (2 * LANES)
    owns = [g[0] for g in gathered]
    fars = [g[1] for g in gathered]
    return pl.pallas_call(
        functools.partial(tokens_back_body, groups=groups, pairs=pairs),
        in_specs=[smem()] + [vmem()] * 10,
        out_specs=[vmem()] * 2,
        out_shape=[
            jax.ShapeDtypeStruct((length, features), BF),
            jax.ShapeDtypeStruct((1, features), F32),
        ],
        scratch_shapes=[pltpu.VMEM((length, features), F32)],
        compiler_params=params(),
        name="tokens_back",
    )(table, tokens, gain.reshape(1, features), x1_grad, dheads, *owns, *fars)


def expert_body(
    expert_ref, x_ref, up_ref, router_ref, gate_w, up_w, down_w,
    y_ref, dx_ref, hidden_ref, dgate_ref, dup_ref, dy_ref,
):
    features = x_ref.shape[1]
    x = x_ref[...]
    logits = mm(x, router_ref[...])
    lane = lax.broadcasted_iota(jnp.int32, logits.shape, 1)
    other_id = up_ref[:, features : features + 1].astype(jnp.int32)
    mine = jnp.sum(jnp.where(lane == expert_ref[0], logits, 0.0), axis=1, keepdims=True)
    other = jnp.sum(jnp.where(lane == other_id, logits, 0.0), axis=1, keepdims=True)
    top = jnp.maximum(mine, other)
    mine_e = jnp.exp(mine - top)
    gate = mine_e / (mine_e + jnp.exp(other - top))
    dy = (gate * up_ref[:, :features].astype(F32)).astype(BF)
    dy_ref[...] = dy
    g = mm(x, gate_w[...])
    u = mm(x, up_w[...])
    t = jnp.tanh(GELU_C * (g + GELU_A * g * g * g))
    act = 0.5 * g * (1.0 + t)
    hidden = (act * u).astype(BF)
    hidden_ref[...] = hidden
    y_ref[...] = mm(hidden, down_w[...]).astype(BF)
    dh = mm(dy, down_w[...], NT)
    slope = 0.5 * (1.0 + t) + 0.5 * g * (1.0 - t * t) * (GELU_C * (1.0 + 3.0 * GELU_A * g * g))
    dg = (dh * u * slope).astype(BF)
    du = (dh * act).astype(BF)
    dgate_ref[...] = dg
    dup_ref[...] = du
    dx_ref[...] = (mm(dg, gate_w[...], NT) + mm(du, up_w[...], NT)).astype(BF)


def row_block(rows):
    for size in (256, 320, 160, 128, 64, 32, 16):
        if rows % size == 0:
            return size
    return rows


def expert_call(expert, x, upstream, router, gate_w, up_w, down_w):
    rows, features = x.shape
    size = row_block(rows)
    wide = gate_w.shape[1]

    def rows_spec(cols):
        return pl.BlockSpec((size, cols), lambda i, e: (i, 0))

    def whole(arr):
        return pl.BlockSpec(arr.shape, lambda i, e: (0, 0))

    return pl.pallas_call(
        expert_body,
        grid_spec=pltpu.PrefetchScalarGridSpec(
            num_scalar_prefetch=1,
            grid=(rows // size,),
            in_specs=[
                rows_spec(features), rows_spec(upstream.shape[1]),
                whole(router), whole(gate_w), whole(up_w), whole(down_w),
            ],
            out_specs=[
                rows_spec(features), rows_spec(features),
                rows_spec(wide), rows_spec(wide), rows_spec(wide), rows_spec(features),
            ],
        ),
        out_shape=[
            jax.ShapeDtypeStruct((rows, features), BF),
            jax.ShapeDtypeStruct((rows, features), BF),
            jax.ShapeDtypeStruct((rows, wide), BF),
            jax.ShapeDtypeStruct((rows, wide), BF),
            jax.ShapeDtypeStruct((rows, wide), BF),
            jax.ShapeDtypeStruct((rows, features), BF),
        ],
        compiler_params=params(),
        name="expert",
    )(expert, x, upstream, router, gate_w, up_w, down_w)


def expert_grad_body(xa, xb, dya, dyb, ha, hb, ga, gb, ua, ub, gate_ref, up_ref, down_ref):
    width = gate_ref.shape[1]
    gate_ref[...] = (mm(xa[...], ga[...], TN) + mm(xb[...], gb[...], TN))[:, :width]
    up_ref[...] = (mm(xa[...], ua[...], TN) + mm(xb[...], ub[...], TN))[:, :width]
    down_ref[...] = (mm(ha[...], dya[...], TN) + mm(hb[...], dyb[...], TN))[:width]


def expert_grad_call(xs, dys, hs, gs, us, width):
    rows, features = xs[0].shape
    padded = hs[0].shape[1]
    size = 256
    cols = pl.BlockSpec((rows, size), lambda i: (0, i))
    whole = pl.BlockSpec((rows, padded), lambda i: (0, 0))
    return pl.pallas_call(
        expert_grad_body,
        grid=(features // size,),
        in_specs=[cols] * 4 + [whole] * 6,
        out_specs=[
            pl.BlockSpec((size, width), lambda i: (i, 0)),
            pl.BlockSpec((size, width), lambda i: (i, 0)),
            pl.BlockSpec((width, size), lambda i: (0, i)),
        ],
        out_shape=[
            jax.ShapeDtypeStruct((features, width), F32),
            jax.ShapeDtypeStruct((features, width), F32),
            jax.ShapeDtypeStruct((width, features), F32),
        ],
        compiler_params=params(),
        name="expert_grad",
    )(*xs, *dys, *hs, *gs, *us)


def spread_body(table_ref, *refs, groups, pairs, count):
    owns, fars = refs[:count], refs[count : 2 * count]
    grads, row_ref, col_ref = refs[2 * count : 3 * count], refs[3 * count], refs[3 * count + 1]
    core = table_ref[0]
    rows = owns[0].shape[1]
    row_ref[...] = jnp.zeros_like(row_ref)
    for m in range(count):

        def column(w2, carry, m=m):
            for j, source in enumerate((owns[m], fars[m])):
                w = 2 * w2 + (core if j == 0 else 1 - core)
                total = jnp.zeros((1, LANES), F32)
                for n in range(groups):
                    at = table_ref[1 + (m * groups + n) * pairs + w2]
                    block = source[at].astype(F32)
                    place = pl.multiple_of(w * LANES, LANES)
                    grads[m][n * rows : (n + 1) * rows, pl.ds(place, LANES)] = block
                    square = block * block
                    total = total + jnp.sum(square, axis=0, keepdims=True)
                    row_ref[m, n * rows : (n + 1) * rows, :] += square
                col_ref[m, w] = total
            return carry

        lax.fori_loop(0, pairs, column, 0)


def spread_call(table, gathered, groups, features):
    pairs = features // (2 * LANES)
    count = len(gathered)
    owns = [g[0] for g in gathered]
    fars = [g[1] for g in gathered]
    out = pl.pallas_call(
        functools.partial(spread_body, groups=groups, pairs=pairs, count=count),
        in_specs=[smem()] + [vmem()] * (2 * count),
        out_specs=[vmem()] * (count + 2),
        out_shape=[jax.ShapeDtypeStruct((features, features), F32)] * count
        + [
            jax.ShapeDtypeStruct((count, features, LANES), F32),
            jax.ShapeDtypeStruct((count, 2 * pairs, 1, LANES), F32),
        ],
        compiler_params=params(),
        name="spread",
    )(table, *owns, *fars)
    row_sums = jnp.sum(out[count], axis=2)
    col_sums = out[count + 1].reshape(count, features)
    return out[:count], row_sums, col_sums


def on_device(
    tokens,
    attn_gain,
    qkv_weights,
    out_weight,
    rel_bias,
    moe_gain,
    router,
    gate_weight,
    up_weight,
    down_weight,
    expert_ids,
    expert_slots,
    buckets,
    upstream,
):
    length, features = tokens.shape
    bucket_count, head_count = rel_bias.shape
    head_dim = features // head_count
    groups = lax.axis_size("narrow")
    wide_count = lax.axis_size("wide")
    my_narrow = lax.axis_index("narrow")
    my_wide = lax.axis_index("wide")
    my_core = my_wide % 2
    part_width = gate_weight.shape[3]
    experts = router.shape[1] * wide_count
    places = experts // groups
    split_parts = wide_count // places
    capacity = (10 * length // experts + 3) // 4
    half_cap = capacity // 2
    slot_total = experts * capacity
    row_count, col_count = qkv_weights.shape[1:]
    half_wide = wide_count // 2
    orders = hop_orders(groups, wide_count)
    all_hops = orders[0]
    slots = [block_slots(order, groups, wide_count) for order in orders]
    direct = col_count % LANES == 0
    pairs = features // (2 * LANES)
    if direct:
        core_entry, tables = my_core, slots
    else:
        core_entry = jnp.int32(0)
        tables = [jnp.arange(groups * pairs, dtype=jnp.int32)] * 3

    def table_of(items):
        return jnp.concatenate(
            [jnp.reshape(core_entry, (1,)).astype(jnp.int32)] + [t.reshape(-1) for t in items]
        )

    qkv_table = table_of(tables)

    def gather_matrix(block, order, slot):
        gathered = gather_blocks(block, order)
        if direct:
            return gathered
        blocks = from_matrix(as_matrix(*gathered, slot, my_core), groups, pairs)
        blocks = blocks.reshape((groups * pairs,) + blocks.shape[2:])
        return blocks[:, 0], blocks[:, 1]

    def reduce_matrix(keep, send, order, slot):
        if direct:
            return scatter_sum(keep, send, order)
        both = jnp.stack([keep, send.astype(F32)], axis=1).reshape(
            groups, pairs, 2, features // groups, LANES
        )
        matrix = jnp.transpose(both, (0, 3, 1, 2, 4)).reshape(features, features)
        parts = from_matrix(matrix, groups, half_wide)
        placed = jnp.zeros((groups * half_wide,) + parts.shape[2:], F32)
        placed = placed.at[slot.reshape(-1)].set(parts.reshape(placed.shape))
        mine = jnp.where(my_core == 0, placed[:, 0], placed[:, 1])
        theirs = jnp.where(my_core == 0, placed[:, 1], placed[:, 0])
        return scatter_sum(mine, theirs.astype(BF), order)

    qkv_low = qkv_weights.astype(BF)
    qkv_parts = [gather_matrix(qkv_low[m], orders[m], slots[m]) for m in range(3)]
    table_hot = (
        jnp.pad(buckets, (0, 1), constant_values=-1)[:, None]
        == jnp.arange(bucket_count, dtype=jnp.int32)[None, :]
    ).astype(F32)
    bias_table = jnp.dot(table_hot, rel_bias, precision=lax.Precision.HIGHEST).T

    owner_slot = expert_ids % groups * places + expert_ids // groups
    kept_pairs = expert_slots >= 0
    row_ids = jnp.where(kept_pairs, owner_slot * capacity + expert_slots, -1)
    slot_ids = jnp.arange(slot_total, dtype=jnp.int32)
    route = [(slot_ids[:, None] == row_ids[:, c][None, :]).astype(BF) for c in range(2)]
    both_route = route[0] + route[1]

    def dispatch(slot_rows):
        width = slot_rows.shape[-1]
        shaped = slot_rows.reshape(groups, places, 1, 2, half_cap, width)
        copies = jnp.broadcast_to(
            shaped, (groups, places, split_parts // 2, 2, half_cap, width)
        ).reshape(groups * wide_count, half_cap, width)
        mine = lax.all_to_all(copies, ("narrow", "wide"), split_axis=0, concat_axis=0, tiled=True)
        return mine.reshape(-1, width), from_partner(mine, ("wide", 0)).reshape(-1, width)

    def collect(partials):
        mine = (
            partials[0].astype(F32) + from_partner(partials[1], ("wide", 0)).astype(F32)
        ).astype(BF)
        back = lax.all_to_all(
            mine.reshape(groups * wide_count, half_cap, features),
            ("narrow", "wide"),
            split_axis=0,
            concat_axis=0,
            tiled=True,
        ).reshape(groups, places, split_parts // 2, 2, half_cap, features)
        return jnp.transpose(back, (2, 0, 1, 3, 4, 5)).reshape(
            split_parts // 2 * slot_total, features
        )

    id_lanes = jnp.broadcast_to(
        expert_ids.astype(BF)[:, ::-1, None], (length, 2, LANES)
    )
    upstream_rows = jnp.concatenate(
        [
            mm(both_route, upstream),
            mm(route[0], id_lanes[:, 0]) + mm(route[1], id_lanes[:, 1]),
        ],
        axis=1,
    ).astype(BF)
    upstream_rows, _ = lax.optimization_barrier((upstream_rows, qkv_parts))
    upstream_got = dispatch(upstream_rows)

    normed_in, heads, probs, attended = attend_call(
        qkv_table, tokens, attn_gain, bias_table, qkv_parts, groups, head_dim
    )
    out_block = jnp.concatenate([out_weight.astype(BF), router.astype(BF)], axis=1)
    gathered_out = gather_blocks(out_block, orders[0])
    matrix_out = as_matrix(*gathered_out, slots[0], my_core).reshape(
        features, wide_count, col_count + router.shape[1]
    )
    full_out = matrix_out[:, :, :col_count].reshape(features, features)
    full_router = matrix_out[:, :, col_count:].reshape(features, experts)
    attended_rows = jnp.transpose(attended, (1, 0, 2)).reshape(length, features)
    inputs = tokens.astype(F32)
    hidden_x1 = inputs + mm(attended_rows, full_out)
    moe_factor = lax.rsqrt(jnp.mean(hidden_x1 * hidden_x1, axis=-1, keepdims=True) + NORM_EPS)
    moe_input = (hidden_x1 * moe_factor * moe_gain).astype(BF)
    expert_rows = dispatch(mm(both_route, moe_input).astype(BF))

    logits = mm(moe_input, full_router)
    pick_mask = expert_ids[:, :, None] == jnp.arange(experts, dtype=jnp.int32)[None, None, :]
    picked = jnp.sum(jnp.where(pick_mask, logits[:, None, :], 0.0), axis=2)
    gate_values = jax.nn.softmax(picked, axis=1)

    pad_width = -part_width % (2 * LANES)
    gate_low = jnp.pad(gate_weight[0, 0].astype(BF), ((0, 0), (0, pad_width)))
    up_low = jnp.pad(up_weight[0, 0].astype(BF), ((0, 0), (0, pad_width)))
    down_low = jnp.pad(down_weight[0, 0].astype(BF), ((0, pad_width), (0, 0)))
    router_wide = jnp.pad(full_router, ((0, 0), (0, -experts % LANES)))
    my_expert = (my_narrow + groups * (my_wide // split_parts)).reshape(1).astype(jnp.int32)
    done = [
        expert_call(my_expert, x, u, router_wide, gate_low, up_low, down_low)
        for x, u in zip(expert_rows, upstream_got)
    ]
    outputs_back = collect([d[0] for d in done])
    inputs_back = collect([d[1] for d in done])
    gate_local, up_local, down_local = expert_grad_call(
        expert_rows,
        [d[5] for d in done],
        [d[2] for d in done],
        [d[3] for d in done],
        [d[4] for d in done],
        part_width,
    )

    def pick(routes, rows):
        return sum(
            mm(routes, rows[h * slot_total : (h + 1) * slot_total], TN)
            for h in range(split_parts // 2)
        )

    first_rows = pick(route[0], outputs_back)
    second_rows = pick(route[1], outputs_back)
    moe_sum = gate_values[:, 0:1] * first_rows + gate_values[:, 1:2] * second_rows
    block_out = (hidden_x1 + moe_sum).astype(BF)
    cotangent = upstream.astype(F32)
    pair_grad = jnp.stack(
        [jnp.sum(cotangent * first_rows, axis=1), jnp.sum(cotangent * second_rows, axis=1)], axis=1
    )
    logit_pair = gate_values * (pair_grad - jnp.sum(gate_values * pair_grad, axis=1, keepdims=True))
    logit_grad = jnp.sum(jnp.where(pick_mask, logit_pair[:, :, None], 0.0), axis=1).astype(BF)
    router_local = mm(moe_input, logit_grad, TN)
    moe_input_grad = pick(both_route, inputs_back) + mm(logit_grad, full_router, NT)
    hat = hidden_x1 * moe_factor
    moe_gain_local = jnp.sum(moe_input_grad * hat, axis=0)
    scaled = moe_input_grad * moe_gain
    inner = jnp.mean(scaled * hat, axis=-1, keepdims=True)
    x1_grad = cotangent + moe_factor * (scaled - hat * inner)
    branch_grad = x1_grad.astype(BF)
    out_local = mm(attended_rows, branch_grad, TN)
    attended_grad = mm(branch_grad, full_out, NT).astype(BF)
    attended_grad = jnp.transpose(attended_grad.reshape(length, 2 * pairs, LANES), (1, 0, 2))

    out_parts = from_matrix(out_local, groups, half_wide).reshape(
        groups * half_wide, 2, row_count, col_count
    )
    back_slots = jnp.argsort(slots[0].reshape(-1))
    out_parts = jnp.take(out_parts, back_slots, axis=0)
    out_keep = jnp.where(my_core == 0, out_parts[:, 0], out_parts[:, 1])
    out_send = jnp.where(my_core == 0, out_parts[:, 1], out_parts[:, 0]).astype(BF)
    out_mine = scatter_sum(out_keep, out_send, orders[0])
    out_total_parts = gather_matrix(out_mine.astype(BF), orders[0], slots[0])

    keeps, sends, dheads, diag = attend_back_call(
        qkv_table, normed_in, heads, probs, attended_grad, groups, head_dim
    )
    qkv_mine = [reduce_matrix(keeps[m], sends[m], orders[m], slots[m]) for m in range(3)]
    qkv_total_parts = [
        gather_matrix(qkv_mine[m].astype(BF), orders[m], slots[m]) for m in range(3)
    ]
    tokens_grad, attn_gain_local = tokens_back_call(
        qkv_table, tokens, attn_gain, x1_grad, dheads, qkv_parts, groups
    )
    tail = jnp.pad(diag, ((0, 0), (0, 0), (0, 8)))
    line = sum(tail[:, s, s : s + 2 * length] for s in range(8))
    bias_local = jnp.dot(line, table_hot, precision=lax.Precision.HIGHEST).T

    small = jnp.concatenate(
        [
            attn_gain_local.reshape(-1),
            moe_gain_local,
            bias_local.reshape(-1),
            router_local.reshape(-1),
        ]
    )
    small = cube_sum(small.reshape(-1, LANES), all_hops).reshape(-1)
    gain_a_total = small[:features]
    gain_m_total = small[features : 2 * features]
    bias_size = bucket_count * head_count
    bias_total = small[2 * features : 2 * features + bias_size].reshape(bucket_count, head_count)
    router_total = small[2 * features + bias_size :].reshape(features, experts)

    local_sums = jnp.stack(
        [
            jnp.sum(gate_local * gate_local, axis=1),
            jnp.sum(up_local * up_local, axis=1),
            jnp.sum(down_local * down_local, axis=0),
        ],
        axis=0,
    )
    part_stats = (
        jnp.stack(
            [
                jnp.mean(gate_local * gate_local, axis=0),
                jnp.mean(up_local * up_local, axis=0),
                jnp.mean(down_local * down_local, axis=1),
            ],
            axis=0,
        )
        + STAT_EPS
    )
    wide_sums = cube_sum(
        local_sums, [("wide", bit) for bit in range(split_parts.bit_length() - 1)]
    )
    wide_stats = wide_sums / (part_width * split_parts) + STAT_EPS
    gate_new = factored(
        gate_weight[0, 0], gate_local, wide_stats[0], part_stats[0], jnp.mean(wide_stats[0])
    )
    up_new = factored(
        up_weight[0, 0], up_local, wide_stats[1], part_stats[1], jnp.mean(wide_stats[1])
    )
    down_new = factored(
        down_weight[0, 0], down_local, part_stats[2], wide_stats[2], jnp.mean(wide_stats[2])
    )

    grads, row_sums, col_sums = spread_call(
        table_of(tables + [tables[0]]), qkv_total_parts + [out_total_parts], groups, features
    )
    qkv_total = jnp.stack(grads[:3], axis=0)
    out_total = grads[3]
    attn_rows = row_sums / features + STAT_EPS
    attn_cols = col_sums / features + STAT_EPS
    attn_means = jnp.mean(attn_rows, axis=1)
    rows_mine = lax.dynamic_slice_in_dim(attn_rows, my_narrow * row_count, row_count, 1)
    cols_mine = lax.dynamic_slice_in_dim(attn_cols, my_wide * col_count, col_count, 1)
    attn_block = jnp.stack(qkv_mine + [out_mine], axis=0)
    qkv_new = factored(qkv_weights, attn_block[:3], rows_mine[:3], cols_mine[:3], attn_means[:3])
    out_step = adafactor_step(attn_block[3], rows_mine[3], cols_mine[3], attn_means[3])
    qkv_stats = jnp.stack([attn_rows[:3], attn_cols[:3]], axis=0)
    out_stats = jnp.stack([attn_rows[3], attn_cols[3]], axis=0)
    router_sq = router_total * router_total
    router_rows = jnp.mean(router_sq, axis=1) + STAT_EPS
    router_cols = jnp.mean(router_sq, axis=0) + STAT_EPS
    router_row_count, router_col_count = router.shape
    router_row_first = my_narrow * router_row_count
    router_col_first = my_wide * router_col_count
    router_block = lax.dynamic_slice(
        router_total, (router_row_first, router_col_first), (router_row_count, router_col_count)
    )
    router_new = factored(
        router,
        router_block,
        lax.dynamic_slice_in_dim(router_rows, router_row_first, router_row_count, 0),
        lax.dynamic_slice_in_dim(router_cols, router_col_first, router_col_count, 0),
        jnp.mean(router_rows),
    )
    return (
        block_out,
        tokens_grad,
        gain_a_total,
        qkv_total,
        out_total,
        bias_total,
        gain_m_total,
        router_total,
        gate_local[None, None],
        up_local[None, None],
        down_local[None, None],
        qkv_new,
        out_step,
        router_new,
        gate_new[None, None],
        up_new[None, None],
        down_new[None, None],
        qkv_stats,
        out_stats,
        router_rows,
        router_cols,
        wide_stats[None, None],
        part_stats[None, None],
    )


def solution(mesh):
    in_specs = (
        P(("narrow", "wide"), None),
        P(),
        P(None, "narrow", "wide"),
        P("narrow", "wide"),
        P(),
        P(),
        P("narrow", "wide"),
        P("narrow", "wide", None, None),
        P("narrow", "wide", None, None),
        P("narrow", "wide", None, None),
        P(("narrow", "wide"), None),
        P(("narrow", "wide"), None),
        P(),
        P(("narrow", "wide"), None),
    )
    out_specs = (
        P(("narrow", "wide"), None),
        P(("narrow", "wide"), None),
        P(),
        P(),
        P(),
        P(),
        P(),
        P(),
        P("narrow", "wide", None, None),
        P("narrow", "wide", None, None),
        P("narrow", "wide", None, None),
        P(None, "narrow", "wide"),
        P("narrow", "wide"),
        P("narrow", "wide"),
        P("narrow", "wide", None, None),
        P("narrow", "wide", None, None),
        P("narrow", "wide", None, None),
        P(),
        P(),
        P(),
        P(),
        P("narrow", "wide", None, None),
        P("narrow", "wide", None, None),
    )
    return jax.shard_map(
        on_device, mesh=mesh, in_specs=in_specs, out_specs=out_specs, check_vma=False
    )
```

```python
import functools

import jax
import jax.numpy as jnp
from jax import lax
from jax.experimental import pallas as pl
from jax.experimental.pallas import tpu as pltpu
from jax.sharding import PartitionSpec as P

NORM_EPS = 1e-06
STAT_EPS = 1e-06
STEP_RATE = 0.01
LANES = 128
GELU_C = 0.7978845608028654
GELU_A = 0.044715
BF = jnp.bfloat16
F32 = jnp.float32
VMEM_LIMIT = 60 * 1024 * 1024
NN = (((1,), (0,)), ((), ()))
NT = (((1,), (1,)), ((), ()))
TN = (((0,), (0,)), ((), ()))


def mm(a, b, dims=NN):
    return lax.dot_general(a, b, dims, preferred_element_type=F32)


def from_partner(value, hop):
    axis, bit = hop
    mask = 2**bit
    pairs = [(source, source ^ mask) for source in range(lax.axis_size(axis))]
    return lax.ppermute(value, axis, pairs)


def after(values, *others):
    return lax.optimization_barrier((values, others))[0]


def hop_orders(groups, wide_count):
    narrow = [("narrow", b) for b in range(groups.bit_length() - 1)]
    wide = [("wide", b) for b in range(1, wide_count.bit_length() - 1)]
    far, near = wide[1:][::-1], wide[:1]
    core = [("wide", 0)]
    return (
        far + narrow + near + core,
        far + near + narrow + core,
        far + narrow[1:] + near + narrow[:1] + core,
        far + narrow[:1] + near + narrow[1:] + core,
    )


def block_slots(order, groups, wide_count):
    n_ids = jnp.arange(groups, dtype=jnp.int32)[:, None]
    w_ids = 2 * jnp.arange(wide_count // 2, dtype=jnp.int32)[None, :]
    slots = jnp.zeros((groups, wide_count // 2), jnp.int32)
    for stage, (axis, bit) in enumerate(order[:-1]):
        ids = n_ids if axis == "narrow" else w_ids
        differs = ((ids ^ lax.axis_index(axis)) >> bit) & 1
        slots = slots | (differs << stage)
    return slots


def together(*values):
    return lax.optimization_barrier(values)


def shared_hops(orders):
    count = 0
    while len({order[count] for order in orders}) == 1 and count < len(orders[0]) - 1:
        count += 1
    return count


def grow(blocks, hop, axis=0):
    return jnp.concatenate([blocks, from_partner(blocks, hop)], axis=axis)


def gather_chains(blocks, orders):
    shared = shared_hops(orders)
    blocks = blocks[:, None]
    for hop in orders[0][:shared]:
        blocks = grow(blocks, hop, 1)
    chains = [blocks[i] for i in range(len(orders))]
    for stage in range(shared, len(orders[0]) - 1):
        chains = [grow(chain, order[stage]) for chain, order in zip(chains, orders)]
    return chains


def core_sum(keep, send, order):
    return keep + from_partner(send, order[-1]).astype(F32)


def halve(total, hop, axis=0):
    half = total.shape[axis] // 2
    mine = lax.slice_in_dim(total, 0, half, axis=axis)
    theirs = lax.slice_in_dim(total, half, 2 * half, axis=axis)
    return mine + from_partner(theirs.astype(BF), hop).astype(F32)


def send_step(state, hop):
    sources, places = state.shape[:2]
    split = state.reshape((sources, 2, places // 2) + state.shape[2:])
    return jnp.concatenate([split[:, 0], from_partner(split[:, 1], hop)], axis=0)


def return_step(state, hop):
    half = state.shape[0] // 2
    got = from_partner(state[half:], hop)
    return jnp.stack([state[:half], got], axis=1).reshape((half, -1) + state.shape[2:])


def row_slots(hops, groups, places, parts):
    n_ids = jnp.arange(groups, dtype=jnp.int32)[:, None]
    w_ids = parts * jnp.arange(places, dtype=jnp.int32)[None, :]
    slots = jnp.zeros((groups, places), jnp.int32)
    for axis, bit in hops:
        ids = n_ids if axis == "narrow" else w_ids
        slots = 2 * slots + (((ids ^ lax.axis_index(axis)) >> bit) & 1)
    return slots.reshape(-1)


def cube_sum(value, hops):
    for hop in hops:
        value = value + from_partner(value, hop)
    return value


def as_matrix(own, other, slots, my_core):
    groups, half_wide = slots.shape
    both = jnp.stack([jnp.where(my_core == 0, own, other), jnp.where(my_core == 0, other, own)], 1)
    picked = jnp.take(both, slots.reshape(-1), axis=0)
    rows, cols = own.shape[1:]
    picked = picked.reshape(groups, half_wide, 2, rows, cols)
    return jnp.transpose(picked, (0, 3, 1, 2, 4)).reshape(groups * rows, half_wide * 2 * cols)


def from_matrix(matrix, groups, half_wide):
    lead = matrix.shape[:-2]
    rows, cols = matrix.shape[-2] // groups, matrix.shape[-1] // (2 * half_wide)
    shaped = matrix.reshape(lead + (groups, rows, half_wide, 2, cols))
    k = len(lead)
    order = tuple(range(k)) + (k, k + 2, k + 3, k + 1, k + 4)
    return jnp.transpose(shaped, order)


def gelu_tanh(values):
    return jax.nn.gelu(values, approximate=True)


def adafactor_step(gradient, row_stats, col_stats, mean_rows):
    return (
        STEP_RATE
        * gradient
        / jnp.sqrt(row_stats[..., :, None] * col_stats[..., None, :] / mean_rows[..., None, None])
    )


def factored(weight, gradient, row_stats, col_stats, mean_rows):
    return weight - adafactor_step(gradient, row_stats, col_stats, mean_rows)


def vmem():
    return pl.BlockSpec(memory_space=pltpu.VMEM)


def smem():
    return pl.BlockSpec(memory_space=pltpu.SMEM)


def params():
    return pltpu.CompilerParams(vmem_limit_bytes=VMEM_LIMIT)


def lane_masks(head_dim):
    heads = LANES // head_dim
    ids = lax.broadcasted_iota(jnp.int32, (1, LANES), 1) // head_dim
    return [ids == i for i in range(heads)]


def attend_body(
    table_ref, tokens_ref, gain_ref, bias_ref,
    own_q, own_k, own_v, far_q, far_k, far_v,
    normed_ref, heads_ref, probs_ref, attended_ref,
    *, groups, pairs, head_dim,
):
    length, features = tokens_ref.shape
    rows = features // groups
    x = tokens_ref[...].astype(F32)
    factor = lax.rsqrt(jnp.mean(x * x, axis=-1, keepdims=True) + NORM_EPS)
    normed_ref[...] = (x * factor * gain_ref[...]).astype(BF)
    core = table_ref[0]

    def project(w2, carry):
        for m, (own, far) in enumerate(((own_q, far_q), (own_k, far_k), (own_v, far_v))):
            total = None
            for n in range(groups):
                at = table_ref[1 + (m * groups + n) * pairs + w2]
                block = jnp.concatenate([own[at], far[at]], axis=1)
                part = mm(normed_ref[:, n * rows : (n + 1) * rows], block)
                total = part if total is None else total + part
            total = total.astype(BF)
            heads_ref[m, 2 * w2 + core] = total[:, :LANES]
            heads_ref[m, 2 * w2 + 1 - core] = total[:, LANES:]
        return carry

    lax.fori_loop(0, pairs, project, 0)
    masks = lane_masks(head_dim)
    scale = head_dim**-0.5

    def attend(w, carry):
        q, k, v = heads_ref[0, w], heads_ref[1, w], heads_ref[2, w]
        mixed = jnp.zeros((length, LANES), F32)
        for i, mask in enumerate(masks):
            head = w * len(masks) + i
            raw = mm(jnp.where(mask, q, jnp.zeros_like(q)), k, NT)
            line = jnp.broadcast_to(bias_ref[pl.ds(head, 1), :], (length, 2 * length))
            bias = pltpu.roll(line, length + 1, 1, stride=1, stride_axis=0)[:, :length]
            scores = raw * scale + bias
            top = jnp.max(scores, axis=-1, keepdims=True)
            grown = jnp.exp(scores - top)
            probs = grown / jnp.sum(grown, axis=-1, keepdims=True)
            probs_ref[head] = probs
            mixed = jnp.where(mask, mm(probs.astype(BF), v), mixed)
        attended_ref[w] = mixed.astype(BF)
        return carry

    lax.fori_loop(0, 2 * pairs, attend, 0)


def attend_call(table, tokens, gain, bias_table, gathered, groups, head_dim):
    length, features = tokens.shape
    pairs = features // (2 * LANES)
    head_count = features // head_dim
    owns = [g[0] for g in gathered]
    fars = [g[1] for g in gathered]
    body = functools.partial(attend_body, groups=groups, pairs=pairs, head_dim=head_dim)
    return pl.pallas_call(
        body,
        in_specs=[smem()] + [vmem()] * 9,
        out_specs=[vmem()] * 4,
        out_shape=[
            jax.ShapeDtypeStruct((length, features), BF),
            jax.ShapeDtypeStruct((3, 2 * pairs, length, LANES), BF),
            jax.ShapeDtypeStruct((head_count, length, length), F32),
            jax.ShapeDtypeStruct((2 * pairs, length, LANES), BF),
        ],
        compiler_params=params(),
        name="attend",
    )(table, tokens, gain.reshape(1, features), bias_table, *owns, *fars)


def expert_hot(ids_ref, expert, cap, length):
    slot = lax.broadcasted_iota(jnp.int32, (cap, length), 0) + expert * cap
    return [slot == ids_ref[c : c + 1, :] for c in range(2)]


def spread_rows(values, ids_ref, slots_ref, sends, experts, cap):
    length, features = values.shape
    half = cap // 2
    for e in range(experts):
        first, second = expert_hot(ids_ref, e, cap, length)
        rows = mm(jnp.where(first | second, 1.0, 0.0).astype(BF), values)
        for chain, send in enumerate(sends):
            at = slots_ref[chain * experts + e]
            send[at, :, :features] = rows[chain * half : (chain + 1) * half].astype(BF)


def upstream_body(slots_ref, values_ref, ids_ref, others_ref, send_a, send_b, *, experts, cap):
    length, features = values_ref.shape
    half = cap // 2
    spread_rows(values_ref[...], ids_ref, slots_ref, (send_a, send_b), experts, cap)
    for e in range(experts):
        first, second = expert_hot(ids_ref, e, cap, length)
        other = jnp.where(first, others_ref[0:1, :], 0.0) + jnp.where(
            second, others_ref[1:2, :], 0.0
        )
        other = jnp.sum(other, axis=1, keepdims=True)
        other = jnp.broadcast_to(other, (cap, LANES))
        for chain, send in enumerate((send_a, send_b)):
            at = slots_ref[chain * experts + e]
            send[at, :, features:] = other[chain * half : (chain + 1) * half].astype(BF)


def upstream_call(row_table, upstream, row_ids, other_ids, experts, cap):
    features = upstream.shape[1]
    return pl.pallas_call(
        functools.partial(upstream_body, experts=experts, cap=cap),
        in_specs=[smem()] + [vmem()] * 3,
        out_specs=[vmem()] * 2,
        out_shape=[jax.ShapeDtypeStruct((experts, cap // 2, features + LANES), BF)] * 2,
        compiler_params=params(),
        name="upstream_rows",
    )(row_table, upstream, row_ids, other_ids)


def post_body(
    table_ref, slots_ref, tokens_ref, attended_ref, own, far, gain_ref, ids_ref,
    x1_ref, normed_ref, send_a, send_b,
    *, groups, experts, cap,
):
    length, features = tokens_ref.shape
    pairs = features // (2 * LANES)
    per_group = 2 * pairs // groups
    depth = features // groups
    core = table_ref[0]
    rows = [
        jnp.concatenate([attended_ref[n * per_group + i] for i in range(per_group)], axis=1)
        for n in range(groups)
    ]
    for w2 in range(pairs):
        total = None
        for n in range(groups):
            at = table_ref[1 + (3 * groups + n) * pairs + w2]
            block = jnp.concatenate([own[at, :depth], far[at, :depth]], axis=1)
            part = mm(rows[n], block)
            total = part if total is None else total + part
        for j in range(2):
            w = 2 * w2 + (core if j == 0 else 1 - core)
            place = pl.multiple_of(w * LANES, LANES)
            mine = total[:, j * LANES : (j + 1) * LANES]
            x1_ref[:, pl.ds(place, LANES)] = mine + tokens_ref[:, pl.ds(place, LANES)].astype(F32)
    x1 = x1_ref[...]
    factor = lax.rsqrt(jnp.mean(x1 * x1, axis=-1, keepdims=True) + NORM_EPS)
    normed = (x1 * factor * gain_ref[...]).astype(BF)
    normed_ref[...] = normed
    spread_rows(normed, ids_ref, slots_ref, (send_a, send_b), experts, cap)


def post_call(table, row_table, tokens, attended, out_halves, gain, row_ids, groups, experts, cap):
    length, features = tokens.shape
    return pl.pallas_call(
        functools.partial(post_body, groups=groups, experts=experts, cap=cap),
        in_specs=[smem()] * 2 + [vmem()] * 6,
        out_specs=[vmem()] * 4,
        out_shape=[
            jax.ShapeDtypeStruct((length, features), F32),
            jax.ShapeDtypeStruct((length, features), BF),
            jax.ShapeDtypeStruct((experts, cap // 2, features), BF),
            jax.ShapeDtypeStruct((experts, cap // 2, features), BF),
        ],
        compiler_params=params(),
        name="post",
    )(table, row_table, tokens, attended, *out_halves, gain.reshape(1, features), row_ids)


def mid_body(
    table_ref, slots_ref, x1_ref, gain_ref, normed_ref, upstream_ref, back_a, back_b,
    ids_ref, choice_ref, router_ref, attended_ref, own, far,
    x1_grad_ref, gates_ref, gain_out_ref, router_out_ref, keep_ref, send_ref, att_grad_ref,
    *, groups, experts, cap,
):
    length, features = x1_ref.shape
    pairs = features // (2 * LANES)
    per_group = 2 * pairs // groups
    rows = features // groups
    half = cap // 2
    core = table_ref[0]
    dmoe = jnp.zeros((length, features), F32)
    dots = [jnp.zeros((length, LANES), F32)] * 2
    for e in range(experts):
        hots = expert_hot(ids_ref, e, cap, length)
        hots = [jnp.where(hot, 1.0, 0.0).astype(BF) for hot in hots]
        both = hots[0] + hots[1]
        for chain, back in enumerate((back_a, back_b)):
            at = slots_ref[chain * experts + e]
            part = slice(chain * half, (chain + 1) * half)
            got = back[at]
            dmoe = dmoe + mm(both[part], got[:, :features], TN)
            for c in range(2):
                dots[c] = dots[c] + mm(hots[c][part], got[:, features:], TN)
    normed = normed_ref[...]
    logits = mm(normed, router_ref[...])
    lane = lax.broadcasted_iota(jnp.int32, logits.shape, 1)
    picks = [lane == choice_ref[:, c : c + 1] for c in range(2)]
    picked = [jnp.sum(jnp.where(pick, logits, 0.0), axis=1, keepdims=True) for pick in picks]
    top = jnp.maximum(picked[0], picked[1])
    grown = [jnp.exp(value - top) for value in picked]
    gates = [value / (grown[0] + grown[1]) for value in grown]
    gates_ref[...] = jnp.where(lane == 0, gates[0], jnp.where(lane == 1, gates[1], 0.0))
    dgates = [dot[:, 0:1] for dot in dots]
    inner = gates[0] * dgates[0] + gates[1] * dgates[1]
    dlogits = jnp.where(picks[0], gates[0] * (dgates[0] - inner), 0.0) + jnp.where(
        picks[1], gates[1] * (dgates[1] - inner), 0.0
    )
    dlogits = dlogits.astype(BF)
    router_out_ref[...] = mm(normed, dlogits, TN)
    dmoe = dmoe + mm(dlogits, router_ref[...], NT)
    x1 = x1_ref[...]
    factor = lax.rsqrt(jnp.mean(x1 * x1, axis=-1, keepdims=True) + NORM_EPS)
    hat = x1 * factor
    gain_out_ref[...] = jnp.sum(dmoe * hat, axis=0, keepdims=True)
    scaled = dmoe * gain_ref[...]
    inner = jnp.mean(scaled * hat, axis=-1, keepdims=True)
    x1_grad_ref[...] = upstream_ref[...].astype(F32) + factor * (scaled - hat * inner)
    branches = []
    for w2 in range(pairs):
        both = []
        for j in range(2):
            w = 2 * w2 + (core if j == 0 else 1 - core)
            both.append(x1_grad_ref[:, pl.ds(pl.multiple_of(w * LANES, LANES), LANES)].astype(BF))
        branches.append(jnp.concatenate(both, axis=1))
    for n in range(groups):
        att = jnp.concatenate(
            [attended_ref[n * per_group + i] for i in range(per_group)], axis=1
        )
        total = None
        for w2 in range(pairs):
            at = table_ref[1 + (3 * groups + n) * pairs + w2]
            block = mm(att, branches[w2], TN)
            keep_ref[at] = block[:, :LANES]
            send_ref[at] = block[:, LANES:].astype(BF)
            block = jnp.concatenate([own[at, :rows], far[at, :rows]], axis=1)
            part = mm(branches[w2], block, NT)
            total = part if total is None else total + part
        for i in range(per_group):
            att_grad_ref[n * per_group + i] = total[:, i * LANES : (i + 1) * LANES].astype(BF)


def mid_call(
    table, row_table, x1, gain, normed, upstream, backs, row_ids, choices, router, attended,
    out_halves, groups, experts, cap,
):
    length, features = x1.shape
    pairs = features // (2 * LANES)
    rows = features // groups
    return pl.pallas_call(
        functools.partial(mid_body, groups=groups, experts=experts, cap=cap),
        in_specs=[smem()] * 2 + [vmem()] * 12,
        out_specs=[vmem()] * 7,
        out_shape=[
            jax.ShapeDtypeStruct((length, features), F32),
            jax.ShapeDtypeStruct((length, LANES), F32),
            jax.ShapeDtypeStruct((1, features), F32),
            jax.ShapeDtypeStruct((features, LANES), F32),
            jax.ShapeDtypeStruct((groups * pairs, rows, LANES), F32),
            jax.ShapeDtypeStruct((groups * pairs, rows, LANES), BF),
            jax.ShapeDtypeStruct((2 * pairs, length, LANES), BF),
        ],
        compiler_params=params(),
        name="mid",
    )(
        table, row_table, x1, gain.reshape(1, features), normed, upstream, *backs,
        row_ids, choices, router, attended, *out_halves,
    )


def block_out_body(
    slots_ref, x1_ref, gates_ref, back_a, back_b, ids_ref, out_ref, *, experts, cap
):
    length, features = x1_ref.shape
    half = cap // 2
    sums = [jnp.zeros((length, features), F32)] * 2
    for e in range(experts):
        hots = [
            jnp.where(hot, 1.0, 0.0).astype(BF) for hot in expert_hot(ids_ref, e, cap, length)
        ]
        for chain, back in enumerate((back_a, back_b)):
            got = back[slots_ref[chain * experts + e]]
            part = slice(chain * half, (chain + 1) * half)
            sums = [total + mm(hot[part], got, TN) for total, hot in zip(sums, hots)]
    moe = gates_ref[:, 0:1] * sums[0] + gates_ref[:, 1:2] * sums[1]
    out_ref[...] = (x1_ref[...] + moe).astype(BF)


def block_out_call(row_table, x1, gates, backs, row_ids, experts, cap):
    return pl.pallas_call(
        functools.partial(block_out_body, experts=experts, cap=cap),
        in_specs=[smem()] + [vmem()] * 5,
        out_specs=vmem(),
        out_shape=jax.ShapeDtypeStruct(x1.shape, BF),
        compiler_params=params(),
        name="block_out",
    )(row_table, x1, gates, *backs, row_ids)


def attend_back_body(
    table_ref, normed_ref, heads_ref, probs_ref, grad_ref,
    keep_ref, send_ref, dheads_ref, diag_ref,
    *, groups, pairs, head_dim,
):
    length, features = normed_ref.shape
    rows = features // groups
    masks = lane_masks(head_dim)
    scale = head_dim**-0.5

    def back(w, carry):
        q, k, v = heads_ref[0, w], heads_ref[1, w], heads_ref[2, w]
        da = grad_ref[w]
        dq = jnp.zeros((length, LANES), F32)
        dk, dv = dq, dq
        for i, mask in enumerate(masks):
            head = w * len(masks) + i
            probs = probs_ref[head]
            dp = mm(jnp.where(mask, da, jnp.zeros_like(da)), v, NT)
            spread = jnp.sum(probs * dp, axis=-1, keepdims=True)
            ds = (probs * (dp - spread)).astype(BF)
            dq = jnp.where(mask, mm(ds, k), dq)
            dk = jnp.where(mask, mm(ds, q, TN), dk)
            dv = jnp.where(mask, mm(probs.astype(BF), da, TN), dv)
            wide_ds = jnp.concatenate([ds.astype(F32), jnp.zeros((length, length), F32)], axis=1)
            diag = jnp.zeros((8, 2 * length), F32)
            for g in range(length // 8):
                diag = diag + pltpu.roll(wide_ds[8 * g : 8 * g + 8], length - 1 - 8 * g, 1)
            diag_ref[head] = diag
        dheads_ref[0, w] = (dq * scale).astype(BF)
        dheads_ref[1, w] = (dk * scale).astype(BF)
        dheads_ref[2, w] = dv.astype(BF)
        return carry

    lax.fori_loop(0, 2 * pairs, back, 0)
    core = table_ref[0]

    def weigh(w2, carry):
        for m in range(3):
            both = jnp.concatenate(
                [dheads_ref[m, 2 * w2 + core], dheads_ref[m, 2 * w2 + 1 - core]], axis=1
            )
            for n in range(groups):
                at = table_ref[1 + (m * groups + n) * pairs + w2]
                block = mm(normed_ref[:, n * rows : (n + 1) * rows], both, TN)
                keep_ref[m, at] = block[:, :LANES]
                send_ref[m, at] = block[:, LANES:].astype(BF)
        return carry

    lax.fori_loop(0, pairs, weigh, 0)


def attend_back_call(table, normed, heads, probs, attended_grad, groups, head_dim):
    length, features = normed.shape
    pairs = features // (2 * LANES)
    head_count = features // head_dim
    rows = features // groups
    body = functools.partial(attend_back_body, groups=groups, pairs=pairs, head_dim=head_dim)
    return pl.pallas_call(
        body,
        in_specs=[smem()] + [vmem()] * 4,
        out_specs=[vmem()] * 4,
        out_shape=[
            jax.ShapeDtypeStruct((3, groups * pairs, rows, LANES), F32),
            jax.ShapeDtypeStruct((3, groups * pairs, rows, LANES), BF),
            jax.ShapeDtypeStruct((3, 2 * pairs, length, LANES), BF),
            jax.ShapeDtypeStruct((head_count, 8, 2 * length), F32),
        ],
        compiler_params=params(),
        name="attend_back",
    )(table, normed, heads, probs, attended_grad)


def tokens_back_body(
    table_ref, tokens_ref, gain_ref, x1_grad_ref, dheads_ref,
    own_q, own_k, own_v, far_q, far_k, far_v,
    out_ref, gain_out_ref, acc_ref,
    *, groups, pairs,
):
    length, features = tokens_ref.shape
    rows = features // groups
    core = table_ref[0]
    for n in range(groups):

        def step(w2, total):
            for m, (own, far) in enumerate(((own_q, far_q), (own_k, far_k), (own_v, far_v))):
                at = table_ref[1 + (m * groups + n) * pairs + w2]
                both = jnp.concatenate(
                    [dheads_ref[m, 2 * w2 + core], dheads_ref[m, 2 * w2 + 1 - core]], axis=1
                )
                total = total + mm(both, jnp.concatenate([own[at], far[at]], axis=1), NT)
            return total

        total = lax.fori_loop(0, pairs, step, jnp.zeros((length, rows), F32))
        acc_ref[:, n * rows : (n + 1) * rows] = total
    x = tokens_ref[...].astype(F32)
    factor = lax.rsqrt(jnp.mean(x * x, axis=-1, keepdims=True) + NORM_EPS)
    hat = x * factor
    grad = acc_ref[...]
    gain_out_ref[...] = jnp.sum(grad * hat, axis=0, keepdims=True)
    scaled = grad * gain_ref[...]
    inner = jnp.mean(scaled * hat, axis=-1, keepdims=True)
    out_ref[...] = (x1_grad_ref[...] + factor * (scaled - hat * inner)).astype(BF)


def tokens_back_call(table, tokens, gain, x1_grad, dheads, gathered, groups):
    length, features = tokens.shape
    pairs = features // (2 * LANES)
    owns = [g[0] for g in gathered]
    fars = [g[1] for g in gathered]
    return pl.pallas_call(
        functools.partial(tokens_back_body, groups=groups, pairs=pairs),
        in_specs=[smem()] + [vmem()] * 10,
        out_specs=[vmem()] * 2,
        out_shape=[
            jax.ShapeDtypeStruct((length, features), BF),
            jax.ShapeDtypeStruct((1, features), F32),
        ],
        scratch_shapes=[pltpu.VMEM((length, features), F32)],
        compiler_params=params(),
        name="tokens_back",
    )(table, tokens, gain.reshape(1, features), x1_grad, dheads, *owns, *fars)


def choose(refs, which):
    value = refs[0][...]
    for i in range(1, len(refs)):
        value = jnp.where(which == i, refs[i][...], value)
    return value


def expert_body(expert_ref, *refs, count):
    x_refs, up_refs, refs = refs[:count], refs[count : 2 * count], refs[2 * count :]
    router_ref, gate_w, up_w, down_w = refs[:4]
    y_refs, dx_refs = refs[-2 * count - 5 : -count - 5], refs[-count - 5 : -5]
    x_out, dy_ref, hidden_ref, dgate_ref, dup_ref = refs[-5:]
    piece = pl.program_id(0)
    x = choose(x_refs, piece)
    up = choose(up_refs, piece)
    x_out[...] = x
    features = x.shape[1]
    logits = mm(x, router_ref[...])
    lane = lax.broadcasted_iota(jnp.int32, logits.shape, 1)
    other_id = up[:, features : features + 1].astype(jnp.int32)
    mine = jnp.sum(jnp.where(lane == expert_ref[0], logits, 0.0), axis=1, keepdims=True)
    other = jnp.sum(jnp.where(lane == other_id, logits, 0.0), axis=1, keepdims=True)
    top = jnp.maximum(mine, other)
    mine_e = jnp.exp(mine - top)
    gate = mine_e / (mine_e + jnp.exp(other - top))
    grad = up[:, :features].astype(F32)
    dy = (gate * grad).astype(BF)
    dy_ref[...] = dy
    y, dx = None, None
    step = 2 * LANES
    width = gate_w.shape[0]
    for f in range(0, width, step):
        chunk = slice(f, min(f + step, width))
        gate_f, up_f, down_f = gate_w[chunk, :], up_w[chunk, :], down_w[chunk, :]
        g = mm(x, gate_f, NT)
        u = mm(x, up_f, NT)
        dh = mm(dy, down_f, NT)
        t = jnp.tanh(g * (GELU_C + (GELU_C * GELU_A) * (g * g)))
        half_t = 0.5 + 0.5 * t
        act = g * half_t
        hidden = (act * u).astype(BF)
        slope = half_t + act * (1.0 - t) * (GELU_C + (3.0 * GELU_C * GELU_A) * (g * g))
        dg = (dh * u * slope).astype(BF)
        du = (dh * act).astype(BF)
        hidden_ref[:, chunk] = hidden
        dgate_ref[:, chunk] = dg
        dup_ref[:, chunk] = du
        y_f = mm(hidden, down_f)
        dx_f = mm(dg, gate_f) + mm(du, up_f)
        y = y_f if y is None else y + y_f
        dx = dx_f if dx is None else dx + dx_f
    y = y.astype(BF)
    dot = jnp.sum(grad * y.astype(F32), axis=1, keepdims=True)
    dx = dx.astype(BF)
    dot = jnp.broadcast_to(dot, (x.shape[0], LANES)).astype(BF)
    for i in range(count):

        @pl.when(piece == i)
        def _(i=i):
            y_refs[i][...] = y
            dx_refs[i][:, :features] = dx
            dx_refs[i][:, features:] = dot


def expert_call(expert, xs, upstreams, router, gate_w, up_w, down_w, first, total, kept):
    rows, features = xs[0].shape
    width = gate_w.shape[0]
    count = len(xs)

    def whole(arr):
        return pl.BlockSpec(arr.shape, lambda i, e: (0, 0))

    def kept_spec(cols):
        return pl.BlockSpec((rows, cols), lambda i, e: (first + i, 0))

    kept_cols = (features, features, width, width, width)
    kept_in = [] if kept is None else list(kept)
    inputs = list(xs) + list(upstreams) + [router, gate_w, up_w, down_w]
    out = pl.pallas_call(
        functools.partial(expert_body, count=count),
        grid_spec=pltpu.PrefetchScalarGridSpec(
            num_scalar_prefetch=1,
            grid=(count,),
            in_specs=[whole(arr) for arr in inputs]
            + [pl.BlockSpec(memory_space=pl.ANY)] * len(kept_in),
            out_specs=[pl.BlockSpec((rows, features), lambda i, e: (0, 0))] * count
            + [pl.BlockSpec((rows, features + LANES), lambda i, e: (0, 0))] * count
            + [kept_spec(cols) for cols in kept_cols],
        ),
        out_shape=[jax.ShapeDtypeStruct((rows, features), BF)] * count
        + [jax.ShapeDtypeStruct((rows, features + LANES), BF)] * count
        + [jax.ShapeDtypeStruct((total, cols), BF) for cols in kept_cols],
        input_output_aliases={
            1 + len(inputs) + i: 2 * count + i for i in range(len(kept_in))
        },
        compiler_params=params(),
        name="expert",
    )(expert, *inputs, *kept_in)
    return out[:count], out[count : 2 * count], out[2 * count :]


def expert_grad_body(left_ref, right_ref, out_ref):
    out_ref[...] = mm(left_ref[...], right_ref[...], TN)


def expert_grad_call(left, right):
    rows, features = right.shape
    width = left.shape[1]
    size = 2 * LANES
    return pl.pallas_call(
        expert_grad_body,
        grid=(features // size,),
        in_specs=[
            pl.BlockSpec((rows, width), lambda i: (0, 0)),
            pl.BlockSpec((rows, size), lambda i: (0, i)),
        ],
        out_specs=pl.BlockSpec((width, size), lambda i: (0, i)),
        out_shape=jax.ShapeDtypeStruct((width, features), F32),
        compiler_params=params(),
        name="expert_grad",
    )(left, right)


def finish_body(table_ref, place_ref, *refs, groups, pairs, count, first, update, subtract):
    owns, fars, refs = refs[:count], refs[count : 2 * count], refs[2 * count :]
    if update:
        mine_ref, weight_ref, refs = refs[0], refs[1], refs[2:]
    grads_ref, rows_ref, cols_ref = refs[:3]
    new_ref = refs[3] if update else None
    acc_ref, line_ref = refs[-2:]
    core = table_ref[0]
    rows = owns[0].shape[1]
    features = acc_ref.shape[0]
    for m in range(count):
        acc_ref[...] = jnp.zeros_like(acc_ref)

        def column(w2, carry, m=m):
            for j, source in enumerate((owns[m], fars[m])):
                w = 2 * w2 + (core if j == 0 else 1 - core)
                place = pl.multiple_of(w * LANES, LANES)
                total = jnp.zeros((1, LANES), F32)
                for n in range(groups):
                    at = table_ref[1 + ((first + m) * groups + n) * pairs + w2]
                    block = source[at].astype(F32)
                    grads_ref[m, n * rows : (n + 1) * rows, pl.ds(place, LANES)] = block
                    square = block * block
                    total = total + jnp.sum(square, axis=0, keepdims=True)
                    acc_ref[n * rows : (n + 1) * rows, :] += square
                cols_ref[m, w] = total / features + STAT_EPS
            return carry

        lax.fori_loop(0, pairs, column, 0)
        squares = acc_ref[...]
        sums = lax.dot_general(
            jnp.ones((8, LANES), F32), squares, NT,
            precision=lax.Precision.HIGHEST, preferred_element_type=F32,
        )
        rows_ref[m] = sums / features + STAT_EPS
        if update:
            line = jnp.sum(squares, axis=1, keepdims=True) / features + STAT_EPS
            line_ref[...] = jnp.broadcast_to(line, line_ref.shape)
            mean = jnp.sum(line, axis=0, keepdims=True) / features
            my_rows = line_ref[pl.ds(pl.multiple_of(place_ref[0] * rows, rows), rows), :]
            my_cols = cols_ref[m, place_ref[1]]
            step = STEP_RATE * mine_ref[m] / jnp.sqrt(my_rows * my_cols / mean)
            new_ref[m] = weight_ref[m] - step if subtract else step


def finish_call(table, place, gathered, first, groups, features, mine, weights, subtract):
    pairs = features // (2 * LANES)
    count = len(gathered)
    rows = features // groups
    owns = [g[0] for g in gathered]
    fars = [g[1] for g in gathered]
    update = mine is not None
    extra = [mine, weights] if update else []
    shapes = [
        jax.ShapeDtypeStruct((count, features, features), F32),
        jax.ShapeDtypeStruct((count, 8, features), F32),
        jax.ShapeDtypeStruct((count, 2 * pairs, 1, LANES), F32),
    ]
    if update:
        shapes.append(jax.ShapeDtypeStruct((count, rows, LANES), F32))
    out = pl.pallas_call(
        functools.partial(
            finish_body, groups=groups, pairs=pairs, count=count, first=first,
            update=update, subtract=subtract,
        ),
        in_specs=[smem()] * 2 + [vmem()] * (2 * count + len(extra)),
        out_specs=[vmem()] * len(shapes),
        out_shape=shapes,
        scratch_shapes=[pltpu.VMEM((features, LANES), F32)] * 2,
        compiler_params=params(),
        name="finish",
    )(table, place, *owns, *fars, *extra)
    stats = (out[0], out[1][:, 0], out[2].reshape(count, features))
    return stats + (out[3] if update else None,)


def on_device(
    tokens,
    attn_gain,
    qkv_weights,
    out_weight,
    rel_bias,
    moe_gain,
    router,
    gate_weight,
    up_weight,
    down_weight,
    expert_ids,
    expert_slots,
    buckets,
    upstream,
):
    length, features = tokens.shape
    bucket_count, head_count = rel_bias.shape
    head_dim = features // head_count
    groups = lax.axis_size("narrow")
    wide_count = lax.axis_size("wide")
    my_narrow = lax.axis_index("narrow")
    my_wide = lax.axis_index("wide")
    my_core = my_wide % 2
    part_width = gate_weight.shape[3]
    experts = router.shape[1] * wide_count
    places = experts // groups
    split_parts = wide_count // places
    capacity = (10 * length // experts + 3) // 4
    half_cap = capacity // 2
    row_count, col_count = qkv_weights.shape[1:]
    half_wide = wide_count // 2
    core_hop = ("wide", 0)
    part_hop = ("wide", 1)
    orders = hop_orders(groups, wide_count)
    slots = [block_slots(order, groups, wide_count) for order in orders]
    direct = col_count == LANES
    pairs = features // (2 * LANES)
    if direct:
        core_entry, tables = my_core, slots
    else:
        core_entry = jnp.int32(0)
        tables = [jnp.arange(groups * pairs, dtype=jnp.int32)] * 4
    table = jnp.concatenate(
        [jnp.reshape(core_entry, (1,)).astype(jnp.int32)] + [t.reshape(-1) for t in tables]
    )
    place = jnp.stack([my_narrow, my_wide]).astype(jnp.int32)

    def as_pairs(matrix):
        blocks = from_matrix(matrix, groups, pairs)
        return blocks.reshape((groups * pairs,) + blocks.shape[2:])

    def as_halves(owns, fars, first):
        if direct:
            return list(zip(owns, fars))
        out = []
        for i, halves in enumerate(zip(owns, fars)):
            both = as_pairs(as_matrix(*halves, slots[first + i], my_core))
            out.append((both[:, 0], both[:, 1]))
        return out

    def halves_of(keep, send, which):
        if direct:
            return keep, send
        both = jnp.stack([keep, send.astype(F32)], axis=1).reshape(
            groups, pairs, 2, features // groups, LANES
        )
        matrix = jnp.transpose(both, (0, 3, 1, 2, 4)).reshape(features, features)
        parts = from_matrix(matrix, groups, half_wide)
        placed = jnp.zeros((groups * half_wide,) + parts.shape[2:], F32)
        placed = placed.at[slots[which].reshape(-1)].set(parts.reshape(placed.shape))
        mine = jnp.where(my_core == 0, placed[:, 0], placed[:, 1])
        theirs = jnp.where(my_core == 0, placed[:, 1], placed[:, 0])
        return mine, theirs.astype(BF)

    narrow_hops = [("narrow", b) for b in range(groups.bit_length() - 1)]
    place_hops = [
        ("wide", b) for b in range(split_parts.bit_length() - 1, wide_count.bit_length() - 1)
    ][::-1]
    chains = (
        narrow_hops[:1] + place_hops + narrow_hops[1:],
        place_hops + narrow_hops[1:] + narrow_hops[:1],
    )
    hop_count = len(chains[0])
    row_table = jnp.concatenate(
        [row_slots(hops, groups, places, split_parts) for hops in chains]
    )
    owner_slot = expert_ids % groups * places + expert_ids // groups
    row_ids = jnp.where(expert_slots >= 0, owner_slot * capacity + expert_slots, -1).T

    def flat(rows):
        return rows.reshape(-1, rows.shape[-1])

    def sends(states, step):
        return [send_step(state, hops[step]) for state, hops in zip(states, chains)]

    def to_core(values):
        return [from_partner(value, core_hop) for value in values]

    def to_part(values):
        return [from_partner(value, part_hop) for value in values]

    def add(a, b):
        return a.astype(F32) + b.astype(F32)

    def homeward(rows):
        return rows.astype(BF).reshape(-1, 1, half_cap, rows.shape[-1])

    def back_step(state, chain, step):
        return return_step(state, chains[chain][hop_count - 1 - step])

    def slots_first(state):
        return state.reshape((-1,) + state.shape[2:])

    router_tail = router.astype(BF).reshape(-1, col_count)
    tail_rows = router_tail.shape[0]
    out_low = jnp.concatenate(
        [
            out_weight.astype(BF),
            router_tail,
            jnp.zeros((-tail_rows % 16, col_count), BF),
        ],
        axis=0,
    )
    qkv_low = qkv_weights.astype(BF)
    upstream_a, upstream_b = upstream_call(
        row_table, upstream, row_ids, expert_ids.T[::-1].astype(F32), experts, capacity
    )
    qkv_chains = gather_chains(qkv_low, orders[:3])
    qkv_far = to_core(qkv_chains)
    out_chain = gather_chains(out_low[None], orders[3:])
    out_gathered = (out_chain[0], from_partner(out_chain[0], core_hop))
    qkv_parts = as_halves(qkv_chains, qkv_far, 0)
    tails = [half[:, row_count : row_count + tail_rows] for half in out_gathered]
    full_router = jnp.transpose(
        as_matrix(*tails, slots[3], my_core)
        .reshape(groups, tail_rows, wide_count, col_count)
        .transpose(0, 2, 1, 3)
        .reshape(groups, wide_count, row_count, router.shape[1]),
        (0, 2, 1, 3),
    ).reshape(features, experts)
    router_wide = jnp.pad(full_router, ((0, 0), (0, -experts % LANES)))
    out_halves = out_gathered
    if not direct:
        out_halves = [half[:, :row_count] for half in out_gathered]
        both = as_pairs(as_matrix(*out_halves, slots[3], my_core))
        out_halves = [both[:, 0], both[:, 1]]
    gate_low = gate_weight[0, 0].T.astype(BF)
    up_low = up_weight[0, 0].T.astype(BF)
    down_low = down_weight[0, 0].astype(BF)
    table_hot = (
        jnp.pad(buckets, (0, 1), constant_values=-1)[:, None]
        == jnp.arange(bucket_count, dtype=jnp.int32)[None, :]
    ).astype(F32)
    bias_table = jnp.dot(table_hot, rel_bias, precision=lax.Precision.HIGHEST).T
    (upstream_a, upstream_b), qkv_chains = together((upstream_a, upstream_b), qkv_chains)
    u_state = sends([upstream_a[None], upstream_b[None]], 0)
    normed_in, heads, probs, attended = attend_call(
        table, tokens, attn_gain, bias_table, qkv_parts, groups, head_dim
    )
    u_state, attended = together(u_state, attended)
    u_state = sends(u_state, 1)
    hidden_x1, moe_input, send_a, send_b = post_call(
        table, row_table, tokens, attended, out_halves, moe_gain, row_ids, groups, experts,
        capacity,
    )
    u_state, send_a, send_b = together(u_state, send_a, send_b)
    x_state = [send_a[None], send_b[None]]
    for step in range(hop_count):
        x_state = sends(x_state, step)
        if step + 2 < hop_count:
            u_state = sends(u_state, step + 2)
        elif step + 2 == hop_count:
            u_own = [flat(state) for state in u_state]
            u_core, u_part = to_core(u_own), to_part(u_own)
            x_state, u_core = together(x_state, u_core)
            continue
        if step + 1 < hop_count:
            x_state, u_state = together(x_state, u_state)
    x_state, u_part = together(x_state, u_part)
    x_own = [flat(state) for state in x_state]
    x_core, x_part = to_core(x_own), to_part(x_own)
    u_part_core = to_core(u_part)

    my_expert = (my_narrow + groups * (my_wide // split_parts)).reshape(1).astype(jnp.int32)
    row_total = 8 * x_own[0].shape[0]

    def run_expert(xs, us, first, kept):
        return expert_call(
            my_expert, xs, us, router_wide, gate_low, up_low, down_low, first, row_total, kept
        )

    y_near, dx_near, kept = run_expert(x_own + x_core, u_own + u_core, 0, None)
    x_part, u_part_core, dx_near = together(x_part, u_part_core, dx_near)
    x_part_core = to_core(x_part)
    dx_near_got = to_core(dx_near[2:])
    y_far, parts_back, far_sums = [], [], []
    for chain in range(2):
        xs = [x_part[chain], x_part_core[chain]]
        us = [u_part[chain], u_part_core[chain]]
        if chain:
            xs, far_sums = together(xs, far_sums)
        y_two, dx_two, kept = run_expert(xs, us, 4 + 2 * chain, kept)
        y_far.append(y_two)
        far_sums.append(add(dx_two[0], from_partner(dx_two[1], core_hop)).astype(BF))
        parts_back.append(from_partner(far_sums[chain], part_hop))
    near_sums = [add(mine, got) for mine, got in zip(dx_near[:2], dx_near_got)]
    near_sums, far_sums[1], kept = together(near_sums, far_sums[1], kept)
    y_near_got = to_core(y_near[2:])
    y_far_got = to_core([two[1] for two in y_far])

    x_all, dy_all, hidden_all, dgate_all, dup_all = kept
    backs = [homeward(add(near_sums[0], parts_back[0])), None]
    for step in range(hop_count + 1):
        if step < hop_count:
            backs[0] = back_step(backs[0], 0, step)
        if step == 1:
            backs[1] = homeward(add(near_sums[1], parts_back[1]))
        if step >= 1:
            backs[1] = back_step(backs[1], 1, step - 1)
        if step == 0:
            gate_local = expert_grad_call(dgate_all, x_all)
            up_local = expert_grad_call(dup_all, x_all)
            backs[0], parts_back[1], gate_local, up_local, hidden_all = together(
                backs[0], parts_back[1], gate_local, up_local, hidden_all
            )
        elif step == 1:
            down_local = expert_grad_call(hidden_all, dy_all)
            y_sums = [add(mine, got) for mine, got in zip(y_near[:2], y_near_got)]
            y_far_sums = [
                add(two[0], got).astype(BF) for two, got in zip(y_far, y_far_got)
            ]
            y_sums = [value.astype(BF) for value in y_sums]
            backs, down_local, y_sums, y_far_sums = together(
                backs, down_local, y_sums, y_far_sums
            )
        elif step == 2:
            y_part_got = to_part(y_far_sums)
            squares = [g * g for g in (gate_local, up_local, down_local)]
            local_sums = jnp.stack([jnp.sum(q, axis=0) for q in squares], axis=0)
            part_stats = jnp.stack([jnp.mean(q, axis=1) for q in squares], axis=0) + STAT_EPS
            wide_sums = cube_sum(local_sums, [core_hop])
            backs, wide_sums = together(backs, wide_sums)
        elif step == 3:
            wide_sums = cube_sum(wide_sums, [part_hop])
            wide_stats = wide_sums / (part_width * split_parts) + STAT_EPS
            gate_new = factored(
                gate_weight[0, 0].T, gate_local, part_stats[0], wide_stats[0],
                jnp.mean(wide_stats[0]),
            )
            up_new = factored(
                up_weight[0, 0].T, up_local, part_stats[1], wide_stats[1],
                jnp.mean(wide_stats[1]),
            )
            down_new = factored(
                down_weight[0, 0], down_local, part_stats[2], wide_stats[2],
                jnp.mean(wide_stats[2]),
            )
            backs, gate_new, up_new, down_new = together(backs, gate_new, up_new, down_new)
    inputs_back = [slots_first(state) for state in backs]

    x1_grad, gates, moe_gain_local, router_local, out_keep, out_send, attended_grad = mid_call(
        table, row_table, hidden_x1, moe_gain, moe_input, upstream, inputs_back, row_ids,
        expert_ids, router_wide, attended, out_halves, groups, experts, capacity,
    )
    y_part_got, attended_grad, out_send = together(y_part_got, attended_grad, out_send)
    y_backs = [homeward(add(near, got)) for near, got in zip(y_sums, y_part_got)]
    y_backs = [back_step(state, chain, 0) for chain, state in enumerate(y_backs)]
    out_keep, out_send = halves_of(out_keep, out_send, 3)
    out_half = core_sum(out_keep, out_send, orders[3])

    keeps, qkv_sends, dheads, diag = attend_back_call(
        table, normed_in, heads, probs, attended_grad, groups, head_dim
    )
    y_backs, out_half, qkv_sends = together(y_backs, out_half, qkv_sends)
    if direct:
        summed = core_sum(keeps, qkv_sends, orders[0])
        summed = [summed[m] for m in range(3)]
    else:
        summed = [
            core_sum(*halves_of(keeps[m], qkv_sends[m], m), orders[m]) for m in range(3)
        ]
    summed = summed + [out_half]
    y_backs = [back_step(state, chain, 1) for chain, state in enumerate(y_backs)]
    summed, y_backs = together(summed, y_backs)

    shared = shared_hops(orders)
    stages = range(shared, len(orders[0]) - 1)
    y_step = 2
    for count, stage in enumerate(stages[::-1]):
        summed = [halve(total, order[stage]) for total, order in zip(summed, orders)]
        if y_step < hop_count:
            y_backs = [back_step(state, c, y_step) for c, state in enumerate(y_backs)]
            y_step += 1
        if count == 0:
            tokens_grad, attn_gain_local = tokens_back_call(
                table, tokens, attn_gain, x1_grad, dheads, qkv_parts, groups
            )
            tail = jnp.pad(diag, ((0, 0), (0, 0), (0, 8)))
            line = sum(tail[:, i, i : i + 2 * length] for i in range(8))
            bias_local = jnp.dot(line, table_hot, precision=lax.Precision.HIGHEST).T
            small = jnp.concatenate(
                [
                    attn_gain_local.reshape(-1),
                    moe_gain_local.reshape(-1),
                    bias_local.reshape(-1),
                    router_local[:, :experts].reshape(-1),
                ]
            ).reshape(-1, LANES)
        summed, y_backs, small = together(summed, y_backs, small)
    while y_step < hop_count:
        y_backs = [back_step(state, c, y_step) for c, state in enumerate(y_backs)]
        y_step += 1
    block_out = block_out_call(
        row_table, hidden_x1, gates, [slots_first(state) for state in y_backs], row_ids,
        experts, capacity,
    )
    small_hops = list(orders[0])

    def small_step(value):
        return cube_sum(value, [small_hops.pop(0)]) if small_hops else value

    total = jnp.stack(summed)
    for hop in orders[0][:shared][::-1]:
        total = halve(total, hop, 1)
        small = small_step(small)
        total, small, block_out = together(total, small, block_out)
    dense_mine = total[:, 0]
    blocks = total.astype(BF)
    for hop in orders[0][:shared]:
        blocks = grow(blocks, hop, 1)
        small = small_step(small)
        blocks, small = together(blocks, small)
    dense = [blocks[i] for i in range(4)]
    for stage in stages:
        dense = [grow(chain, order[stage]) for chain, order in zip(dense, orders)]
        small = small_step(small)
        dense, small = together(dense, small)
    small = cube_sum(small, small_hops).reshape(-1)
    dense_parts = as_halves(dense, to_core(dense), 0)
    gain_a_total = small[:features]
    gain_m_total = small[features : 2 * features]
    bias_size = bucket_count * head_count
    bias_total = small[2 * features : 2 * features + bias_size].reshape(bucket_count, head_count)
    router_total = small[2 * features + bias_size :].reshape(features, experts)

    def finish(parts, first, mine, weights, subtract):
        mine_in = mine if direct else None
        grads, rows, cols, new = finish_call(
            table, place, parts, first, groups, features, mine_in, weights, subtract
        )
        if not direct:
            rows_mine = lax.dynamic_slice_in_dim(rows, my_narrow * row_count, row_count, 1)
            cols_mine = lax.dynamic_slice_in_dim(cols, my_wide * col_count, col_count, 1)
            step = adafactor_step(mine, rows_mine, cols_mine, jnp.mean(rows, axis=1))
            new = weights - step if subtract else step
        return grads, rows, cols, new

    out_total, out_rows, out_cols, out_step = finish(
        dense_parts[3:], 3, dense_mine[3:], out_weight[None], False
    )
    qkv_total, qkv_rows, qkv_cols, qkv_new = finish(
        dense_parts[:3], 0, dense_mine[:3], qkv_weights, True
    )
    qkv_stats = jnp.stack([qkv_rows, qkv_cols], axis=0)
    out_stats = jnp.concatenate([out_rows, out_cols], axis=0)
    router_sq = router_total * router_total
    router_rows = jnp.mean(router_sq, axis=1) + STAT_EPS
    router_cols = jnp.mean(router_sq, axis=0) + STAT_EPS
    router_row_count, router_col_count = router.shape
    router_row_first = my_narrow * router_row_count
    router_col_first = my_wide * router_col_count
    router_block = lax.dynamic_slice(
        router_total, (router_row_first, router_col_first), (router_row_count, router_col_count)
    )
    router_new = factored(
        router,
        router_block,
        lax.dynamic_slice_in_dim(router_rows, router_row_first, router_row_count, 0),
        lax.dynamic_slice_in_dim(router_cols, router_col_first, router_col_count, 0),
        jnp.mean(router_rows),
    )
    return (
        block_out,
        tokens_grad,
        gain_a_total,
        qkv_total,
        out_total[0],
        bias_total,
        gain_m_total,
        router_total,
        gate_local.T[None, None],
        up_local.T[None, None],
        down_local[None, None],
        qkv_new,
        out_step[0],
        router_new,
        gate_new.T[None, None],
        up_new.T[None, None],
        down_new[None, None],
        qkv_stats,
        out_stats,
        router_rows,
        router_cols,
        wide_stats[None, None],
        part_stats[None, None],
    )


def solution(mesh):
    in_specs = (
        P(("narrow", "wide"), None),
        P(),
        P(None, "narrow", "wide"),
        P("narrow", "wide"),
        P(),
        P(),
        P("narrow", "wide"),
        P("narrow", "wide", None, None),
        P("narrow", "wide", None, None),
        P("narrow", "wide", None, None),
        P(("narrow", "wide"), None),
        P(("narrow", "wide"), None),
        P(),
        P(("narrow", "wide"), None),
    )
    out_specs = (
        P(("narrow", "wide"), None),
        P(("narrow", "wide"), None),
        P(),
        P(),
        P(),
        P(),
        P(),
        P(),
        P("narrow", "wide", None, None),
        P("narrow", "wide", None, None),
        P("narrow", "wide", None, None),
        P(None, "narrow", "wide"),
        P("narrow", "wide"),
        P("narrow", "wide"),
        P("narrow", "wide", None, None),
        P("narrow", "wide", None, None),
        P("narrow", "wide", None, None),
        P(),
        P(),
        P(),
        P(),
        P("narrow", "wide", None, None),
        P("narrow", "wide", None, None),
    )
    return jax.shard_map(
        on_device, mesh=mesh, in_specs=in_specs, out_specs=out_specs, check_vma=False
    )
```

```python
import functools

import jax
import jax.numpy as jnp
from jax import lax
from jax.experimental import pallas as pl
from jax.experimental.pallas import tpu as pltpu
from jax.sharding import PartitionSpec as P

NORM_EPS = 1e-06
STAT_EPS = 1e-06
STEP_RATE = 0.01
LANES = 128
GELU_C = 0.7978845608028654
GELU_A = 0.044715
BF = jnp.bfloat16
F32 = jnp.float32
NN = (((1,), (0,)), ((), ()))
NT = (((1,), (1,)), ((), ()))
TN = (((0,), (0,)), ((), ()))


def mm(a, b, dims=NN):
    return lax.dot_general(a, b, dims, preferred_element_type=F32)


def from_partner(value, hop):
    axis, bit = hop
    mask = 2**bit
    pairs = [(source, source ^ mask) for source in range(lax.axis_size(axis))]
    return lax.ppermute(value, axis, pairs)


def after(values, *others):
    return lax.optimization_barrier((values, others))[0]


def hop_orders(groups, wide_count):
    narrow = [("narrow", b) for b in range(groups.bit_length() - 1)]
    wide = [("wide", b) for b in range(1, wide_count.bit_length() - 1)]
    far, near = wide[1:][::-1], wide[:1]
    core = [("wide", 0)]
    return (
        far + narrow + near + core,
        far + near + narrow + core,
        far + narrow[1:] + near + narrow[:1] + core,
    )


def row_cuts(count):
    share = -(-count // 48) * 16
    return [min(i * share, count) for i in range(4)]


def block_slots(order, groups, wide_count):
    n_ids = jnp.arange(groups, dtype=jnp.int32)[:, None]
    w_ids = 2 * jnp.arange(wide_count // 2, dtype=jnp.int32)[None, :]
    slots = jnp.zeros((groups, wide_count // 2), jnp.int32)
    for stage, (axis, bit) in enumerate(order[:-1]):
        ids = n_ids if axis == "narrow" else w_ids
        differs = ((ids ^ lax.axis_index(axis)) >> bit) & 1
        slots = slots | (differs << stage)
    return slots


def together(*values):
    return lax.optimization_barrier(values)


def shared_hops(orders):
    count = 0
    while len({order[count] for order in orders}) == 1 and count < len(orders[0]) - 1:
        count += 1
    return count


def grow(blocks, got, axis=0):
    return jnp.concatenate([blocks, got], axis=axis)


def core_sum(keep, got):
    return keep + got.astype(F32)


def halve_send(total, hop, axis=0):
    half = total.shape[axis] // 2
    return from_partner(lax.slice_in_dim(total, half, 2 * half, axis=axis).astype(BF), hop)


def halve_add(total, got, axis=0):
    half = total.shape[axis] // 2
    return lax.slice_in_dim(total, 0, half, axis=axis) + got.astype(F32)


def row_send(state, hop):
    sources, places = state.shape[:2]
    return from_partner(state.reshape((sources, 2, places // 2) + state.shape[2:])[:, 1], hop)


def row_join(state, got):
    sources, places = state.shape[:2]
    kept = state.reshape((sources, 2, places // 2) + state.shape[2:])[:, 0]
    return jnp.concatenate([kept, got], axis=0)


def back_split(state, left, hop):
    low = 2 ** left.index(hop)
    split = state.reshape((-1, 2, low) + state.shape[1:])
    return [split[:, i].reshape((-1,) + state.shape[1:]) for i in range(2)]


def back_send(state, left, hop):
    return from_partner(back_split(state, left, hop)[1], hop)


def back_join(state, left, hop, got):
    kept = back_split(state, left, hop)[0]
    joined = jnp.stack([kept, got], axis=1).reshape((got.shape[0], -1) + state.shape[2:])
    return joined, [other for other in left if other != hop]


def row_slots(hops, groups, places, parts):
    n_ids = jnp.arange(groups, dtype=jnp.int32)[:, None]
    w_ids = parts * jnp.arange(places, dtype=jnp.int32)[None, :]
    slots = jnp.zeros((groups, places), jnp.int32)
    for axis, bit in hops:
        ids = n_ids if axis == "narrow" else w_ids
        slots = 2 * slots + (((ids ^ lax.axis_index(axis)) >> bit) & 1)
    return slots.reshape(-1)


def cube_sum(value, hops):
    for hop in hops:
        value = value + from_partner(value, hop)
    return value


def as_matrix(own, other, slots, my_core):
    groups, half_wide = slots.shape
    both = jnp.stack([jnp.where(my_core == 0, own, other), jnp.where(my_core == 0, other, own)], 1)
    picked = jnp.take(both, slots.reshape(-1), axis=0)
    rows, cols = own.shape[1:]
    picked = picked.reshape(groups, half_wide, 2, rows, cols)
    return jnp.transpose(picked, (0, 3, 1, 2, 4)).reshape(groups * rows, half_wide * 2 * cols)


def from_matrix(matrix, groups, half_wide):
    lead = matrix.shape[:-2]
    rows, cols = matrix.shape[-2] // groups, matrix.shape[-1] // (2 * half_wide)
    shaped = matrix.reshape(lead + (groups, rows, half_wide, 2, cols))
    k = len(lead)
    order = tuple(range(k)) + (k, k + 2, k + 3, k + 1, k + 4)
    return jnp.transpose(shaped, order)


def gelu_tanh(values):
    return jax.nn.gelu(values, approximate=True)


def adafactor_step(gradient, row_stats, col_stats, mean_rows):
    return (
        STEP_RATE
        * gradient
        / jnp.sqrt(row_stats[..., :, None] * col_stats[..., None, :] / mean_rows[..., None, None])
    )


def factored(weight, gradient, row_stats, col_stats, mean_rows):
    return weight - adafactor_step(gradient, row_stats, col_stats, mean_rows)


def vmem():
    return pl.BlockSpec(memory_space=pltpu.VMEM)


def smem():
    return pl.BlockSpec(memory_space=pltpu.SMEM)


def params(mebibytes):
    return pltpu.CompilerParams(vmem_limit_bytes=mebibytes * 1024 * 1024)


def cost(micros):
    return pl.CostEstimate(
        flops=int(micros * 1153e6), transcendentals=0, bytes_accessed=int(micros * 3690e3)
    )


def lane_masks(head_dim):
    heads = LANES // head_dim
    ids = lax.broadcasted_iota(jnp.int32, (1, LANES), 1) // head_dim
    return [ids == i for i in range(heads)]


def attend_body(
    table_ref, tokens_ref, gain_ref, bias_ref,
    own_q, own_k, own_v, far_q, far_k, far_v,
    normed_ref, heads_ref, probs_ref, attended_ref,
    *, groups, pairs, head_dim,
):
    length, features = tokens_ref.shape
    rows = features // groups
    x = tokens_ref[...].astype(F32)
    factor = lax.rsqrt(jnp.mean(x * x, axis=-1, keepdims=True) + NORM_EPS)
    normed_ref[...] = (x * factor * gain_ref[...]).astype(BF)
    core = table_ref[0]

    def project(w2, carry):
        for m, (own, far) in enumerate(((own_q, far_q), (own_k, far_k), (own_v, far_v))):
            total = None
            for n in range(groups):
                at = table_ref[1 + (m * groups + n) * pairs + w2]
                block = jnp.concatenate([own[at, :rows], far[at, :rows]], axis=1)
                part = mm(normed_ref[:, n * rows : (n + 1) * rows], block)
                total = part if total is None else total + part
            total = total.astype(BF)
            heads_ref[m, 2 * w2 + core] = total[:, :LANES]
            heads_ref[m, 2 * w2 + 1 - core] = total[:, LANES:]
        return carry

    lax.fori_loop(0, pairs, project, 0)
    masks = lane_masks(head_dim)
    scale = head_dim**-0.5

    def attend(w, carry):
        q, k, v = heads_ref[0, w], heads_ref[1, w], heads_ref[2, w]
        mixed = jnp.zeros((length, LANES), F32)
        for i, mask in enumerate(masks):
            head = w * len(masks) + i
            raw = mm(jnp.where(mask, q, jnp.zeros_like(q)), k, NT)
            line = jnp.broadcast_to(bias_ref[pl.ds(head, 1), :], (length, 2 * length))
            bias = pltpu.roll(line, length + 1, 1, stride=1, stride_axis=0)[:, :length]
            scores = raw * scale + bias
            top = jnp.max(scores, axis=-1, keepdims=True)
            grown = jnp.exp(scores - top)
            probs = grown / jnp.sum(grown, axis=-1, keepdims=True)
            probs_ref[head] = probs
            mixed = jnp.where(mask, mm(probs.astype(BF), v), mixed)
        attended_ref[w] = mixed.astype(BF)
        return carry

    lax.fori_loop(0, 2 * pairs, attend, 0)


def attend_call(table, tokens, gain, bias_table, gathered, groups, head_dim):
    length, features = tokens.shape
    pairs = features // (2 * LANES)
    head_count = features // head_dim
    owns = [g[0] for g in gathered]
    fars = [g[1] for g in gathered]
    body = functools.partial(attend_body, groups=groups, pairs=pairs, head_dim=head_dim)
    return pl.pallas_call(
        body,
        in_specs=[smem()] + [vmem()] * 9,
        out_specs=[vmem()] * 4,
        out_shape=[
            jax.ShapeDtypeStruct((length, features), BF),
            jax.ShapeDtypeStruct((3, 2 * pairs, length, LANES), BF),
            jax.ShapeDtypeStruct((head_count, length, length), F32),
            jax.ShapeDtypeStruct((2 * pairs, length, LANES), BF),
        ],
        compiler_params=params(14),
        name="attend",
        cost_estimate=cost(16),
    )(table, tokens, gain.reshape(1, features), bias_table, *owns, *fars)


def expert_hot(ids_ref, expert, cap, length):
    slot = lax.broadcasted_iota(jnp.int32, (cap, length), 0) + expert * cap
    return [slot == ids_ref[c : c + 1, :] for c in range(2)]


def spread_rows(values, ids_ref, slots_ref, sends, experts, cap):
    length, features = values.shape
    half = cap // 2
    for e in range(experts):
        first, second = expert_hot(ids_ref, e, cap, length)
        rows = mm(jnp.where(first | second, 1.0, 0.0).astype(BF), values)
        for chain, send in enumerate(sends):
            at = slots_ref[chain * experts + e]
            send[at, :, :features] = rows[chain * half : (chain + 1) * half].astype(BF)


def upstream_body(slots_ref, values_ref, ids_ref, others_ref, send_a, send_b, *, experts, cap):
    length, features = values_ref.shape
    half = cap // 2
    spread_rows(values_ref[...], ids_ref, slots_ref, (send_a, send_b), experts, cap)
    for e in range(experts):
        first, second = expert_hot(ids_ref, e, cap, length)
        other = jnp.where(first, others_ref[0:1, :], 0.0) + jnp.where(
            second, others_ref[1:2, :], 0.0
        )
        other = jnp.sum(other, axis=1, keepdims=True)
        other = jnp.broadcast_to(other, (cap, LANES))
        for chain, send in enumerate((send_a, send_b)):
            at = slots_ref[chain * experts + e]
            send[at, :, features:] = other[chain * half : (chain + 1) * half].astype(BF)


def upstream_call(row_table, upstream, row_ids, other_ids, experts, cap):
    features = upstream.shape[1]
    return pl.pallas_call(
        functools.partial(upstream_body, experts=experts, cap=cap),
        in_specs=[smem()] + [vmem()] * 3,
        out_specs=[vmem()] * 2,
        out_shape=[jax.ShapeDtypeStruct((experts, cap // 2, features + LANES), BF)] * 2,
        compiler_params=params(8),
        name="upstream_rows",
        cost_estimate=cost(3),
    )(row_table, upstream, row_ids, other_ids)


def projection_block(halves, table_ref, n, w2, groups, pairs, depth, cuts):
    sides = []
    for refs in halves:
        parts = []
        for i in range(3):
            at = table_ref[1 + (i * groups + n) * pairs + w2]
            first = depth if refs[i].shape[1] > depth else 0
            parts.append(refs[i][at, first : first + cuts[i + 1] - cuts[i]])
        sides.append(jnp.concatenate(parts, axis=0))
    return jnp.concatenate(sides, axis=1)


def post_body(
    table_ref, slots_ref, tokens_ref, attended_ref,
    own_q, own_k, own_v, far_q, far_k, far_v, gain_ref, ids_ref,
    x1_ref, normed_ref, send_a, send_b,
    *, groups, experts, cap, cuts,
):
    length, features = tokens_ref.shape
    pairs = features // (2 * LANES)
    per_group = 2 * pairs // groups
    depth = features // groups
    halves = ((own_q, own_k, own_v), (far_q, far_k, far_v))
    core = table_ref[0]
    rows = [
        jnp.concatenate([attended_ref[n * per_group + i] for i in range(per_group)], axis=1)
        for n in range(groups)
    ]
    for w2 in range(pairs):
        total = None
        for n in range(groups):
            block = projection_block(halves, table_ref, n, w2, groups, pairs, depth, cuts)
            part = mm(rows[n], block)
            total = part if total is None else total + part
        for j in range(2):
            w = 2 * w2 + (core if j == 0 else 1 - core)
            place = pl.multiple_of(w * LANES, LANES)
            mine = total[:, j * LANES : (j + 1) * LANES]
            x1_ref[:, pl.ds(place, LANES)] = mine + tokens_ref[:, pl.ds(place, LANES)].astype(F32)
    x1 = x1_ref[...]
    factor = lax.rsqrt(jnp.mean(x1 * x1, axis=-1, keepdims=True) + NORM_EPS)
    normed = (x1 * factor * gain_ref[...]).astype(BF)
    normed_ref[...] = normed
    spread_rows(normed, ids_ref, slots_ref, (send_a, send_b), experts, cap)


def post_call(table, row_table, tokens, attended, gathered, gain, row_ids, groups, experts, cap):
    length, features = tokens.shape
    owns = [g[0] for g in gathered]
    fars = [g[1] for g in gathered]
    cuts = row_cuts(features // groups)
    return pl.pallas_call(
        functools.partial(post_body, groups=groups, experts=experts, cap=cap, cuts=cuts),
        in_specs=[smem()] * 2 + [vmem()] * 10,
        out_specs=[vmem()] * 4,
        out_shape=[
            jax.ShapeDtypeStruct((length, features), F32),
            jax.ShapeDtypeStruct((length, features), BF),
            jax.ShapeDtypeStruct((experts, cap // 2, features), BF),
            jax.ShapeDtypeStruct((experts, cap // 2, features), BF),
        ],
        compiler_params=params(12),
        name="post",
        cost_estimate=cost(3),
    )(
        table, row_table, tokens, attended, *owns, *fars, gain.reshape(1, features), row_ids
    )


def mid_body(
    table_ref, slots_ref, x1_ref, gain_ref, normed_ref, upstream_ref, back_a, back_b,
    ids_ref, choice_ref, router_ref, attended_ref,
    own_q, own_k, own_v, far_q, far_k, far_v,
    x1_grad_ref, gates_ref, gain_out_ref, router_out_ref, keep_ref, send_ref, att_grad_ref,
    *, groups, experts, cap, cuts,
):
    length, features = x1_ref.shape
    pairs = features // (2 * LANES)
    per_group = 2 * pairs // groups
    rows = features // groups
    half = cap // 2
    halves = ((own_q, own_k, own_v), (far_q, far_k, far_v))
    core = table_ref[0]
    dmoe = jnp.zeros((length, features), F32)
    dots = [jnp.zeros((length, LANES), F32)] * 2
    for e in range(experts):
        hots = expert_hot(ids_ref, e, cap, length)
        hots = [jnp.where(hot, 1.0, 0.0).astype(BF) for hot in hots]
        both = hots[0] + hots[1]
        for chain, back in enumerate((back_a, back_b)):
            at = slots_ref[chain * experts + e]
            part = slice(chain * half, (chain + 1) * half)
            got = back[at]
            dmoe = dmoe + mm(both[part], got[:, :features], TN)
            for c in range(2):
                dots[c] = dots[c] + mm(hots[c][part], got[:, features:], TN)
    normed = normed_ref[...]
    logits = mm(normed, router_ref[...])
    lane = lax.broadcasted_iota(jnp.int32, logits.shape, 1)
    picks = [lane == choice_ref[:, c : c + 1] for c in range(2)]
    picked = [jnp.sum(jnp.where(pick, logits, 0.0), axis=1, keepdims=True) for pick in picks]
    top = jnp.maximum(picked[0], picked[1])
    grown = [jnp.exp(value - top) for value in picked]
    gates = [value / (grown[0] + grown[1]) for value in grown]
    gates_ref[...] = jnp.where(lane == 0, gates[0], jnp.where(lane == 1, gates[1], 0.0))
    dgates = [dot[:, 0:1] for dot in dots]
    inner = gates[0] * dgates[0] + gates[1] * dgates[1]
    dlogits = jnp.where(picks[0], gates[0] * (dgates[0] - inner), 0.0) + jnp.where(
        picks[1], gates[1] * (dgates[1] - inner), 0.0
    )
    dlogits = dlogits.astype(BF)
    router_out_ref[...] = mm(dlogits, normed, TN)
    dmoe = dmoe + mm(dlogits, router_ref[...], NT)
    x1 = x1_ref[...]
    factor = lax.rsqrt(jnp.mean(x1 * x1, axis=-1, keepdims=True) + NORM_EPS)
    hat = x1 * factor
    gain_out_ref[...] = jnp.sum(dmoe * hat, axis=0, keepdims=True)
    scaled = dmoe * gain_ref[...]
    inner = jnp.mean(scaled * hat, axis=-1, keepdims=True)
    x1_grad_ref[...] = upstream_ref[...].astype(F32) + factor * (scaled - hat * inner)
    branches = []
    for w2 in range(pairs):
        both = []
        for j in range(2):
            w = 2 * w2 + (core if j == 0 else 1 - core)
            both.append(x1_grad_ref[:, pl.ds(pl.multiple_of(w * LANES, LANES), LANES)].astype(BF))
        branches.append(jnp.concatenate(both, axis=1))
    for n in range(groups):
        att = jnp.concatenate(
            [attended_ref[n * per_group + i] for i in range(per_group)], axis=1
        )
        total = None
        for w2 in range(pairs):
            block = mm(att, branches[w2], TN)
            for i in range(3):
                at = table_ref[1 + (i * groups + n) * pairs + w2]
                keep_ref[at, cuts[i] : cuts[i + 1]] = block[cuts[i] : cuts[i + 1], :LANES]
                send = block[cuts[i] : cuts[i + 1], LANES:].astype(BF)
                send_ref[at, cuts[i] : cuts[i + 1]] = send
            block = projection_block(halves, table_ref, n, w2, groups, pairs, rows, cuts)
            part = mm(branches[w2], block, NT)
            total = part if total is None else total + part
        for i in range(per_group):
            att_grad_ref[n * per_group + i] = total[:, i * LANES : (i + 1) * LANES].astype(BF)


def mid_call(
    table, row_table, x1, gain, normed, upstream, backs, row_ids, choices, router, attended,
    gathered, groups, experts, cap,
):
    length, features = x1.shape
    pairs = features // (2 * LANES)
    rows = features // groups
    owns = [g[0] for g in gathered]
    fars = [g[1] for g in gathered]
    return pl.pallas_call(
        functools.partial(
            mid_body, groups=groups, experts=experts, cap=cap, cuts=row_cuts(rows)
        ),
        in_specs=[smem()] * 2 + [vmem()] * 16,
        out_specs=[vmem()] * 7,
        out_shape=[
            jax.ShapeDtypeStruct((length, features), F32),
            jax.ShapeDtypeStruct((length, LANES), F32),
            jax.ShapeDtypeStruct((1, features), F32),
            jax.ShapeDtypeStruct((LANES, features), F32),
            jax.ShapeDtypeStruct((groups * pairs, rows, LANES), F32),
            jax.ShapeDtypeStruct((groups * pairs, rows, LANES), BF),
            jax.ShapeDtypeStruct((2 * pairs, length, LANES), BF),
        ],
        compiler_params=params(16),
        name="mid",
        cost_estimate=cost(7),
    )(
        table, row_table, x1, gain.reshape(1, features), normed, upstream, *backs,
        row_ids, choices, router, attended, *owns, *fars,
    )


def block_out_body(
    slots_ref, x1_ref, gates_ref, back_a, back_b, ids_ref, out_ref, *, experts, cap
):
    length, features = x1_ref.shape
    half = cap // 2
    sums = [jnp.zeros((length, features), F32)] * 2
    for e in range(experts):
        hots = [
            jnp.where(hot, 1.0, 0.0).astype(BF) for hot in expert_hot(ids_ref, e, cap, length)
        ]
        for chain, back in enumerate((back_a, back_b)):
            got = back[slots_ref[chain * experts + e]]
            part = slice(chain * half, (chain + 1) * half)
            sums = [total + mm(hot[part], got, TN) for total, hot in zip(sums, hots)]
    moe = gates_ref[:, 0:1] * sums[0] + gates_ref[:, 1:2] * sums[1]
    out_ref[...] = (x1_ref[...] + moe).astype(BF)


def block_out_call(row_table, x1, gates, backs, row_ids, experts, cap):
    return pl.pallas_call(
        functools.partial(block_out_body, experts=experts, cap=cap),
        in_specs=[smem()] + [vmem()] * 5,
        out_specs=vmem(),
        out_shape=jax.ShapeDtypeStruct(x1.shape, BF),
        compiler_params=params(8),
        name="block_out",
        cost_estimate=cost(7),
    )(row_table, x1, gates, *backs, row_ids)


def attend_back_body(
    table_ref, normed_ref, heads_ref, probs_ref, grad_ref, out_keep_ref, out_send_ref,
    keep_q, keep_k, keep_v, send_q, send_k, send_v, dheads_ref, diag_ref,
    *, groups, pairs, head_dim, cuts,
):
    length, features = normed_ref.shape
    rows = features // groups
    keeps, sends = (keep_q, keep_k, keep_v), (send_q, send_k, send_v)
    for i in range(3):
        keeps[i][:, rows:] = out_keep_ref[:, cuts[i] : cuts[i + 1]]
        sends[i][:, rows:] = out_send_ref[:, cuts[i] : cuts[i + 1]]
    masks = lane_masks(head_dim)
    scale = head_dim**-0.5

    def back(w, carry):
        q, k, v = heads_ref[0, w], heads_ref[1, w], heads_ref[2, w]
        da = grad_ref[w]
        dq = jnp.zeros((length, LANES), F32)
        dk, dv = dq, dq
        for i, mask in enumerate(masks):
            head = w * len(masks) + i
            probs = probs_ref[head]
            dp = mm(jnp.where(mask, da, jnp.zeros_like(da)), v, NT)
            spread = jnp.sum(probs * dp, axis=-1, keepdims=True)
            ds = (probs * (dp - spread)).astype(BF)
            dq = jnp.where(mask, mm(ds, k), dq)
            dk = jnp.where(mask, mm(ds, q, TN), dk)
            dv = jnp.where(mask, mm(probs.astype(BF), da, TN), dv)
            wide_ds = jnp.concatenate([ds.astype(F32), jnp.zeros((length, length), F32)], axis=1)
            diag = jnp.zeros((8, 2 * length), F32)
            for g in range(length // 8):
                diag = diag + pltpu.roll(wide_ds[8 * g : 8 * g + 8], length - 1 - 8 * g, 1)
            diag_ref[head] = diag
        dheads_ref[0, w] = (dq * scale).astype(BF)
        dheads_ref[1, w] = (dk * scale).astype(BF)
        dheads_ref[2, w] = dv.astype(BF)
        return carry

    lax.fori_loop(0, 2 * pairs, back, 0)
    core = table_ref[0]

    def weigh(w2, carry):
        for m in range(3):
            both = jnp.concatenate(
                [dheads_ref[m, 2 * w2 + core], dheads_ref[m, 2 * w2 + 1 - core]], axis=1
            )
            for n in range(groups):
                at = table_ref[1 + (m * groups + n) * pairs + w2]
                block = mm(normed_ref[:, n * rows : (n + 1) * rows], both, TN)
                keeps[m][at, :rows] = block[:, :LANES]
                sends[m][at, :rows] = block[:, LANES:].astype(BF)
        return carry

    lax.fori_loop(0, pairs, weigh, 0)


def attend_back_call(
    table, normed, heads, probs, attended_grad, out_keep, out_send, groups, head_dim
):
    length, features = normed.shape
    pairs = features // (2 * LANES)
    head_count = features // head_dim
    rows = features // groups
    cuts = row_cuts(rows)
    body = functools.partial(
        attend_back_body, groups=groups, pairs=pairs, head_dim=head_dim, cuts=cuts
    )
    shapes = [(groups * pairs, rows + b - a, LANES) for a, b in zip(cuts[:-1], cuts[1:])]
    return pl.pallas_call(
        body,
        in_specs=[smem()] + [vmem()] * 6,
        out_specs=[vmem()] * 8,
        out_shape=[jax.ShapeDtypeStruct(shape, F32) for shape in shapes]
        + [jax.ShapeDtypeStruct(shape, BF) for shape in shapes]
        + [
            jax.ShapeDtypeStruct((3, 2 * pairs, length, LANES), BF),
            jax.ShapeDtypeStruct((head_count, 8, 2 * length), F32),
        ],
        compiler_params=params(22),
        name="attend_back",
        cost_estimate=cost(12),
    )(table, normed, heads, probs, attended_grad, out_keep, out_send)


def tokens_back_body(
    table_ref, tokens_ref, gain_ref, x1_grad_ref, dheads_ref,
    own_q, own_k, own_v, far_q, far_k, far_v,
    out_ref, gain_out_ref, acc_ref,
    *, groups, pairs,
):
    length, features = tokens_ref.shape
    rows = features // groups
    core = table_ref[0]
    for n in range(groups):

        def step(w2, total):
            for m, (own, far) in enumerate(((own_q, far_q), (own_k, far_k), (own_v, far_v))):
                at = table_ref[1 + (m * groups + n) * pairs + w2]
                both = jnp.concatenate(
                    [dheads_ref[m, 2 * w2 + core], dheads_ref[m, 2 * w2 + 1 - core]], axis=1
                )
                block = jnp.concatenate([own[at, :rows], far[at, :rows]], axis=1)
                total = total + mm(both, block, NT)
            return total

        total = lax.fori_loop(0, pairs, step, jnp.zeros((length, rows), F32))
        acc_ref[:, n * rows : (n + 1) * rows] = total
    x = tokens_ref[...].astype(F32)
    factor = lax.rsqrt(jnp.mean(x * x, axis=-1, keepdims=True) + NORM_EPS)
    hat = x * factor
    grad = acc_ref[...]
    gain_out_ref[...] = jnp.sum(grad * hat, axis=0, keepdims=True)
    scaled = grad * gain_ref[...]
    inner = jnp.mean(scaled * hat, axis=-1, keepdims=True)
    out_ref[...] = (x1_grad_ref[...] + factor * (scaled - hat * inner)).astype(BF)


def tokens_back_call(table, tokens, gain, x1_grad, dheads, gathered, groups):
    length, features = tokens.shape
    pairs = features // (2 * LANES)
    owns = [g[0] for g in gathered]
    fars = [g[1] for g in gathered]
    return pl.pallas_call(
        functools.partial(tokens_back_body, groups=groups, pairs=pairs),
        in_specs=[smem()] + [vmem()] * 10,
        out_specs=[vmem()] * 2,
        out_shape=[
            jax.ShapeDtypeStruct((length, features), BF),
            jax.ShapeDtypeStruct((1, features), F32),
        ],
        scratch_shapes=[pltpu.VMEM((length, features), F32)],
        compiler_params=params(14),
        name="tokens_back",
        cost_estimate=cost(10),
    )(table, tokens, gain.reshape(1, features), x1_grad, dheads, *owns, *fars)


def choose(refs, which):
    value = refs[0][...]
    for i in range(1, len(refs)):
        value = jnp.where(which == i, refs[i][...], value)
    return value


def expert_body(expert_ref, *refs, count):
    x_refs, up_refs, refs = refs[:count], refs[count : 2 * count], refs[2 * count :]
    router_ref, gate_w, up_w, down_w = refs[:4]
    y_refs, dx_refs = refs[-2 * count - 5 : -count - 5], refs[-count - 5 : -5]
    x_out, dy_ref, hidden_ref, dgate_ref, dup_ref = refs[-5:]
    piece = pl.program_id(0)
    x = choose(x_refs, piece)
    up = choose(up_refs, piece)
    x_out[...] = x
    features = x.shape[1]
    logits = mm(x, router_ref[...])
    lane = lax.broadcasted_iota(jnp.int32, logits.shape, 1)
    other_id = up[:, features : features + 1].astype(jnp.int32)
    mine = jnp.sum(jnp.where(lane == expert_ref[0], logits, 0.0), axis=1, keepdims=True)
    other = jnp.sum(jnp.where(lane == other_id, logits, 0.0), axis=1, keepdims=True)
    top = jnp.maximum(mine, other)
    mine_e = jnp.exp(mine - top)
    gate = mine_e / (mine_e + jnp.exp(other - top))
    grad = up[:, :features].astype(F32)
    dy = (gate * grad).astype(BF)
    dy_ref[...] = dy
    step = 2 * LANES
    width = gate_w.shape[0]
    for f in range(0, width, step):
        chunk = slice(f, min(f + step, width))
        g = mm(x, gate_w[chunk, :], NT)
        u = mm(x, up_w[chunk, :], NT)
        dh = mm(dy, down_w[chunk, :], NT)
        square = g * g
        t = jnp.tanh(g * (GELU_C + (GELU_C * GELU_A) * square))
        half_t = 0.5 + 0.5 * t
        act = g * half_t
        slope = half_t + act * ((1.0 - t) * (GELU_C + (3.0 * GELU_C * GELU_A) * square))
        hidden_ref[:, chunk] = (act * u).astype(BF)
        dgate_ref[:, chunk] = (dh * u * slope).astype(BF)
        dup_ref[:, chunk] = (dh * act).astype(BF)
    y = mm(hidden_ref[...], down_w[...]).astype(BF)
    dx = mm(dgate_ref[...], gate_w[...]) + mm(dup_ref[...], up_w[...])
    dot = jnp.sum(grad * y.astype(F32), axis=1, keepdims=True)
    dx = dx.astype(BF)
    dot = jnp.broadcast_to(dot, (x.shape[0], LANES)).astype(BF)
    for i in range(count):

        @pl.when(piece == i)
        def _(i=i):
            y_refs[i][...] = y
            dx_refs[i][:, :features] = dx
            dx_refs[i][:, features:] = dot


def expert_call(expert, xs, upstreams, router, gate_w, up_w, down_w, first, total, kept):
    rows, features = xs[0].shape
    width = gate_w.shape[0]
    count = len(xs)

    def whole(arr):
        return pl.BlockSpec(arr.shape, lambda i, e: (0, 0), pipeline_mode=pl.Buffered(1))

    def kept_spec(cols):
        return pl.BlockSpec((rows, cols), lambda i, e: (first + i, 0))

    kept_cols = (features, features, width, width, width)
    kept_in = [] if kept is None else list(kept)
    inputs = list(xs) + list(upstreams) + [router, gate_w, up_w, down_w]
    out = pl.pallas_call(
        functools.partial(expert_body, count=count),
        grid_spec=pltpu.PrefetchScalarGridSpec(
            num_scalar_prefetch=1,
            grid=(count,),
            in_specs=[whole(arr) for arr in inputs]
            + [pl.BlockSpec(memory_space=pl.ANY)] * len(kept_in),
            out_specs=[pl.BlockSpec((rows, features), lambda i, e: (0, 0))] * count
            + [pl.BlockSpec((rows, features + LANES), lambda i, e: (0, 0))] * count
            + [kept_spec(cols) for cols in kept_cols],
        ),
        out_shape=[jax.ShapeDtypeStruct((rows, features), BF)] * count
        + [jax.ShapeDtypeStruct((rows, features + LANES), BF)] * count
        + [jax.ShapeDtypeStruct((total, cols), BF) for cols in kept_cols],
        input_output_aliases={
            1 + len(inputs) + i: 2 * count + i for i in range(len(kept_in))
        },
        compiler_params=params(48),
        name="expert",
        cost_estimate=cost(6 * count),
    )(expert, *inputs, *kept_in)
    return out[:count], out[count : 2 * count], out[2 * count :]


def expert_grad_body(left_ref, right_ref, out_ref):
    out_ref[...] = mm(left_ref[...], right_ref[...], TN)


def expert_grad_call(left, right):
    rows, features = right.shape
    width = left.shape[1]
    size = 2 * LANES
    return pl.pallas_call(
        expert_grad_body,
        grid=(features // size,),
        in_specs=[
            pl.BlockSpec((rows, width), lambda i: (0, 0)),
            pl.BlockSpec((rows, size), lambda i: (0, i)),
        ],
        out_specs=pl.BlockSpec((width, size), lambda i: (0, i)),
        out_shape=jax.ShapeDtypeStruct((width, features), F32),
        compiler_params=params(30),
        name="expert_grad",
        cost_estimate=cost(9),
    )(left, right)


def finish_body(
    table_ref, place_ref, own_q, own_k, own_v, far_q, far_k, far_v, *refs,
    groups, pairs, cuts, update,
):
    if update:
        mine_ref, weight_ref, refs = refs[0], refs[1], refs[2:]
    qkv_ref, out_ref, rows_ref, cols_ref = refs[:4]
    new_ref = refs[4] if update else None
    acc_ref, line_ref = refs[-2:]
    features = acc_ref.shape[0]
    rows = features // groups
    core = table_ref[0]
    chunk = 32

    def fill(grads_ref, source_of, n, start, stop, cols):
        def step(c, cols):
            first = pl.multiple_of(c * chunk, chunk)
            total = jnp.zeros((chunk, LANES), F32)
            grown = []
            for index in range(2 * pairs):
                w2, j = index // 2, index % 2
                block = source_of(n, w2, j, first).astype(F32)
                w = 2 * w2 + (core if j == 0 else 1 - core)
                place = pl.multiple_of(w * LANES, LANES)
                grads_ref[pl.ds(n * rows + first, chunk), pl.ds(place, LANES)] = block
                square = block * block
                total = total + square
                grown.append(cols[index] + jnp.sum(square.reshape(-1, 8, LANES), axis=0))
            acc_ref[pl.ds(n * rows + first, chunk), :] = total
            return tuple(grown)

        return lax.fori_loop(start // chunk, stop // chunk, step, cols)

    def matrix(m, grads_ref, pieces):
        cols = tuple(jnp.zeros((8, LANES), F32) for _ in range(2 * pairs))
        for n in range(groups):
            for chain, start, stop, shift, own, far in pieces:

                def source_of(n, w2, j, first, chain=chain, shift=shift, own=own, far=far):
                    at = table_ref[1 + (chain * groups + n) * pairs + w2]
                    ref = own if j == 0 else far
                    return ref[at, pl.ds(pl.multiple_of(first + shift, 16), chunk), :]

                cols = fill(grads_ref, source_of, n, start, stop, cols)
        for index in range(2 * pairs):
            w = 2 * (index // 2) + (core if index % 2 == 0 else 1 - core)
            total = jnp.sum(cols[index], axis=0, keepdims=True)
            cols_ref[0, w] = total / features + STAT_EPS
        squares = acc_ref[...]
        sums = lax.dot_general(
            jnp.ones((8, LANES), F32), squares, NT,
            precision=lax.Precision.HIGHEST, preferred_element_type=F32,
        )
        rows_ref[0] = sums / features + STAT_EPS
        if update:
            line = jnp.sum(squares, axis=1, keepdims=True) / features + STAT_EPS
            line_ref[...] = jnp.broadcast_to(line, line_ref.shape)
            mean = jnp.sum(line, axis=0, keepdims=True) / features
            my_rows = line_ref[pl.ds(pl.multiple_of(place_ref[0] * rows, rows), rows), :]
            my_cols = cols_ref[0, place_ref[1]]
            step = STEP_RATE * mine_ref[0] / jnp.sqrt(my_rows * my_cols / mean)
            new_ref[0] = weight_ref[0] - step if m < 3 else step

    owns, fars = (own_q, own_k, own_v), (far_q, far_k, far_v)
    for m in range(4):

        @pl.when(pl.program_id(0) == m)
        def _(m=m):
            if m < 3:
                matrix(m, qkv_ref.at[0], [(m, 0, rows, 0, owns[m], fars[m])])
            else:
                pieces = [
                    (i, cuts[i], cuts[i + 1], rows - cuts[i], owns[i], fars[i]) for i in range(3)
                ]
                matrix(m, out_ref, pieces)


def finish_call(table, place, gathered, groups, features, mine, weights):
    pairs = features // (2 * LANES)
    rows = features // groups
    owns = [g[0] for g in gathered]
    fars = [g[1] for g in gathered]
    update = mine is not None
    extra = [mine, weights] if update else []
    block = pl.BlockSpec((1, rows, LANES), lambda m: (m, 0, 0))
    shapes = [
        jax.ShapeDtypeStruct((3, features, features), F32),
        jax.ShapeDtypeStruct((features, features), F32),
        jax.ShapeDtypeStruct((4, 8, features), F32),
        jax.ShapeDtypeStruct((4, 2 * pairs, 1, LANES), F32),
    ]
    specs = [
        pl.BlockSpec((1, features, features), lambda m: (jnp.minimum(m, 2), 0, 0)),
        pl.BlockSpec((features, features), lambda m: (0, 0)),
        pl.BlockSpec((1, 8, features), lambda m: (m, 0, 0)),
        pl.BlockSpec((1, 2 * pairs, 1, LANES), lambda m: (m, 0, 0, 0)),
    ]
    if update:
        shapes.append(jax.ShapeDtypeStruct((4, rows, LANES), F32))
        specs.append(block)

    out = pl.pallas_call(
        functools.partial(
            finish_body, groups=groups, pairs=pairs, cuts=row_cuts(rows), update=update
        ),
        grid=(4,),
        in_specs=[smem()] * 2 + [vmem()] * 6 + [block] * len(extra),
        out_specs=specs,
        out_shape=shapes,
        scratch_shapes=[pltpu.VMEM((features, LANES), F32)] * 2,
        compiler_params=params(26),
        name="finish",
        cost_estimate=cost(10),
    )(table, place, *owns, *fars, *extra)
    stats = (out[0], out[1], out[2][:, 0], out[3].reshape(4, features))
    return stats + (out[4] if update else None,)


def on_device(
    tokens,
    attn_gain,
    qkv_weights,
    out_weight,
    rel_bias,
    moe_gain,
    router,
    gate_weight,
    up_weight,
    down_weight,
    expert_ids,
    expert_slots,
    buckets,
    upstream,
):
    length, features = tokens.shape
    bucket_count, head_count = rel_bias.shape
    head_dim = features // head_count
    groups = lax.axis_size("narrow")
    wide_count = lax.axis_size("wide")
    my_narrow = lax.axis_index("narrow")
    my_wide = lax.axis_index("wide")
    my_core = my_wide % 2
    part_width = gate_weight.shape[3]
    experts = router.shape[1] * wide_count
    places = experts // groups
    split_parts = wide_count // places
    capacity = (10 * length // experts + 3) // 4
    half_cap = capacity // 2
    row_count, col_count = qkv_weights.shape[1:]
    half_wide = wide_count // 2
    core_hop = ("wide", 0)
    part_hop = ("wide", 1)
    orders = hop_orders(groups, wide_count)
    slots = [block_slots(order, groups, wide_count) for order in orders]
    direct = col_count == LANES
    pairs = features // (2 * LANES)
    if direct:
        core_entry, tables = my_core, slots
    else:
        core_entry = jnp.int32(0)
        tables = [jnp.arange(groups * pairs, dtype=jnp.int32)] * 3
    table = jnp.concatenate(
        [jnp.reshape(core_entry, (1,)).astype(jnp.int32)] + [t.reshape(-1) for t in tables]
    )
    place = jnp.stack([my_narrow, my_wide]).astype(jnp.int32)

    def as_pairs(matrix):
        blocks = from_matrix(matrix, groups, pairs)
        return blocks.reshape((groups * pairs,) + blocks.shape[2:])

    def as_halves(owns, fars):
        if direct:
            return list(zip(owns, fars))
        out = []
        for own, far, slot in zip(owns, fars, slots):
            both = as_pairs(as_matrix(own, far, slot, my_core))
            out.append((both[:, 0], both[:, 1]))
        return out

    def halves_of(keep, send, chain):
        if direct:
            return keep, send
        rows = keep.shape[1]
        both = jnp.stack([keep, send.astype(F32)], axis=1).reshape(
            groups, pairs, 2, rows, LANES
        )
        matrix = jnp.transpose(both, (0, 3, 1, 2, 4)).reshape(groups * rows, features)
        parts = from_matrix(matrix, groups, half_wide)
        placed = jnp.zeros((groups * half_wide,) + parts.shape[2:], F32)
        placed = placed.at[slots[chain].reshape(-1)].set(parts.reshape(placed.shape))
        mine = jnp.where(my_core == 0, placed[:, 0], placed[:, 1])
        theirs = jnp.where(my_core == 0, placed[:, 1], placed[:, 0])
        return mine, theirs.astype(BF)

    def split_rows(values, ends):
        return [
            lax.slice_in_dim(values, a, b, axis=1) for a, b in zip([0] + ends[:-1], ends)
        ]

    narrow_hops = [("narrow", b) for b in range(groups.bit_length() - 1)]
    place_hops = [
        ("wide", b) for b in range(split_parts.bit_length() - 1, wide_count.bit_length() - 1)
    ][::-1]
    chains = (
        narrow_hops[:1] + place_hops + narrow_hops[1:],
        place_hops + narrow_hops[1:] + narrow_hops[:1],
    )
    hop_count = len(chains[0])
    row_table = jnp.concatenate(
        [row_slots(hops, groups, places, split_parts) for hops in chains]
    )
    back_hops = (chains[0][::-1], chains[0])
    back_table = jnp.concatenate(
        [row_slots(hops[::-1], groups, places, split_parts) for hops in back_hops]
    )
    owner_slot = expert_ids % groups * places + expert_ids // groups
    row_ids = jnp.where(expert_slots >= 0, owner_slot * capacity + expert_slots, -1).T

    def flat(rows):
        return rows.reshape(-1, rows.shape[-1])

    def sends(states, step):
        return [row_send(state, hops[step]) for state, hops in zip(states, chains)]

    def joins(states, gots):
        return [row_join(state, got) for state, got in zip(states, gots)]

    def to_core(values):
        return [from_partner(value, core_hop) for value in values]

    def to_part(values):
        return [from_partner(value, part_hop) for value in values]

    def add(a, b):
        return a.astype(F32) + b.astype(F32)

    def homeward(rows):
        return rows.astype(BF).reshape(-1, 1, half_cap, rows.shape[-1])

    def homeward_start(states):
        return [(state, list(hops)) for state, hops in zip(states, chains)]

    def backs_out(states, step):
        gots = {}
        for chain in range(2):
            at = step - chain
            if 0 <= at < hop_count:
                gots[chain] = back_send(*states[chain], back_hops[chain][at])
        return gots

    def backs_join(states, gots, step):
        return [
            back_join(*state, back_hops[chain][step - chain], gots[chain])
            if chain in gots
            else state
            for chain, state in enumerate(states)
        ]

    def slots_first(states):
        return [state.reshape((-1,) + state.shape[2:]) for state, _ in states]

    router_tail = router.astype(BF).reshape(-1, col_count)
    tail_rows = router_tail.shape[0]
    out_low = jnp.concatenate(
        [
            out_weight.astype(BF),
            router_tail,
            jnp.zeros((-tail_rows % 16, col_count), BF),
        ],
        axis=0,
    )
    qkv_low = qkv_weights.astype(BF)
    upstream_a, upstream_b = upstream_call(
        row_table, upstream, row_ids, expert_ids.T[::-1].astype(F32), experts, capacity
    )
    shared = shared_hops(orders)
    stages = range(shared, len(orders[0]) - 1)
    u_state = [upstream_a[None], upstream_b[None]]
    cuts = row_cuts(row_count)
    low_cuts = cuts[:3] + [out_low.shape[0]]
    pieces, ends = [], []
    for i in range(3):
        pieces += [qkv_low[i], out_low[low_cuts[i] : low_cuts[i + 1]]]
        ends.append(sum(piece.shape[0] for piece in pieces))
    blocks = jnp.concatenate(pieces, axis=0)[None]
    for hop in orders[0][:shared]:
        blocks = grow(blocks, from_partner(blocks, hop))
    u_state, blocks = together(u_state, blocks)
    u_got = sends(u_state, 0)
    dense = split_rows(blocks, ends)
    for count, stage in enumerate(stages):
        got = [from_partner(c, order[stage]) for c, order in zip(dense, orders)]
        if count == 1:
            u_got, got = together(u_got, got)
            u_state = joins(u_state, u_got)
            u_got = sends(u_state, 1)
        dense = [grow(c, g) for c, g in zip(dense, got)]
    dense_far = to_core(dense)
    weight_parts = as_halves(dense, dense_far)
    tails = [half[:, -(out_low.shape[0] - row_count) :][:, :tail_rows] for half in (dense[2], dense_far[2])]
    full_router = jnp.transpose(
        as_matrix(*tails, slots[2], my_core)
        .reshape(groups, tail_rows, wide_count, col_count)
        .transpose(0, 2, 1, 3)
        .reshape(groups, wide_count, row_count, router.shape[1]),
        (0, 2, 1, 3),
    ).reshape(features, experts)
    router_wide = jnp.pad(full_router, ((0, 0), (0, -experts % LANES)))
    gate_low = gate_weight[0, 0].T.astype(BF)
    up_low = up_weight[0, 0].T.astype(BF)
    down_low = down_weight[0, 0].astype(BF)
    table_hot = (
        jnp.pad(buckets, (0, 1), constant_values=-1)[:, None]
        == jnp.arange(bucket_count, dtype=jnp.int32)[None, :]
    ).astype(F32)
    bias_table = jnp.dot(table_hot, rel_bias, precision=lax.Precision.HIGHEST).T
    normed_in, heads, probs, attended = attend_call(
        table, tokens, attn_gain, bias_table, weight_parts, groups, head_dim
    )
    u_got, attended = together(u_got, attended)
    for step in range(2, hop_count):
        u_state = joins(u_state, u_got)
        u_got = sends(u_state, step)
    hidden_x1, moe_input, send_a, send_b = post_call(
        table, row_table, tokens, attended, weight_parts, moe_gain, row_ids, groups, experts,
        capacity,
    )
    u_got, send_a, send_b = together(u_got, send_a, send_b)
    u_own = [flat(state) for state in joins(u_state, u_got)]
    u_core, u_part = to_core(u_own), to_part(u_own[:1])
    x_state = [send_a[None], send_b[None]]
    for step in range(hop_count):
        x_got = sends(x_state, step)
        if step == 0:
            x_got, u_core, u_part[0], router_wide = together(
                x_got, u_core, u_part[0], router_wide
            )
        else:
            x_got = together(*x_got)
        x_state = joins(x_state, x_got)
    late_parts, _ = together(weight_parts, send_a)
    projection_parts = [tuple(half[:, row_count:] for half in part) for part in late_parts]
    projection_parts, x_state = together(projection_parts, x_state)
    x_own = [flat(state) for state in x_state]
    x_core, x_part = to_core(x_own), to_part(x_own)
    late_u, _ = together(u_own[1], x_own)
    u_part.append(from_partner(late_u, part_hop))

    my_expert = (my_narrow + groups * (my_wide // split_parts)).reshape(1).astype(jnp.int32)
    row_total = 8 * x_own[0].shape[0]

    def run_expert(xs, us, first, kept):
        return expert_call(
            my_expert, xs, us, router_wide, gate_low, up_low, down_low, first, row_total, kept
        )

    y_near, dx_near, kept = run_expert(x_own + x_core, u_own + u_core, 0, None)
    x_part[0], u_part[0], dx_near = together(x_part[0], u_part[0], dx_near)
    dx_near_got = to_core(dx_near[2:])
    y_far, parts_back = [], []
    for chain in range(2):
        if chain:
            x_part[1], u_part[1], y_far = together(x_part[1], u_part[1], y_far)
        xs = [x_part[chain], from_partner(x_part[chain], core_hop)]
        us = [u_part[chain], from_partner(u_part[chain], core_hop)]
        y_two, dx_two, kept = run_expert(xs, us, 4 + 2 * chain, kept)
        if chain:
            y_two, dx_two, kept, parts_back[0] = together(y_two, dx_two, kept, parts_back[0])
        y_far.append(y_two)
        far_got = from_partner(dx_two[1], core_hop)
        far_sum = add(dx_two[0], far_got).astype(BF)
        if not chain:
            kept, far_sum = together(kept, far_sum)
        parts_back.append(from_partner(far_sum, part_hop))
    kept, far_sum = together(kept, far_sum)
    y_near_got = to_core(y_near[2:])
    y_far_got = to_core([two[1] for two in y_far])

    def home_sum(chain, part):
        near = add(dx_near[chain], dx_near_got[chain])
        return homeward(near + part.astype(F32))

    x_all, dy_all, hidden_all, dgate_all, dup_all = kept
    states = homeward_start([home_sum(0, parts_back[0]), None])
    for step in range(hop_count + 1):
        gots = backs_out(states, step)
        if step == 0:
            gate_local = expert_grad_call(dgate_all, x_all)
            up_local = expert_grad_call(dup_all, x_all)
            gots, part_b, gate_local, up_local, hidden_all = together(
                gots, parts_back[1], gate_local, up_local, hidden_all
            )
            states[1] = (home_sum(1, part_b), list(chains[1]))
        elif step == 1:
            down_local = expert_grad_call(hidden_all, dy_all)
            y_sums = [add(mine, got).astype(BF) for mine, got in zip(y_near[:2], y_near_got)]
            y_far_sums = [
                add(two[0], got).astype(BF) for two, got in zip(y_far, y_far_got)
            ]
            gots, down_local, y_sums, y_far_sums = together(
                gots, down_local, y_sums, y_far_sums
            )
            y_part_got = to_part(y_far_sums[:1])
        elif step == 2:
            squares = [g * g for g in (gate_local, up_local, down_local)]
            local_sums = jnp.stack([jnp.sum(q, axis=0) for q in squares], axis=0)
            part_stats = jnp.stack([jnp.mean(q, axis=1) for q in squares], axis=0) + STAT_EPS
            sums_got = from_partner(local_sums, core_hop)
            gots, local_sums, y_part_got, sums_got = together(
                gots, local_sums, y_part_got, sums_got
            )
        elif step == 3:
            sums_got, y_far_sums = together(sums_got, y_far_sums)
            local_sums = local_sums + sums_got
            sums_got = from_partner(local_sums, part_hop)
            sums_got, y_far_sums = together(sums_got, y_far_sums)
            y_part_got = y_part_got + to_part(y_far_sums[1:])
            wide_stats = (local_sums + sums_got) / (part_width * split_parts) + STAT_EPS
            gate_new = factored(
                gate_weight[0, 0].T, gate_local, part_stats[0], wide_stats[0],
                jnp.mean(wide_stats[0]),
            )
            up_new = factored(
                up_weight[0, 0].T, up_local, part_stats[1], wide_stats[1],
                jnp.mean(wide_stats[1]),
            )
            down_new = factored(
                down_weight[0, 0], down_local, part_stats[2], wide_stats[2],
                jnp.mean(wide_stats[2]),
            )
            gots, gate_new, up_new, down_new, wide_stats = together(
                gots, gate_new, up_new, down_new, wide_stats
            )
        else:
            gots = together(gots)[0]
        states = backs_join(states, gots, step)
    inputs_back = slots_first(states)
    y_home = homeward(add(y_sums[0], y_part_got[0]))
    inputs_back, y_home = together(inputs_back, y_home)
    y_states = homeward_start([y_home, None])
    y_gots = backs_out(y_states, 0)

    x1_grad, gates, moe_gain_local, router_local, out_keep, out_send, attended_grad = mid_call(
        table, back_table, hidden_x1, moe_gain, moe_input, upstream, inputs_back, row_ids,
        expert_ids, router_wide, attended, projection_parts, groups, experts, capacity,
    )
    y_part_got, y_gots, attended_grad, out_send = together(
        y_part_got, y_gots, attended_grad, out_send
    )
    y_states = backs_join(y_states, y_gots, 0)
    y_states[1] = (homeward(add(y_sums[1], y_part_got[1])), list(chains[1]))
    y_gots = backs_out(y_states, 1)

    *grads, dheads, diag = attend_back_call(
        table, normed_in, heads, probs, attended_grad, out_keep, out_send, groups, head_dim
    )
    halves = [halves_of(grads[i], grads[3 + i], i) for i in range(3)]
    addends = [[keep, from_partner(send, core_hop)] for keep, send in halves]
    ends, size = [], 0
    for value, _ in addends:
        size += value.shape[1]
        ends.append(size)
    y_gots, addends = together(y_gots, addends)
    y_step = 1
    router_local, moe_gain_local, dheads, x1_grad, diag, _ = together(
        router_local, moe_gain_local, dheads, x1_grad, diag, addends
    )

    def halve(values, hop):
        half = values[0].shape[0] // 2
        send = sum(value[half:].astype(F32) for value in values).astype(BF)
        return [value[:half] for value in values], from_partner(send, hop)

    def more_outputs():
        joined = backs_join(y_states, y_gots, y_step)
        return joined, backs_out(joined, y_step + 1), y_step + 1

    small_hops = list(orders[0])
    y_states, y_gots, y_step = more_outputs()
    for count, stage in enumerate(stages[::-1]):
        halved = [halve(values, order[stage]) for values, order in zip(addends, orders)]
        gots = [got for _, got in halved]
        if count == 0:
            tokens_grad, attn_gain_local = tokens_back_call(
                table, tokens, attn_gain, x1_grad, dheads, weight_parts, groups
            )
            tail = jnp.pad(diag, ((0, 0), (0, 0), (0, 8)))
            line = sum(tail[:, i, i : i + 2 * length] for i in range(8))
            bias_local = jnp.dot(line, table_hot, precision=lax.Precision.HIGHEST)
            small = jnp.concatenate(
                [
                    attn_gain_local.reshape(-1),
                    moe_gain_local.reshape(-1),
                    bias_local.reshape(-1),
                    router_local[:experts].reshape(-1),
                ]
            ).reshape(-1, LANES)
            gots, small, y_gots = together(gots, small, y_gots)
            y_states, y_gots, y_step = more_outputs()
        else:
            small_got = from_partner(small, small_hops.pop(0))
            if y_gots:
                gots, small_got, y_gots = together(gots, small_got, y_gots)
                y_states, y_gots, y_step = more_outputs()
            else:
                gots, small_got = together(gots, small_got)
            small = small + small_got
        addends = [kept + [got] for (kept, _), got in zip(halved, gots)]
    summed = [sum(value.astype(F32) for value in values) for values in addends]
    while y_gots:
        y_states, y_gots, y_step = more_outputs()
    block_out = block_out_call(
        back_table, hidden_x1, gates, slots_first(y_states), row_ids, experts, capacity
    )

    def small_beside(value, others):
        if not small_hops:
            return value, together(*others)
        got = from_partner(value, small_hops.pop(0))
        out = together(got, *others)
        return value + out[0], out[1:]

    total = jnp.concatenate(summed, axis=1)
    for hop in orders[0][:shared][::-1]:
        got = halve_send(total, hop)
        small, (got, block_out) = small_beside(small, (got, block_out))
        total = halve_add(total, got)
    blocks = total.astype(BF)
    for hop in orders[0][:shared]:
        got = from_partner(blocks, hop)
        small, (got, total) = small_beside(small, (got, total))
        blocks = grow(blocks, got)
    pieces = split_rows(total, ends)
    dense_mine = jnp.concatenate(
        [piece[:, :row_count] for piece in pieces]
        + [jnp.concatenate([piece[:, row_count:] for piece in pieces], axis=1)],
        axis=0,
    )
    dense_weights = jnp.concatenate([qkv_weights, out_weight[None]], axis=0)
    dense = split_rows(blocks, ends)
    router_size = features * experts
    for count, stage in enumerate(stages):
        gots = [from_partner(chain, order[stage]) for chain, order in zip(dense, orders)]
        if count == 0:
            small, (gots,) = small_beside(small, (gots,))
            small, small_hops = cube_sum(small, small_hops), []
        elif count == 1:
            small, (gots, dense_mine, dense_weights) = small_beside(
                small, (gots, dense_mine, dense_weights)
            )
        else:
            gots, router_out = together(gots, router_out)
        if count == 0:
            router_total = small.reshape(-1)[-router_size:].reshape(experts, features)
            router_sq = router_total * router_total
            router_rows = jnp.mean(router_sq, axis=0) + STAT_EPS
            router_cols = jnp.mean(router_sq, axis=1) + STAT_EPS
            rows_first, cols_first = my_narrow * router.shape[0], my_wide * router.shape[1]
            router_new = factored(
                router.T,
                lax.dynamic_slice(router_total, (cols_first, rows_first), router.T.shape),
                lax.dynamic_slice_in_dim(router_cols, cols_first, router.shape[1], 0),
                lax.dynamic_slice_in_dim(router_rows, rows_first, router.shape[0], 0),
                jnp.mean(router_rows),
            )
            small_flat = small.reshape(-1)
            router_out = (
                small_flat[:features],
                small_flat[features : 2 * features],
                small_flat[2 * features : -router_size].reshape(head_count, bucket_count),
                router_total, router_new, router_rows, router_cols,
            )
        dense = [grow(chain, got) for chain, got in zip(dense, gots)]
    gain_a_total, gain_m_total, bias_total, router_total, router_new, router_rows, router_cols = (
        router_out
    )
    dense_parts = as_halves(dense, to_core(dense))
    qkv_total, out_total, rows, cols, dense_new = finish_call(
        table, place, dense_parts, groups, features, dense_mine if direct else None,
        dense_weights,
    )
    if not direct:
        rows_mine = lax.dynamic_slice_in_dim(rows, my_narrow * row_count, row_count, 1)
        cols_mine = lax.dynamic_slice_in_dim(cols, my_wide * col_count, col_count, 1)
        step = adafactor_step(dense_mine, rows_mine, cols_mine, jnp.mean(rows, axis=1))
        dense_new = jnp.concatenate([qkv_weights - step[:3], step[3:]], axis=0)
    qkv_stats = jnp.stack([rows[:3], cols[:3]], axis=0)
    out_stats = jnp.concatenate([rows[3:], cols[3:]], axis=0)
    return (
        block_out,
        tokens_grad,
        gain_a_total,
        qkv_total,
        out_total,
        bias_total.T,
        gain_m_total,
        router_total.T,
        gate_local.T[None, None],
        up_local.T[None, None],
        down_local[None, None],
        dense_new[:3],
        dense_new[3],
        router_new.T,
        gate_new.T[None, None],
        up_new.T[None, None],
        down_new[None, None],
        qkv_stats,
        out_stats,
        router_rows,
        router_cols,
        wide_stats[None, None],
        part_stats[None, None],
    )


def solution(mesh):
    in_specs = (
        P(("narrow", "wide"), None),
        P(),
        P(None, "narrow", "wide"),
        P("narrow", "wide"),
        P(),
        P(),
        P("narrow", "wide"),
        P("narrow", "wide", None, None),
        P("narrow", "wide", None, None),
        P("narrow", "wide", None, None),
        P(("narrow", "wide"), None),
        P(("narrow", "wide"), None),
        P(),
        P(("narrow", "wide"), None),
    )
    out_specs = (
        P(("narrow", "wide"), None),
        P(("narrow", "wide"), None),
        P(),
        P(),
        P(),
        P(),
        P(),
        P(),
        P("narrow", "wide", None, None),
        P("narrow", "wide", None, None),
        P("narrow", "wide", None, None),
        P(None, "narrow", "wide"),
        P("narrow", "wide"),
        P("narrow", "wide"),
        P("narrow", "wide", None, None),
        P("narrow", "wide", None, None),
        P("narrow", "wide", None, None),
        P(),
        P(),
        P(),
        P(),
        P("narrow", "wide", None, None),
        P("narrow", "wide", None, None),
    )
    return jax.shard_map(
        on_device, mesh=mesh, in_specs=in_specs, out_specs=out_specs, check_vma=False
    )
```

```python
import functools

import jax
import jax.numpy as jnp
from jax import lax
from jax.experimental import pallas as pl
from jax.experimental.pallas import tpu as pltpu
from jax.sharding import PartitionSpec as P

NORM_EPS = 1e-06
STAT_EPS = 1e-06
STEP_RATE = 0.01
LANES = 128
GELU_C = 0.7978845608028654
GELU_A = 0.044715
BF = jnp.bfloat16
F32 = jnp.float32
NN = (((1,), (0,)), ((), ()))
NT = (((1,), (1,)), ((), ()))
TN = (((0,), (0,)), ((), ()))


def mm(a, b, dims=NN):
    return lax.dot_general(a, b, dims, preferred_element_type=F32)


def from_partner(value, hop):
    axis, bit = hop
    mask = 2**bit
    pairs = [(source, source ^ mask) for source in range(lax.axis_size(axis))]
    return lax.ppermute(value, axis, pairs)


def after(values, *others):
    return lax.optimization_barrier((values, others))[0]


def hop_orders(groups, wide_count):
    narrow = [("narrow", b) for b in range(groups.bit_length() - 1)]
    wide = [("wide", b) for b in range(1, wide_count.bit_length() - 1)]
    far, near = wide[1:][::-1], wide[:1]
    core = [("wide", 0)]
    return (
        far + narrow + near + core,
        far + near + narrow + core,
        far + narrow[1:] + near + narrow[:1] + core,
    )


def row_cuts(count):
    share = -(-count // 48) * 16
    return [min(i * share, count) for i in range(4)]


def block_slots(order, groups, wide_count):
    n_ids = jnp.arange(groups, dtype=jnp.int32)[:, None]
    w_ids = 2 * jnp.arange(wide_count // 2, dtype=jnp.int32)[None, :]
    slots = jnp.zeros((groups, wide_count // 2), jnp.int32)
    for stage, (axis, bit) in enumerate(order[:-1]):
        ids = n_ids if axis == "narrow" else w_ids
        differs = ((ids ^ lax.axis_index(axis)) >> bit) & 1
        slots = slots | (differs << stage)
    return slots


def together(*values):
    return lax.optimization_barrier(values)


def shared_hops(orders):
    count = 0
    while len({order[count] for order in orders}) == 1 and count < len(orders[0]) - 1:
        count += 1
    return count


def grow(blocks, got, axis=0):
    return jnp.concatenate([blocks, got], axis=axis)


def core_sum(keep, got):
    return keep + got.astype(F32)


def halve_send(total, hop, axis=0):
    half = total.shape[axis] // 2
    return from_partner(lax.slice_in_dim(total, half, 2 * half, axis=axis).astype(BF), hop)


def halve_add(total, got, axis=0):
    half = total.shape[axis] // 2
    return lax.slice_in_dim(total, 0, half, axis=axis) + got.astype(F32)


def row_send(state, hop):
    sources, places = state.shape[:2]
    return from_partner(state.reshape((sources, 2, places // 2) + state.shape[2:])[:, 1], hop)


def row_join(state, got):
    sources, places = state.shape[:2]
    kept = state.reshape((sources, 2, places // 2) + state.shape[2:])[:, 0]
    return jnp.concatenate([kept, got], axis=0)


def back_split(state, left, hop):
    low = 2 ** left.index(hop)
    split = state.reshape((-1, 2, low) + state.shape[1:])
    return [split[:, i].reshape((-1,) + state.shape[1:]) for i in range(2)]


def back_send(state, left, hop):
    return from_partner(back_split(state, left, hop)[1], hop)


def back_join(state, left, hop, got):
    kept = back_split(state, left, hop)[0]
    joined = jnp.stack([kept, got], axis=1).reshape((got.shape[0], -1) + state.shape[2:])
    return joined, [other for other in left if other != hop]


def row_slots(hops, groups, places, parts):
    n_ids = jnp.arange(groups, dtype=jnp.int32)[:, None]
    w_ids = parts * jnp.arange(places, dtype=jnp.int32)[None, :]
    slots = jnp.zeros((groups, places), jnp.int32)
    for axis, bit in hops:
        ids = n_ids if axis == "narrow" else w_ids
        slots = 2 * slots + (((ids ^ lax.axis_index(axis)) >> bit) & 1)
    return slots.reshape(-1)


def cube_sum(value, hops):
    for hop in hops:
        value = value + from_partner(value, hop)
    return value


def as_matrix(own, other, slots, my_core):
    groups, half_wide = slots.shape
    both = jnp.stack([jnp.where(my_core == 0, own, other), jnp.where(my_core == 0, other, own)], 1)
    picked = jnp.take(both, slots.reshape(-1), axis=0)
    rows, cols = own.shape[1:]
    picked = picked.reshape(groups, half_wide, 2, rows, cols)
    return jnp.transpose(picked, (0, 3, 1, 2, 4)).reshape(groups * rows, half_wide * 2 * cols)


def from_matrix(matrix, groups, half_wide):
    lead = matrix.shape[:-2]
    rows, cols = matrix.shape[-2] // groups, matrix.shape[-1] // (2 * half_wide)
    shaped = matrix.reshape(lead + (groups, rows, half_wide, 2, cols))
    k = len(lead)
    order = tuple(range(k)) + (k, k + 2, k + 3, k + 1, k + 4)
    return jnp.transpose(shaped, order)


def gelu_tanh(values):
    return jax.nn.gelu(values, approximate=True)


def adafactor_step(gradient, row_stats, col_stats, mean_rows):
    return (
        STEP_RATE
        * gradient
        / jnp.sqrt(row_stats[..., :, None] * col_stats[..., None, :] / mean_rows[..., None, None])
    )


def factored(weight, gradient, row_stats, col_stats, mean_rows):
    return weight - adafactor_step(gradient, row_stats, col_stats, mean_rows)


def vmem():
    return pl.BlockSpec(memory_space=pltpu.VMEM)


def smem():
    return pl.BlockSpec(memory_space=pltpu.SMEM)


def params(mebibytes):
    return pltpu.CompilerParams(vmem_limit_bytes=mebibytes * 1024 * 1024)


def cost(micros):
    return pl.CostEstimate(
        flops=int(micros * 1153e6), transcendentals=0, bytes_accessed=int(micros * 3690e3)
    )


def lane_masks(head_dim):
    heads = LANES // head_dim
    ids = lax.broadcasted_iota(jnp.int32, (1, LANES), 1) // head_dim
    return [ids == i for i in range(heads)]


def attend_body(
    table_ref, tokens_ref, gain_ref, bias_ref,
    own_q, own_k, own_v, far_q, far_k, far_v,
    normed_ref, heads_ref, probs_ref, attended_ref,
    *, groups, pairs, head_dim,
):
    length, features = tokens_ref.shape
    rows = features // groups
    x = tokens_ref[...].astype(F32)
    factor = lax.rsqrt(jnp.mean(x * x, axis=-1, keepdims=True) + NORM_EPS)
    normed_ref[...] = (x * factor * gain_ref[...]).astype(BF)
    core = table_ref[0]

    def project(w2, carry):
        for m, (own, far) in enumerate(((own_q, far_q), (own_k, far_k), (own_v, far_v))):
            total = None
            for n in range(groups):
                at = table_ref[1 + (m * groups + n) * pairs + w2]
                block = jnp.concatenate([own[at, :rows], far[at, :rows]], axis=1)
                part = mm(normed_ref[:, n * rows : (n + 1) * rows], block)
                total = part if total is None else total + part
            total = total.astype(BF)
            heads_ref[m, 2 * w2 + core] = total[:, :LANES]
            heads_ref[m, 2 * w2 + 1 - core] = total[:, LANES:]
        return carry

    lax.fori_loop(0, pairs, project, 0)
    masks = lane_masks(head_dim)
    scale = head_dim**-0.5

    def attend(w, carry):
        q, k, v = heads_ref[0, w], heads_ref[1, w], heads_ref[2, w]
        mixed = jnp.zeros((length, LANES), F32)
        for i, mask in enumerate(masks):
            head = w * len(masks) + i
            raw = mm(jnp.where(mask, q, jnp.zeros_like(q)), k, NT)
            line = jnp.broadcast_to(bias_ref[pl.ds(head, 1), :], (length, 2 * length))
            bias = pltpu.roll(line, length + 1, 1, stride=1, stride_axis=0)[:, :length]
            scores = raw * scale + bias
            top = jnp.max(scores, axis=-1, keepdims=True)
            grown = jnp.exp(scores - top)
            probs = grown / jnp.sum(grown, axis=-1, keepdims=True)
            probs_ref[head] = probs
            mixed = jnp.where(mask, mm(probs.astype(BF), v), mixed)
        attended_ref[w] = mixed.astype(BF)
        return carry

    lax.fori_loop(0, 2 * pairs, attend, 0)


def attend_call(table, tokens, gain, bias_table, gathered, groups, head_dim):
    length, features = tokens.shape
    pairs = features // (2 * LANES)
    head_count = features // head_dim
    owns = [g[0] for g in gathered]
    fars = [g[1] for g in gathered]
    body = functools.partial(attend_body, groups=groups, pairs=pairs, head_dim=head_dim)
    return pl.pallas_call(
        body,
        in_specs=[smem()] + [vmem()] * 9,
        out_specs=[vmem()] * 4,
        out_shape=[
            jax.ShapeDtypeStruct((length, features), BF),
            jax.ShapeDtypeStruct((3, 2 * pairs, length, LANES), BF),
            jax.ShapeDtypeStruct((head_count, length, length), F32),
            jax.ShapeDtypeStruct((2 * pairs, length, LANES), BF),
        ],
        compiler_params=params(14),
        name="attend",
        cost_estimate=cost(16),
    )(table, tokens, gain.reshape(1, features), bias_table, *owns, *fars)


def expert_hot(ids_ref, expert, cap, length):
    slot = lax.broadcasted_iota(jnp.int32, (cap, length), 0) + expert * cap
    return [slot == ids_ref[c : c + 1, :] for c in range(2)]


def spread_rows(values, ids_ref, slots_ref, sends, experts, cap):
    length, features = values.shape
    half = cap // 2
    for e in range(experts):
        first, second = expert_hot(ids_ref, e, cap, length)
        rows = mm(jnp.where(first | second, 1.0, 0.0).astype(BF), values)
        for chain, send in enumerate(sends):
            at = slots_ref[chain * experts + e]
            send[at, :, :features] = rows[chain * half : (chain + 1) * half].astype(BF)


def upstream_body(slots_ref, values_ref, ids_ref, others_ref, send_a, send_b, *, experts, cap):
    length, features = values_ref.shape
    half = cap // 2
    spread_rows(values_ref[...], ids_ref, slots_ref, (send_a, send_b), experts, cap)
    for e in range(experts):
        first, second = expert_hot(ids_ref, e, cap, length)
        other = jnp.where(first, others_ref[0:1, :], 0.0) + jnp.where(
            second, others_ref[1:2, :], 0.0
        )
        other = jnp.sum(other, axis=1, keepdims=True)
        other = jnp.broadcast_to(other, (cap, LANES))
        for chain, send in enumerate((send_a, send_b)):
            at = slots_ref[chain * experts + e]
            send[at, :, features:] = other[chain * half : (chain + 1) * half].astype(BF)


def upstream_call(row_table, upstream, row_ids, other_ids, experts, cap):
    features = upstream.shape[1]
    return pl.pallas_call(
        functools.partial(upstream_body, experts=experts, cap=cap),
        in_specs=[smem()] + [vmem()] * 3,
        out_specs=[vmem()] * 2,
        out_shape=[jax.ShapeDtypeStruct((experts, cap // 2, features + LANES), BF)] * 2,
        compiler_params=params(8),
        name="upstream_rows",
        cost_estimate=cost(3),
    )(row_table, upstream, row_ids, other_ids)


def projection_block(halves, table_ref, n, w2, groups, pairs, depth, cuts):
    sides = []
    for refs in halves:
        parts = []
        for i in range(3):
            at = table_ref[1 + (i * groups + n) * pairs + w2]
            first = depth if refs[i].shape[1] > depth else 0
            parts.append(refs[i][at, first : first + cuts[i + 1] - cuts[i]])
        sides.append(jnp.concatenate(parts, axis=0))
    return jnp.concatenate(sides, axis=1)


def post_body(
    table_ref, slots_ref, tokens_ref, attended_ref,
    own_q, own_k, own_v, far_q, far_k, far_v, gain_ref, ids_ref,
    x1_ref, normed_ref, send_a, send_b,
    *, groups, experts, cap, cuts,
):
    length, features = tokens_ref.shape
    pairs = features // (2 * LANES)
    per_group = 2 * pairs // groups
    depth = features // groups
    halves = ((own_q, own_k, own_v), (far_q, far_k, far_v))
    core = table_ref[0]
    rows = [
        jnp.concatenate([attended_ref[n * per_group + i] for i in range(per_group)], axis=1)
        for n in range(groups)
    ]
    for w2 in range(pairs):
        total = None
        for n in range(groups):
            block = projection_block(halves, table_ref, n, w2, groups, pairs, depth, cuts)
            part = mm(rows[n], block)
            total = part if total is None else total + part
        for j in range(2):
            w = 2 * w2 + (core if j == 0 else 1 - core)
            place = pl.multiple_of(w * LANES, LANES)
            mine = total[:, j * LANES : (j + 1) * LANES]
            x1_ref[:, pl.ds(place, LANES)] = mine + tokens_ref[:, pl.ds(place, LANES)].astype(F32)
    x1 = x1_ref[...]
    factor = lax.rsqrt(jnp.mean(x1 * x1, axis=-1, keepdims=True) + NORM_EPS)
    normed = (x1 * factor * gain_ref[...]).astype(BF)
    normed_ref[...] = normed
    spread_rows(normed, ids_ref, slots_ref, (send_a, send_b), experts, cap)


def post_call(table, row_table, tokens, attended, gathered, gain, row_ids, groups, experts, cap):
    length, features = tokens.shape
    owns = [g[0] for g in gathered]
    fars = [g[1] for g in gathered]
    cuts = row_cuts(features // groups)
    return pl.pallas_call(
        functools.partial(post_body, groups=groups, experts=experts, cap=cap, cuts=cuts),
        in_specs=[smem()] * 2 + [vmem()] * 10,
        out_specs=[vmem()] * 4,
        out_shape=[
            jax.ShapeDtypeStruct((length, features), F32),
            jax.ShapeDtypeStruct((length, features), BF),
            jax.ShapeDtypeStruct((experts, cap // 2, features), BF),
            jax.ShapeDtypeStruct((experts, cap // 2, features), BF),
        ],
        compiler_params=params(12),
        name="post",
        cost_estimate=cost(3),
    )(
        table, row_table, tokens, attended, *owns, *fars, gain.reshape(1, features), row_ids
    )


def mid_body(
    table_ref, slots_ref, x1_ref, gain_ref, normed_ref, upstream_ref, back_a, back_b,
    ids_ref, choice_ref, router_ref, attended_ref,
    own_q, own_k, own_v, far_q, far_k, far_v,
    x1_grad_ref, gates_ref, gain_out_ref, router_out_ref, keep_ref, send_ref, att_grad_ref,
    *, groups, experts, cap, cuts,
):
    length, features = x1_ref.shape
    pairs = features // (2 * LANES)
    per_group = 2 * pairs // groups
    rows = features // groups
    half = cap // 2
    halves = ((own_q, own_k, own_v), (far_q, far_k, far_v))
    core = table_ref[0]
    dmoe = jnp.zeros((length, features), F32)
    dots = [jnp.zeros((length, LANES), F32)] * 2
    for e in range(experts):
        hots = expert_hot(ids_ref, e, cap, length)
        hots = [jnp.where(hot, 1.0, 0.0).astype(BF) for hot in hots]
        both = hots[0] + hots[1]
        for chain, back in enumerate((back_a, back_b)):
            at = slots_ref[chain * experts + e]
            part = slice(chain * half, (chain + 1) * half)
            got = back[at]
            dmoe = dmoe + mm(both[part], got[:, :features], TN)
            for c in range(2):
                dots[c] = dots[c] + mm(hots[c][part], got[:, features:], TN)
    normed = normed_ref[...]
    logits = mm(normed, router_ref[...])
    lane = lax.broadcasted_iota(jnp.int32, logits.shape, 1)
    picks = [lane == choice_ref[:, c : c + 1] for c in range(2)]
    picked = [jnp.sum(jnp.where(pick, logits, 0.0), axis=1, keepdims=True) for pick in picks]
    top = jnp.maximum(picked[0], picked[1])
    grown = [jnp.exp(value - top) for value in picked]
    gates = [value / (grown[0] + grown[1]) for value in grown]
    gates_ref[...] = jnp.where(lane == 0, gates[0], jnp.where(lane == 1, gates[1], 0.0))
    dgates = [dot[:, 0:1] for dot in dots]
    inner = gates[0] * dgates[0] + gates[1] * dgates[1]
    dlogits = jnp.where(picks[0], gates[0] * (dgates[0] - inner), 0.0) + jnp.where(
        picks[1], gates[1] * (dgates[1] - inner), 0.0
    )
    dlogits = dlogits.astype(BF)
    router_out_ref[...] = mm(dlogits, normed, TN)
    dmoe = dmoe + mm(dlogits, router_ref[...], NT)
    x1 = x1_ref[...]
    factor = lax.rsqrt(jnp.mean(x1 * x1, axis=-1, keepdims=True) + NORM_EPS)
    hat = x1 * factor
    gain_out_ref[...] = jnp.sum(dmoe * hat, axis=0, keepdims=True)
    scaled = dmoe * gain_ref[...]
    inner = jnp.mean(scaled * hat, axis=-1, keepdims=True)
    x1_grad_ref[...] = upstream_ref[...].astype(F32) + factor * (scaled - hat * inner)
    branches = []
    for w2 in range(pairs):
        both = []
        for j in range(2):
            w = 2 * w2 + (core if j == 0 else 1 - core)
            both.append(x1_grad_ref[:, pl.ds(pl.multiple_of(w * LANES, LANES), LANES)].astype(BF))
        branches.append(jnp.concatenate(both, axis=1))
    for n in range(groups):
        att = jnp.concatenate(
            [attended_ref[n * per_group + i] for i in range(per_group)], axis=1
        )
        total = None
        for w2 in range(pairs):
            block = mm(att, branches[w2], TN)
            for i in range(3):
                at = table_ref[1 + (i * groups + n) * pairs + w2]
                keep_ref[at, cuts[i] : cuts[i + 1]] = block[cuts[i] : cuts[i + 1], :LANES]
                send = block[cuts[i] : cuts[i + 1], LANES:].astype(BF)
                send_ref[at, cuts[i] : cuts[i + 1]] = send
            block = projection_block(halves, table_ref, n, w2, groups, pairs, rows, cuts)
            part = mm(branches[w2], block, NT)
            total = part if total is None else total + part
        for i in range(per_group):
            att_grad_ref[n * per_group + i] = total[:, i * LANES : (i + 1) * LANES].astype(BF)


def mid_call(
    table, row_table, x1, gain, normed, upstream, backs, row_ids, choices, router, attended,
    gathered, groups, experts, cap,
):
    length, features = x1.shape
    pairs = features // (2 * LANES)
    rows = features // groups
    owns = [g[0] for g in gathered]
    fars = [g[1] for g in gathered]
    return pl.pallas_call(
        functools.partial(
            mid_body, groups=groups, experts=experts, cap=cap, cuts=row_cuts(rows)
        ),
        in_specs=[smem()] * 2 + [vmem()] * 16,
        out_specs=[vmem()] * 7,
        out_shape=[
            jax.ShapeDtypeStruct((length, features), F32),
            jax.ShapeDtypeStruct((length, LANES), F32),
            jax.ShapeDtypeStruct((1, features), F32),
            jax.ShapeDtypeStruct((LANES, features), F32),
            jax.ShapeDtypeStruct((groups * pairs, rows, LANES), F32),
            jax.ShapeDtypeStruct((groups * pairs, rows, LANES), BF),
            jax.ShapeDtypeStruct((2 * pairs, length, LANES), BF),
        ],
        compiler_params=params(16),
        name="mid",
        cost_estimate=cost(7),
    )(
        table, row_table, x1, gain.reshape(1, features), normed, upstream, *backs,
        row_ids, choices, router, attended, *owns, *fars,
    )


def block_out_body(
    slots_ref, x1_ref, gates_ref, back_a, back_b, ids_ref, out_ref, *, experts, cap
):
    length, features = x1_ref.shape
    half = cap // 2
    sums = [jnp.zeros((length, features), F32)] * 2
    for e in range(experts):
        hots = [
            jnp.where(hot, 1.0, 0.0).astype(BF) for hot in expert_hot(ids_ref, e, cap, length)
        ]
        for chain, back in enumerate((back_a, back_b)):
            got = back[slots_ref[chain * experts + e]]
            part = slice(chain * half, (chain + 1) * half)
            sums = [total + mm(hot[part], got, TN) for total, hot in zip(sums, hots)]
    moe = gates_ref[:, 0:1] * sums[0] + gates_ref[:, 1:2] * sums[1]
    out_ref[...] = (x1_ref[...] + moe).astype(BF)


def block_out_call(row_table, x1, gates, backs, row_ids, experts, cap):
    return pl.pallas_call(
        functools.partial(block_out_body, experts=experts, cap=cap),
        in_specs=[smem()] + [vmem()] * 5,
        out_specs=vmem(),
        out_shape=jax.ShapeDtypeStruct(x1.shape, BF),
        compiler_params=params(8),
        name="block_out",
        cost_estimate=cost(7),
    )(row_table, x1, gates, *backs, row_ids)


def attend_back_body(
    table_ref, normed_ref, heads_ref, probs_ref, grad_ref, out_keep_ref, out_send_ref,
    keep_q, keep_k, keep_v, send_q, send_k, send_v, dheads_ref, diag_ref,
    *, groups, pairs, head_dim, cuts,
):
    length, features = normed_ref.shape
    rows = features // groups
    keeps, sends = (keep_q, keep_k, keep_v), (send_q, send_k, send_v)
    for i in range(3):
        keeps[i][:, rows:] = out_keep_ref[:, cuts[i] : cuts[i + 1]]
        sends[i][:, rows:] = out_send_ref[:, cuts[i] : cuts[i + 1]]
    masks = lane_masks(head_dim)
    scale = head_dim**-0.5

    def back(w, carry):
        q, k, v = heads_ref[0, w], heads_ref[1, w], heads_ref[2, w]
        da = grad_ref[w]
        dq = jnp.zeros((length, LANES), F32)
        dk, dv = dq, dq
        for i, mask in enumerate(masks):
            head = w * len(masks) + i
            probs = probs_ref[head]
            dp = mm(jnp.where(mask, da, jnp.zeros_like(da)), v, NT)
            spread = jnp.sum(probs * dp, axis=-1, keepdims=True)
            ds = (probs * (dp - spread)).astype(BF)
            dq = jnp.where(mask, mm(ds, k), dq)
            dk = jnp.where(mask, mm(ds, q, TN), dk)
            dv = jnp.where(mask, mm(probs.astype(BF), da, TN), dv)
            wide_ds = jnp.concatenate([ds.astype(F32), jnp.zeros((length, length), F32)], axis=1)
            diag = jnp.zeros((8, 2 * length), F32)
            for g in range(length // 8):
                diag = diag + pltpu.roll(wide_ds[8 * g : 8 * g + 8], length - 1 - 8 * g, 1)
            diag_ref[head] = diag
        dheads_ref[0, w] = (dq * scale).astype(BF)
        dheads_ref[1, w] = (dk * scale).astype(BF)
        dheads_ref[2, w] = dv.astype(BF)
        return carry

    lax.fori_loop(0, 2 * pairs, back, 0)
    core = table_ref[0]

    def weigh(w2, carry):
        for m in range(3):
            both = jnp.concatenate(
                [dheads_ref[m, 2 * w2 + core], dheads_ref[m, 2 * w2 + 1 - core]], axis=1
            )
            for n in range(groups):
                at = table_ref[1 + (m * groups + n) * pairs + w2]
                block = mm(normed_ref[:, n * rows : (n + 1) * rows], both, TN)
                keeps[m][at, :rows] = block[:, :LANES]
                sends[m][at, :rows] = block[:, LANES:].astype(BF)
        return carry

    lax.fori_loop(0, pairs, weigh, 0)


def attend_back_call(
    table, normed, heads, probs, attended_grad, out_keep, out_send, groups, head_dim
):
    length, features = normed.shape
    pairs = features // (2 * LANES)
    head_count = features // head_dim
    rows = features // groups
    cuts = row_cuts(rows)
    body = functools.partial(
        attend_back_body, groups=groups, pairs=pairs, head_dim=head_dim, cuts=cuts
    )
    shapes = [(groups * pairs, rows + b - a, LANES) for a, b in zip(cuts[:-1], cuts[1:])]
    return pl.pallas_call(
        body,
        in_specs=[smem()] + [vmem()] * 6,
        out_specs=[vmem()] * 8,
        out_shape=[jax.ShapeDtypeStruct(shape, F32) for shape in shapes]
        + [jax.ShapeDtypeStruct(shape, BF) for shape in shapes]
        + [
            jax.ShapeDtypeStruct((3, 2 * pairs, length, LANES), BF),
            jax.ShapeDtypeStruct((head_count, 8, 2 * length), F32),
        ],
        compiler_params=params(22),
        name="attend_back",
        cost_estimate=cost(12),
    )(table, normed, heads, probs, attended_grad, out_keep, out_send)


def tokens_back_body(
    table_ref, tokens_ref, gain_ref, x1_grad_ref, dheads_ref,
    own_q, own_k, own_v, far_q, far_k, far_v,
    out_ref, gain_out_ref, acc_ref,
    *, groups, pairs,
):
    length, features = tokens_ref.shape
    rows = features // groups
    core = table_ref[0]
    for n in range(groups):

        def step(w2, total):
            for m, (own, far) in enumerate(((own_q, far_q), (own_k, far_k), (own_v, far_v))):
                at = table_ref[1 + (m * groups + n) * pairs + w2]
                both = jnp.concatenate(
                    [dheads_ref[m, 2 * w2 + core], dheads_ref[m, 2 * w2 + 1 - core]], axis=1
                )
                block = jnp.concatenate([own[at, :rows], far[at, :rows]], axis=1)
                total = total + mm(both, block, NT)
            return total

        total = lax.fori_loop(0, pairs, step, jnp.zeros((length, rows), F32))
        acc_ref[:, n * rows : (n + 1) * rows] = total
    x = tokens_ref[...].astype(F32)
    factor = lax.rsqrt(jnp.mean(x * x, axis=-1, keepdims=True) + NORM_EPS)
    hat = x * factor
    grad = acc_ref[...]
    gain_out_ref[...] = jnp.sum(grad * hat, axis=0, keepdims=True)
    scaled = grad * gain_ref[...]
    inner = jnp.mean(scaled * hat, axis=-1, keepdims=True)
    out_ref[...] = (x1_grad_ref[...] + factor * (scaled - hat * inner)).astype(BF)


def tokens_back_call(table, tokens, gain, x1_grad, dheads, gathered, groups):
    length, features = tokens.shape
    pairs = features // (2 * LANES)
    owns = [g[0] for g in gathered]
    fars = [g[1] for g in gathered]
    return pl.pallas_call(
        functools.partial(tokens_back_body, groups=groups, pairs=pairs),
        in_specs=[smem()] + [vmem()] * 10,
        out_specs=[vmem()] * 2,
        out_shape=[
            jax.ShapeDtypeStruct((length, features), BF),
            jax.ShapeDtypeStruct((1, features), F32),
        ],
        scratch_shapes=[pltpu.VMEM((length, features), F32)],
        compiler_params=params(30),
        name="tokens_back",
        cost_estimate=cost(10),
    )(table, tokens, gain.reshape(1, features), x1_grad, dheads, *owns, *fars)


def choose(refs, which):
    value = refs[0][...]
    for i in range(1, len(refs)):
        value = jnp.where(which == i, refs[i][...], value)
    return value


def expert_body(expert_ref, *refs, count, apart):
    x_refs, up_refs, refs = refs[:count], refs[count:apart], refs[apart:]
    router_ref, gate_w, up_w, down_w = refs[:4]
    y_refs, dx_refs = refs[-2 * count - 5 : -count - 5], refs[-count - 5 : -5]
    x_out, dy_ref, hidden_ref, dgate_ref, dup_ref = refs[-5:]
    piece = pl.program_id(0)
    features = x_out.shape[1]
    x = choose(x_refs, piece)
    up = choose(up_refs, piece) if up_refs else x[:, features:]
    x = x[:, :features]
    x_out[...] = x
    logits = mm(x, router_ref[...])
    lane = lax.broadcasted_iota(jnp.int32, logits.shape, 1)
    other_id = up[:, features : features + 1].astype(jnp.int32)
    mine = jnp.sum(jnp.where(lane == expert_ref[0], logits, 0.0), axis=1, keepdims=True)
    other = jnp.sum(jnp.where(lane == other_id, logits, 0.0), axis=1, keepdims=True)
    top = jnp.maximum(mine, other)
    mine_e = jnp.exp(mine - top)
    gate = mine_e / (mine_e + jnp.exp(other - top))
    grad = up[:, :features].astype(F32)
    dy = (gate * grad).astype(BF)
    dy_ref[...] = dy
    step = 2 * LANES
    width = gate_w.shape[0]
    for f in range(0, width, step):
        chunk = slice(f, min(f + step, width))
        g = mm(x, gate_w[chunk, :], NT)
        u = mm(x, up_w[chunk, :], NT)
        dh = mm(dy, down_w[chunk, :], NT)
        square = g * g
        t = jnp.tanh(g * (GELU_C + (GELU_C * GELU_A) * square))
        half_t = 0.5 + 0.5 * t
        act = g * half_t
        slope = half_t + act * ((1.0 - t) * (GELU_C + (3.0 * GELU_C * GELU_A) * square))
        hidden_ref[:, chunk] = (act * u).astype(BF)
        dgate_ref[:, chunk] = (dh * u * slope).astype(BF)
        dup_ref[:, chunk] = (dh * act).astype(BF)
    y = mm(hidden_ref[...], down_w[...]).astype(BF)
    dx = mm(dgate_ref[...], gate_w[...]) + mm(dup_ref[...], up_w[...])
    dot = jnp.sum(grad * y.astype(F32), axis=1, keepdims=True)
    dx = dx.astype(BF)
    dot = jnp.broadcast_to(dot, (x.shape[0], LANES)).astype(BF)
    for i in range(count):

        @pl.when(piece == i)
        def _(i=i):
            y_refs[i][...] = y
            dx_refs[i][:, :features] = dx
            dx_refs[i][:, features:] = dot


def expert_call(expert, xs, upstreams, router, gate_w, up_w, down_w, first, total, kept):
    rows, features = xs[0].shape[0], gate_w.shape[1]
    width = gate_w.shape[0]
    count = len(xs)

    def whole(arr):
        return pl.BlockSpec(arr.shape, lambda i, e: (0, 0), pipeline_mode=pl.Buffered(1))

    def kept_spec(cols):
        return pl.BlockSpec((rows, cols), lambda i, e: (first + i, 0))

    kept_cols = (features, features, width, width, width)
    kept_in = [] if kept is None else list(kept)
    inputs = list(xs) + list(upstreams) + [router, gate_w, up_w, down_w]
    out = pl.pallas_call(
        functools.partial(expert_body, count=count, apart=count + len(upstreams)),
        grid_spec=pltpu.PrefetchScalarGridSpec(
            num_scalar_prefetch=1,
            grid=(count,),
            in_specs=[whole(arr) for arr in inputs]
            + [pl.BlockSpec(memory_space=pl.ANY)] * len(kept_in),
            out_specs=[pl.BlockSpec((rows, features), lambda i, e: (0, 0))] * count
            + [pl.BlockSpec((rows, features + LANES), lambda i, e: (0, 0))] * count
            + [kept_spec(cols) for cols in kept_cols],
        ),
        out_shape=[jax.ShapeDtypeStruct((rows, features), BF)] * count
        + [jax.ShapeDtypeStruct((rows, features + LANES), BF)] * count
        + [jax.ShapeDtypeStruct((total, cols), BF) for cols in kept_cols],
        input_output_aliases={
            1 + len(inputs) + i: 2 * count + i for i in range(len(kept_in))
        },
        compiler_params=params(48),
        name="expert",
        cost_estimate=cost(20 if count == 4 else 1),
    )(expert, *inputs, *kept_in)
    return out[:count], out[count : 2 * count], out[2 * count :]


def expert_grad_body(left_ref, right_ref, out_ref):
    out_ref[...] = mm(left_ref[...], right_ref[...], TN)


def expert_grad_call(left, right):
    rows, features = right.shape
    width = left.shape[1]
    size = 2 * LANES
    return pl.pallas_call(
        expert_grad_body,
        grid=(features // size,),
        in_specs=[
            pl.BlockSpec((rows, width), lambda i: (0, 0)),
            pl.BlockSpec((rows, size), lambda i: (0, i)),
        ],
        out_specs=pl.BlockSpec((width, size), lambda i: (0, i)),
        out_shape=jax.ShapeDtypeStruct((width, features), F32),
        compiler_params=params(30),
        name="expert_grad",
        cost_estimate=cost(9),
    )(left, right)


def finish_body(
    table_ref, place_ref, own_q, own_k, own_v, far_q, far_k, far_v, *refs,
    groups, pairs, cuts, update,
):
    if update:
        mine_ref, weight_ref, refs = refs[0], refs[1], refs[2:]
    qkv_ref, out_ref, rows_ref, cols_ref = refs[:4]
    new_ref = refs[4] if update else None
    acc_ref, line_ref = refs[-2:]
    features = acc_ref.shape[0]
    rows = features // groups
    core = table_ref[0]
    chunk = 32

    def fill(grads_ref, source_of, n, start, stop, cols):
        def step(c, cols):
            first = pl.multiple_of(c * chunk, chunk)
            total = jnp.zeros((chunk, LANES), F32)
            grown = []
            for index in range(2 * pairs):
                w2, j = index // 2, index % 2
                block = source_of(n, w2, j, first).astype(F32)
                w = 2 * w2 + (core if j == 0 else 1 - core)
                place = pl.multiple_of(w * LANES, LANES)
                grads_ref[pl.ds(n * rows + first, chunk), pl.ds(place, LANES)] = block
                square = block * block
                total = total + square
                grown.append(cols[index] + jnp.sum(square.reshape(-1, 8, LANES), axis=0))
            acc_ref[pl.ds(n * rows + first, chunk), :] = total
            return tuple(grown)

        return lax.fori_loop(start // chunk, stop // chunk, step, cols)

    def matrix(m, grads_ref, pieces):
        cols = tuple(jnp.zeros((8, LANES), F32) for _ in range(2 * pairs))
        for n in range(groups):
            for chain, start, stop, shift, own, far in pieces:

                def source_of(n, w2, j, first, chain=chain, shift=shift, own=own, far=far):
                    at = table_ref[1 + (chain * groups + n) * pairs + w2]
                    ref = own if j == 0 else far
                    return ref[at, pl.ds(pl.multiple_of(first + shift, 16), chunk), :]

                cols = fill(grads_ref, source_of, n, start, stop, cols)
        for index in range(2 * pairs):
            w = 2 * (index // 2) + (core if index % 2 == 0 else 1 - core)
            total = jnp.sum(cols[index], axis=0, keepdims=True)
            cols_ref[0, w] = total / features + STAT_EPS
        squares = acc_ref[...]
        sums = lax.dot_general(
            jnp.ones((8, LANES), F32), squares, NT,
            precision=lax.Precision.HIGHEST, preferred_element_type=F32,
        )
        rows_ref[0] = sums / features + STAT_EPS
        if update:
            line = jnp.sum(squares, axis=1, keepdims=True) / features + STAT_EPS
            line_ref[...] = jnp.broadcast_to(line, line_ref.shape)
            mean = jnp.sum(line, axis=0, keepdims=True) / features
            my_rows = line_ref[pl.ds(pl.multiple_of(place_ref[0] * rows, rows), rows), :]
            my_cols = cols_ref[0, place_ref[1]]
            step = STEP_RATE * mine_ref[0] / jnp.sqrt(my_rows * my_cols / mean)
            new_ref[0] = weight_ref[0] - step if m < 3 else step

    owns, fars = (own_q, own_k, own_v), (far_q, far_k, far_v)
    for m in range(4):

        @pl.when(pl.program_id(0) == m)
        def _(m=m):
            if m < 3:
                matrix(m, qkv_ref.at[0], [(m, 0, rows, 0, owns[m], fars[m])])
            else:
                pieces = [
                    (i, cuts[i], cuts[i + 1], rows - cuts[i], owns[i], fars[i]) for i in range(3)
                ]
                matrix(m, out_ref, pieces)


def finish_call(table, place, gathered, groups, features, mine, weights):
    pairs = features // (2 * LANES)
    rows = features // groups
    owns = [g[0] for g in gathered]
    fars = [g[1] for g in gathered]
    update = mine is not None
    extra = [mine, weights] if update else []
    block = pl.BlockSpec((1, rows, LANES), lambda m: (m, 0, 0))
    shapes = [
        jax.ShapeDtypeStruct((3, features, features), F32),
        jax.ShapeDtypeStruct((features, features), F32),
        jax.ShapeDtypeStruct((4, 8, features), F32),
        jax.ShapeDtypeStruct((4, 2 * pairs, 1, LANES), F32),
    ]
    specs = [
        pl.BlockSpec((1, features, features), lambda m: (jnp.minimum(m, 2), 0, 0)),
        pl.BlockSpec((features, features), lambda m: (0, 0)),
        pl.BlockSpec((1, 8, features), lambda m: (m, 0, 0)),
        pl.BlockSpec((1, 2 * pairs, 1, LANES), lambda m: (m, 0, 0, 0)),
    ]
    if update:
        shapes.append(jax.ShapeDtypeStruct((4, rows, LANES), F32))
        specs.append(block)

    out = pl.pallas_call(
        functools.partial(
            finish_body, groups=groups, pairs=pairs, cuts=row_cuts(rows), update=update
        ),
        grid=(4,),
        in_specs=[smem()] * 2 + [vmem()] * 6 + [block] * len(extra),
        out_specs=specs,
        out_shape=shapes,
        scratch_shapes=[pltpu.VMEM((features, LANES), F32)] * 2,
        compiler_params=params(26),
        name="finish",
        cost_estimate=cost(10),
    )(table, place, *owns, *fars, *extra)
    stats = (out[0], out[1], out[2][:, 0], out[3].reshape(4, features))
    return stats + (out[4] if update else None,)


def on_device(
    tokens,
    attn_gain,
    qkv_weights,
    out_weight,
    rel_bias,
    moe_gain,
    router,
    gate_weight,
    up_weight,
    down_weight,
    expert_ids,
    expert_slots,
    buckets,
    upstream,
):
    length, features = tokens.shape
    bucket_count, head_count = rel_bias.shape
    head_dim = features // head_count
    groups = lax.axis_size("narrow")
    wide_count = lax.axis_size("wide")
    my_narrow = lax.axis_index("narrow")
    my_wide = lax.axis_index("wide")
    my_core = my_wide % 2
    part_width = gate_weight.shape[3]
    experts = router.shape[1] * wide_count
    places = experts // groups
    split_parts = wide_count // places
    capacity = (10 * length // experts + 3) // 4
    half_cap = capacity // 2
    row_count, col_count = qkv_weights.shape[1:]
    half_wide = wide_count // 2
    core_hop = ("wide", 0)
    part_hop = ("wide", 1)
    orders = hop_orders(groups, wide_count)
    slots = [block_slots(order, groups, wide_count) for order in orders]
    direct = col_count == LANES
    pairs = features // (2 * LANES)
    if direct:
        core_entry, tables = my_core, slots
    else:
        core_entry = jnp.int32(0)
        tables = [jnp.arange(groups * pairs, dtype=jnp.int32)] * 3
    table = jnp.concatenate(
        [jnp.reshape(core_entry, (1,)).astype(jnp.int32)] + [t.reshape(-1) for t in tables]
    )
    place = jnp.stack([my_narrow, my_wide]).astype(jnp.int32)

    def as_pairs(matrix):
        blocks = from_matrix(matrix, groups, pairs)
        return blocks.reshape((groups * pairs,) + blocks.shape[2:])

    def as_halves(owns, fars):
        if direct:
            return list(zip(owns, fars))
        out = []
        for own, far, slot in zip(owns, fars, slots):
            both = as_pairs(as_matrix(own, far, slot, my_core))
            out.append((both[:, 0], both[:, 1]))
        return out

    def halves_of(keep, send, chain):
        if direct:
            return keep, send
        rows = keep.shape[1]
        both = jnp.stack([keep, send.astype(F32)], axis=1).reshape(
            groups, pairs, 2, rows, LANES
        )
        matrix = jnp.transpose(both, (0, 3, 1, 2, 4)).reshape(groups * rows, features)
        parts = from_matrix(matrix, groups, half_wide)
        placed = jnp.zeros((groups * half_wide,) + parts.shape[2:], F32)
        placed = placed.at[slots[chain].reshape(-1)].set(parts.reshape(placed.shape))
        mine = jnp.where(my_core == 0, placed[:, 0], placed[:, 1])
        theirs = jnp.where(my_core == 0, placed[:, 1], placed[:, 0])
        return mine, theirs.astype(BF)

    def split_rows(values, ends):
        return [
            lax.slice_in_dim(values, a, b, axis=1) for a, b in zip([0] + ends[:-1], ends)
        ]

    narrow_hops = [("narrow", b) for b in range(groups.bit_length() - 1)]
    place_hops = [
        ("wide", b) for b in range(split_parts.bit_length() - 1, wide_count.bit_length() - 1)
    ][::-1]
    chains = (
        narrow_hops[:1] + place_hops + narrow_hops[1:],
        place_hops + narrow_hops[1:] + narrow_hops[:1],
    )
    hop_count = len(chains[0])
    row_table = jnp.concatenate(
        [row_slots(hops, groups, places, split_parts) for hops in chains]
    )
    back_hops = (chains[0][::-1], chains[0])
    back_table = jnp.concatenate(
        [row_slots(hops[::-1], groups, places, split_parts) for hops in back_hops]
    )
    owner_slot = expert_ids % groups * places + expert_ids // groups
    row_ids = jnp.where(expert_slots >= 0, owner_slot * capacity + expert_slots, -1).T

    def flat(rows):
        return rows.reshape(-1, rows.shape[-1])

    def sends(states, step):
        return [row_send(state, hops[step]) for state, hops in zip(states, chains)]

    def joins(states, gots):
        return [row_join(state, got) for state, got in zip(states, gots)]

    def to_core(values):
        return [from_partner(value, core_hop) for value in values]

    def to_part(values):
        return [from_partner(value, part_hop) for value in values]

    def add(a, b):
        return a.astype(F32) + b.astype(F32)

    def homeward(rows):
        return rows.astype(BF).reshape(-1, 1, half_cap, rows.shape[-1])

    def homeward_start(states):
        return [(state, list(hops)) for state, hops in zip(states, chains)]

    def backs_out(states, step):
        gots = {}
        for chain in range(2):
            at = step - chain
            if 0 <= at < hop_count:
                gots[chain] = back_send(*states[chain], back_hops[chain][at])
        return gots

    def backs_join(states, gots, step):
        return [
            back_join(*state, back_hops[chain][step - chain], gots[chain])
            if chain in gots
            else state
            for chain, state in enumerate(states)
        ]

    def slots_first(states):
        return [state.reshape((-1,) + state.shape[2:]) for state, _ in states]

    router_tail = router.astype(BF).reshape(-1, col_count)
    tail_rows = router_tail.shape[0]
    out_low = jnp.concatenate(
        [
            out_weight.astype(BF),
            router_tail,
            jnp.zeros((-tail_rows % 16, col_count), BF),
        ],
        axis=0,
    )
    qkv_low = qkv_weights.astype(BF)
    upstream_a, upstream_b = upstream_call(
        row_table, upstream, row_ids, expert_ids.T[::-1].astype(F32), experts, capacity
    )
    shared = shared_hops(orders)
    stages = range(shared, len(orders[0]) - 1)
    u_state = [upstream_a[None], upstream_b[None]]
    cuts = row_cuts(row_count)
    low_cuts = cuts[:3] + [out_low.shape[0]]
    pieces, ends = [], []
    for i in range(3):
        pieces += [qkv_low[i], out_low[low_cuts[i] : low_cuts[i + 1]]]
        ends.append(sum(piece.shape[0] for piece in pieces))
    blocks = jnp.concatenate(pieces, axis=0)[None]
    for hop in orders[0][:shared]:
        blocks = grow(blocks, from_partner(blocks, hop))
    u_state, blocks = together(u_state, blocks)
    u_got = sends(u_state, 0)
    dense = split_rows(blocks, ends)
    for count, stage in enumerate(stages):
        got = [from_partner(c, order[stage]) for c, order in zip(dense, orders)]
        if count == 1:
            u_got, got = together(u_got, got)
            u_state = joins(u_state, u_got)
            u_got = sends(u_state, 1)
        dense = [grow(c, g) for c, g in zip(dense, got)]
    dense_far = to_core(dense)
    weight_parts = as_halves(dense, dense_far)
    tails = [half[:, -(out_low.shape[0] - row_count) :][:, :tail_rows] for half in (dense[2], dense_far[2])]
    full_router = jnp.transpose(
        as_matrix(*tails, slots[2], my_core)
        .reshape(groups, tail_rows, wide_count, col_count)
        .transpose(0, 2, 1, 3)
        .reshape(groups, wide_count, row_count, router.shape[1]),
        (0, 2, 1, 3),
    ).reshape(features, experts)
    router_wide = jnp.pad(full_router, ((0, 0), (0, -experts % LANES)))
    gate_low = gate_weight[0, 0].T.astype(BF)
    up_low = up_weight[0, 0].T.astype(BF)
    down_low = down_weight[0, 0].astype(BF)
    table_hot = (
        jnp.pad(buckets, (0, 1), constant_values=-1)[:, None]
        == jnp.arange(bucket_count, dtype=jnp.int32)[None, :]
    ).astype(F32)
    bias_table = jnp.dot(table_hot, rel_bias, precision=lax.Precision.HIGHEST).T
    normed_in, heads, probs, attended = attend_call(
        table, tokens, attn_gain, bias_table, weight_parts, groups, head_dim
    )
    u_got, attended = together(u_got, attended)
    for step in range(2, hop_count):
        u_state = joins(u_state, u_got)
        u_got = sends(u_state, step)
    hidden_x1, moe_input, send_a, send_b = post_call(
        table, row_table, tokens, attended, weight_parts, moe_gain, row_ids, groups, experts,
        capacity,
    )
    u_got, send_a, send_b = together(u_got, send_a, send_b)
    u_own = [flat(state) for state in joins(u_state, u_got)]
    u_core, u_part = to_core(u_own), to_part(u_own[:1])
    x_state = [send_a[None], send_b[None]]
    for step in range(hop_count):
        x_got = sends(x_state, step)
        if step == 0:
            x_got, u_core, u_part[0], router_wide = together(
                x_got, u_core, u_part[0], router_wide
            )
        else:
            x_got = together(*x_got)
        x_state = joins(x_state, x_got)
    late_parts, _ = together(weight_parts, send_a)
    projection_parts = [tuple(half[:, row_count:] for half in part) for part in late_parts]
    projection_parts, x_state = together(projection_parts, x_state)
    x_own = [flat(state) for state in x_state]
    x_core, x_part = to_core(x_own), to_part(x_own[:1])
    joined_part = from_partner(jnp.concatenate([x_own[1], u_own[1]], axis=1), part_hop)

    my_expert = (my_narrow + groups * (my_wide // split_parts)).reshape(1).astype(jnp.int32)
    row_total = 8 * x_own[0].shape[0]

    def run_expert(xs, us, first, kept):
        return expert_call(
            my_expert, xs, us, router_wide, gate_low, up_low, down_low, first, row_total, kept
        )

    y_near, dx_near, kept = run_expert(x_own + x_core, u_own + u_core, 0, None)
    x_part[0], u_part[0], dx_near = together(x_part[0], u_part[0], dx_near)
    dx_near_got = to_core(dx_near[2:])
    y_far, parts_back = [], []
    for chain in range(2):
        if chain:
            joined_part, y_far = together(joined_part, y_far)
            xs = [joined_part, from_partner(joined_part, core_hop)]
            us = []
        else:
            xs = [x_part[0], from_partner(x_part[0], core_hop)]
            us = [u_part[0], from_partner(u_part[0], core_hop)]
        y_two, dx_two, kept = run_expert(xs, us, 4 + 2 * chain, kept)
        if chain:
            y_two, dx_two, kept, parts_back[0] = together(y_two, dx_two, kept, parts_back[0])
        y_far.append(y_two)
        far_got = from_partner(dx_two[1], core_hop)
        far_sum = add(dx_two[0], far_got).astype(BF)
        if not chain:
            kept, far_sum = together(kept, far_sum)
        parts_back.append(from_partner(far_sum, part_hop))
    kept, far_sum = together(kept, far_sum)
    y_near_got = to_core(y_near[2:])
    y_far_got = to_core([two[1] for two in y_far])

    def home_sum(chain, part):
        near = add(dx_near[chain], dx_near_got[chain])
        return homeward(near + part.astype(F32))

    x_all, dy_all, hidden_all, dgate_all, dup_all = kept
    states = homeward_start([home_sum(0, parts_back[0]), None])
    for step in range(hop_count + 1):
        gots = backs_out(states, step)
        if step == 0:
            gate_local = expert_grad_call(dgate_all, x_all)
            up_local = expert_grad_call(dup_all, x_all)
            gots, part_b, gate_local, up_local, hidden_all = together(
                gots, parts_back[1], gate_local, up_local, hidden_all
            )
            states[1] = (home_sum(1, part_b), list(chains[1]))
        elif step == 1:
            down_local = expert_grad_call(hidden_all, dy_all)
            y_sums = [add(mine, got).astype(BF) for mine, got in zip(y_near[:2], y_near_got)]
            y_far_sums = [
                add(two[0], got).astype(BF) for two, got in zip(y_far, y_far_got)
            ]
            gots, down_local, y_sums, y_far_sums = together(
                gots, down_local, y_sums, y_far_sums
            )
            y_part_got = to_part(y_far_sums[:1])
        elif step == 2:
            squares = [g * g for g in (gate_local, up_local, down_local)]
            local_sums = jnp.stack([jnp.sum(q, axis=0) for q in squares], axis=0)
            part_stats = jnp.stack([jnp.mean(q, axis=1) for q in squares], axis=0) + STAT_EPS
            sums_got = from_partner(local_sums, core_hop)
            gots, local_sums, y_part_got, sums_got = together(
                gots, local_sums, y_part_got, sums_got
            )
        elif step == 3:
            sums_got, y_far_sums = together(sums_got, y_far_sums)
            local_sums = local_sums + sums_got
            sums_got = from_partner(local_sums, part_hop)
            sums_got, y_far_sums = together(sums_got, y_far_sums)
            y_part_got = y_part_got + to_part(y_far_sums[1:])
            wide_stats = (local_sums + sums_got) / (part_width * split_parts) + STAT_EPS
            gate_new = factored(
                gate_weight[0, 0].T, gate_local, part_stats[0], wide_stats[0],
                jnp.mean(wide_stats[0]),
            )
            up_new = factored(
                up_weight[0, 0].T, up_local, part_stats[1], wide_stats[1],
                jnp.mean(wide_stats[1]),
            )
            down_new = factored(
                down_weight[0, 0], down_local, part_stats[2], wide_stats[2],
                jnp.mean(wide_stats[2]),
            )
            gots, gate_new, up_new, down_new, wide_stats = together(
                gots, gate_new, up_new, down_new, wide_stats
            )
        else:
            gots = together(gots)[0]
        states = backs_join(states, gots, step)
    inputs_back = slots_first(states)
    y_home = homeward(add(y_sums[0], y_part_got[0]))
    inputs_back, y_home = together(inputs_back, y_home)
    y_states = homeward_start([y_home, None])
    y_gots = backs_out(y_states, 0)

    x1_grad, gates, moe_gain_local, router_local, out_keep, out_send, attended_grad = mid_call(
        table, back_table, hidden_x1, moe_gain, moe_input, upstream, inputs_back, row_ids,
        expert_ids, router_wide, attended, projection_parts, groups, experts, capacity,
    )
    y_part_got, y_gots, attended_grad, out_send = together(
        y_part_got, y_gots, attended_grad, out_send
    )
    y_states = backs_join(y_states, y_gots, 0)
    y_states[1] = (homeward(add(y_sums[1], y_part_got[1])), list(chains[1]))
    y_gots = backs_out(y_states, 1)

    *grads, dheads, diag = attend_back_call(
        table, normed_in, heads, probs, attended_grad, out_keep, out_send, groups, head_dim
    )
    halves = [halves_of(grads[i], grads[3 + i], i) for i in range(3)]
    addends = [[keep, from_partner(send, core_hop)] for keep, send in halves]
    ends, size = [], 0
    for value, _ in addends:
        size += value.shape[1]
        ends.append(size)
    y_step = 1
    router_local, moe_gain_local, dheads, x1_grad, diag, _ = together(
        router_local, moe_gain_local, dheads, x1_grad, diag, addends
    )

    def halve(values, hop):
        half = values[0].shape[0] // 2
        send = sum(value[half:].astype(F32) for value in values).astype(BF)
        return [value[:half] for value in values], from_partner(send, hop)

    def more_outputs():
        joined = backs_join(y_states, y_gots, y_step)
        return joined, backs_out(joined, y_step + 1), y_step + 1

    small_hops = list(orders[0])
    for count, stage in enumerate(stages[::-1]):
        halved = [halve(values, order[stage]) for values, order in zip(addends, orders)]
        gots = [got for _, got in halved]
        if count == 0:
            tokens_grad, attn_gain_local = tokens_back_call(
                table, tokens, attn_gain, x1_grad, dheads, weight_parts, groups
            )
            tail = jnp.pad(diag, ((0, 0), (0, 0), (0, 8)))
            line = sum(tail[:, i, i : i + 2 * length] for i in range(8))
            bias_local = jnp.dot(line, table_hot, precision=lax.Precision.HIGHEST)
            small = jnp.concatenate(
                [
                    attn_gain_local.reshape(-1),
                    moe_gain_local.reshape(-1),
                    bias_local.reshape(-1),
                    router_local[:experts].reshape(-1),
                ]
            ).reshape(-1, LANES)
            gots, small, y_gots = together(gots, small, y_gots)
            y_states, y_gots, y_step = more_outputs()
        else:
            small_got = from_partner(small, small_hops.pop(0))
            if y_gots:
                gots, small_got, y_gots = together(gots, small_got, y_gots)
                y_states, y_gots, y_step = more_outputs()
            else:
                gots, small_got = together(gots, small_got)
            small = small + small_got
        addends = [kept + [got] for (kept, _), got in zip(halved, gots)]
    summed = [sum(value.astype(F32) for value in values) for values in addends]
    while y_gots:
        y_states, y_gots, y_step = more_outputs()
    def small_beside(value, others):
        if not small_hops:
            return value, together(*others)
        got = from_partner(value, small_hops.pop(0))
        out = together(got, *others)
        return value + out[0], out[1:]

    total = jnp.concatenate(summed, axis=1)
    for hop in orders[0][:shared][::-1]:
        got = halve_send(total, hop)
        small, (got, y_states) = small_beside(small, (got, y_states))
        total = halve_add(total, got)
    block_out = block_out_call(
        back_table, hidden_x1, gates, slots_first(y_states), row_ids, experts, capacity
    )
    blocks = total.astype(BF)
    for hop in orders[0][:shared]:
        got = from_partner(blocks, hop)
        small, (got, total, block_out) = small_beside(small, (got, total, block_out))
        blocks = grow(blocks, got)
    pieces = split_rows(total, ends)
    dense_mine = jnp.concatenate(
        [piece[:, :row_count] for piece in pieces]
        + [jnp.concatenate([piece[:, row_count:] for piece in pieces], axis=1)],
        axis=0,
    )
    dense_weights = jnp.concatenate([qkv_weights, out_weight[None]], axis=0)
    dense = split_rows(blocks, ends)
    router_size = features * experts
    for count, stage in enumerate(stages):
        gots = [from_partner(chain, order[stage]) for chain, order in zip(dense, orders)]
        if count == 0:
            small, (gots,) = small_beside(small, (gots,))
            small, small_hops = cube_sum(small, small_hops), []
        elif count == 1:
            small, (gots, dense_mine, dense_weights) = small_beside(
                small, (gots, dense_mine, dense_weights)
            )
        else:
            gots, router_out = together(gots, router_out)
        if count == 0:
            router_total = small.reshape(-1)[-router_size:].reshape(experts, features)
            router_sq = router_total * router_total
            router_rows = jnp.mean(router_sq, axis=0) + STAT_EPS
            router_cols = jnp.mean(router_sq, axis=1) + STAT_EPS
            rows_first, cols_first = my_narrow * router.shape[0], my_wide * router.shape[1]
            router_new = factored(
                router.T,
                lax.dynamic_slice(router_total, (cols_first, rows_first), router.T.shape),
                lax.dynamic_slice_in_dim(router_cols, cols_first, router.shape[1], 0),
                lax.dynamic_slice_in_dim(router_rows, rows_first, router.shape[0], 0),
                jnp.mean(router_rows),
            )
            small_flat = small.reshape(-1)
            router_out = (
                small_flat[:features],
                small_flat[features : 2 * features],
                small_flat[2 * features : -router_size].reshape(head_count, bucket_count),
                router_total, router_new, router_rows, router_cols,
            )
        dense = [grow(chain, got) for chain, got in zip(dense, gots)]
    gain_a_total, gain_m_total, bias_total, router_total, router_new, router_rows, router_cols = (
        router_out
    )
    dense_parts = as_halves(dense, to_core(dense))
    qkv_total, out_total, rows, cols, dense_new = finish_call(
        table, place, dense_parts, groups, features, dense_mine if direct else None,
        dense_weights,
    )
    if not direct:
        rows_mine = lax.dynamic_slice_in_dim(rows, my_narrow * row_count, row_count, 1)
        cols_mine = lax.dynamic_slice_in_dim(cols, my_wide * col_count, col_count, 1)
        step = adafactor_step(dense_mine, rows_mine, cols_mine, jnp.mean(rows, axis=1))
        dense_new = jnp.concatenate([qkv_weights - step[:3], step[3:]], axis=0)
    qkv_stats = jnp.stack([rows[:3], cols[:3]], axis=0)
    out_stats = jnp.concatenate([rows[3:], cols[3:]], axis=0)
    return (
        block_out,
        tokens_grad,
        gain_a_total,
        qkv_total,
        out_total,
        bias_total.T,
        gain_m_total,
        router_total.T,
        gate_local.T[None, None],
        up_local.T[None, None],
        down_local[None, None],
        dense_new[:3],
        dense_new[3],
        router_new.T,
        gate_new.T[None, None],
        up_new.T[None, None],
        down_new[None, None],
        qkv_stats,
        out_stats,
        router_rows,
        router_cols,
        wide_stats[None, None],
        part_stats[None, None],
    )


def solution(mesh):
    in_specs = (
        P(("narrow", "wide"), None),
        P(),
        P(None, "narrow", "wide"),
        P("narrow", "wide"),
        P(),
        P(),
        P("narrow", "wide"),
        P("narrow", "wide", None, None),
        P("narrow", "wide", None, None),
        P("narrow", "wide", None, None),
        P(("narrow", "wide"), None),
        P(("narrow", "wide"), None),
        P(),
        P(("narrow", "wide"), None),
    )
    out_specs = (
        P(("narrow", "wide"), None),
        P(("narrow", "wide"), None),
        P(),
        P(),
        P(),
        P(),
        P(),
        P(),
        P("narrow", "wide", None, None),
        P("narrow", "wide", None, None),
        P("narrow", "wide", None, None),
        P(None, "narrow", "wide"),
        P("narrow", "wide"),
        P("narrow", "wide"),
        P("narrow", "wide", None, None),
        P("narrow", "wide", None, None),
        P("narrow", "wide", None, None),
        P(),
        P(),
        P(),
        P(),
        P("narrow", "wide", None, None),
        P("narrow", "wide", None, None),
    )
    return jax.shard_map(
        on_device, mesh=mesh, in_specs=in_specs, out_specs=out_specs, check_vma=False
    )
```

```python
import functools

import jax
import jax.numpy as jnp
from jax import lax
from jax.experimental import pallas as pl
from jax.experimental.pallas import tpu as pltpu
from jax.sharding import PartitionSpec as P

NORM_EPS = 1e-06
STAT_EPS = 1e-06
STEP_RATE = 0.01
LANES = 128
GELU_C = 0.7978845608028654
GELU_A = 0.044715
BF = jnp.bfloat16
F32 = jnp.float32
NN = (((1,), (0,)), ((), ()))
NT = (((1,), (1,)), ((), ()))
TN = (((0,), (0,)), ((), ()))


def mm(a, b, dims=NN):
    return lax.dot_general(a, b, dims, preferred_element_type=F32)


def from_partner(value, hop):
    axis, bit = hop
    mask = 2**bit
    pairs = [(source, source ^ mask) for source in range(lax.axis_size(axis))]
    return lax.ppermute(value, axis, pairs)


def after(values, *others):
    return lax.optimization_barrier((values, others))[0]


def hop_orders(groups, wide_count):
    narrow = [("narrow", b) for b in range(groups.bit_length() - 1)]
    wide = [("wide", b) for b in range(1, wide_count.bit_length() - 1)]
    far, near = wide[1:][::-1], wide[:1]
    core = [("wide", 0)]
    return (
        far + narrow + near + core,
        far + near + narrow + core,
        far + narrow[1:] + near + narrow[:1] + core,
    )


def row_cuts(count):
    share = -(-count // 48) * 16
    return [min(i * share, count) for i in range(4)]


def block_slots(order, groups, wide_count):
    n_ids = jnp.arange(groups, dtype=jnp.int32)[:, None]
    w_ids = 2 * jnp.arange(wide_count // 2, dtype=jnp.int32)[None, :]
    slots = jnp.zeros((groups, wide_count // 2), jnp.int32)
    for stage, (axis, bit) in enumerate(order[:-1]):
        ids = n_ids if axis == "narrow" else w_ids
        differs = ((ids ^ lax.axis_index(axis)) >> bit) & 1
        slots = slots | (differs << stage)
    return slots


def together(*values):
    return lax.optimization_barrier(values)


def shared_hops(orders):
    count = 0
    while len({order[count] for order in orders}) == 1 and count < len(orders[0]) - 1:
        count += 1
    return count


def grow(blocks, got, axis=0):
    return jnp.concatenate([blocks, got], axis=axis)


def core_sum(keep, got):
    return keep + got.astype(F32)


def halve_send(total, hop, axis=0):
    half = total.shape[axis] // 2
    return from_partner(lax.slice_in_dim(total, half, 2 * half, axis=axis).astype(BF), hop)


def halve_add(total, got, axis=0):
    half = total.shape[axis] // 2
    return lax.slice_in_dim(total, 0, half, axis=axis) + got.astype(F32)


def row_send(state, hop):
    sources, places = state.shape[:2]
    return from_partner(state.reshape((sources, 2, places // 2) + state.shape[2:])[:, 1], hop)


def row_join(state, got):
    sources, places = state.shape[:2]
    kept = state.reshape((sources, 2, places // 2) + state.shape[2:])[:, 0]
    return jnp.concatenate([kept, got], axis=0)


def back_split(state, left, hop):
    low = 2 ** left.index(hop)
    split = state.reshape((-1, 2, low) + state.shape[1:])
    return [split[:, i].reshape((-1,) + state.shape[1:]) for i in range(2)]


def back_send(state, left, hop):
    return from_partner(back_split(state, left, hop)[1], hop)


def back_join(state, left, hop, got):
    kept = back_split(state, left, hop)[0]
    joined = jnp.stack([kept, got], axis=1).reshape((got.shape[0], -1) + state.shape[2:])
    return joined, [other for other in left if other != hop]


def row_slots(hops, groups, places, parts):
    n_ids = jnp.arange(groups, dtype=jnp.int32)[:, None]
    w_ids = parts * jnp.arange(places, dtype=jnp.int32)[None, :]
    slots = jnp.zeros((groups, places), jnp.int32)
    for axis, bit in hops:
        ids = n_ids if axis == "narrow" else w_ids
        slots = 2 * slots + (((ids ^ lax.axis_index(axis)) >> bit) & 1)
    return slots.reshape(-1)


def cube_sum(value, hops):
    for hop in hops:
        value = value + from_partner(value, hop)
    return value


def as_matrix(own, other, slots, my_core):
    groups, half_wide = slots.shape
    both = jnp.stack([jnp.where(my_core == 0, own, other), jnp.where(my_core == 0, other, own)], 1)
    picked = jnp.take(both, slots.reshape(-1), axis=0)
    rows, cols = own.shape[1:]
    picked = picked.reshape(groups, half_wide, 2, rows, cols)
    return jnp.transpose(picked, (0, 3, 1, 2, 4)).reshape(groups * rows, half_wide * 2 * cols)


def from_matrix(matrix, groups, half_wide):
    lead = matrix.shape[:-2]
    rows, cols = matrix.shape[-2] // groups, matrix.shape[-1] // (2 * half_wide)
    shaped = matrix.reshape(lead + (groups, rows, half_wide, 2, cols))
    k = len(lead)
    order = tuple(range(k)) + (k, k + 2, k + 3, k + 1, k + 4)
    return jnp.transpose(shaped, order)


def gelu_tanh(values):
    return jax.nn.gelu(values, approximate=True)


def adafactor_step(gradient, row_stats, col_stats, mean_rows):
    return (
        STEP_RATE
        * gradient
        / jnp.sqrt(row_stats[..., :, None] * col_stats[..., None, :] / mean_rows[..., None, None])
    )


def factored(weight, gradient, row_stats, col_stats, mean_rows):
    return weight - adafactor_step(gradient, row_stats, col_stats, mean_rows)


def vmem():
    return pl.BlockSpec(memory_space=pltpu.VMEM)


def smem():
    return pl.BlockSpec(memory_space=pltpu.SMEM)


def params(mebibytes):
    return pltpu.CompilerParams(vmem_limit_bytes=mebibytes * 1024 * 1024)


def cost(micros):
    return pl.CostEstimate(
        flops=int(micros * 1153e6), transcendentals=0, bytes_accessed=int(micros * 3690e3)
    )


def lane_masks(head_dim):
    heads = LANES // head_dim
    ids = lax.broadcasted_iota(jnp.int32, (1, LANES), 1) // head_dim
    return [ids == i for i in range(heads)]


def attend_body(
    table_ref, tokens_ref, gain_ref, bias_ref,
    own_q, own_k, own_v, far_q, far_k, far_v,
    normed_ref, heads_ref, probs_ref, attended_ref,
    *, groups, pairs, head_dim,
):
    length, features = tokens_ref.shape
    rows = features // groups
    x = tokens_ref[...].astype(F32)
    factor = lax.rsqrt(jnp.mean(x * x, axis=-1, keepdims=True) + NORM_EPS)
    normed_ref[...] = (x * factor * gain_ref[...]).astype(BF)
    core = table_ref[0]

    def project(w2, carry):
        for m, (own, far) in enumerate(((own_q, far_q), (own_k, far_k), (own_v, far_v))):
            total = None
            for n in range(groups):
                at = table_ref[1 + (m * groups + n) * pairs + w2]
                block = jnp.concatenate([own[at, :rows], far[at, :rows]], axis=1)
                part = mm(normed_ref[:, n * rows : (n + 1) * rows], block)
                total = part if total is None else total + part
            total = total.astype(BF)
            heads_ref[m, 2 * w2 + core] = total[:, :LANES]
            heads_ref[m, 2 * w2 + 1 - core] = total[:, LANES:]
        return carry

    lax.fori_loop(0, pairs, project, 0)
    masks = lane_masks(head_dim)
    scale = head_dim**-0.5

    def attend(w, carry):
        q, k, v = heads_ref[0, w], heads_ref[1, w], heads_ref[2, w]
        mixed = jnp.zeros((length, LANES), F32)
        for i, mask in enumerate(masks):
            head = w * len(masks) + i
            raw = mm(jnp.where(mask, q, jnp.zeros_like(q)), k, NT)
            line = jnp.broadcast_to(bias_ref[pl.ds(head, 1), :], (length, 2 * length))
            bias = pltpu.roll(line, length + 1, 1, stride=1, stride_axis=0)[:, :length]
            scores = raw * scale + bias
            top = jnp.max(scores, axis=-1, keepdims=True)
            grown = jnp.exp(scores - top)
            probs = grown / jnp.sum(grown, axis=-1, keepdims=True)
            probs_ref[head] = probs
            mixed = jnp.where(mask, mm(probs.astype(BF), v), mixed)
        attended_ref[w] = mixed.astype(BF)
        return carry

    lax.fori_loop(0, 2 * pairs, attend, 0)


def attend_call(table, tokens, gain, bias_table, gathered, groups, head_dim):
    length, features = tokens.shape
    pairs = features // (2 * LANES)
    head_count = features // head_dim
    owns = [g[0] for g in gathered]
    fars = [g[1] for g in gathered]
    body = functools.partial(attend_body, groups=groups, pairs=pairs, head_dim=head_dim)
    return pl.pallas_call(
        body,
        in_specs=[smem()] + [vmem()] * 9,
        out_specs=[vmem()] * 4,
        out_shape=[
            jax.ShapeDtypeStruct((length, features), BF),
            jax.ShapeDtypeStruct((3, 2 * pairs, length, LANES), BF),
            jax.ShapeDtypeStruct((head_count, length, length), F32),
            jax.ShapeDtypeStruct((2 * pairs, length, LANES), BF),
        ],
        compiler_params=params(14),
        name="attend",
        cost_estimate=cost(16),
    )(table, tokens, gain.reshape(1, features), bias_table, *owns, *fars)


def expert_hot(ids_ref, expert, cap, length):
    slot = lax.broadcasted_iota(jnp.int32, (cap, length), 0) + expert * cap
    return [slot == ids_ref[c : c + 1, :] for c in range(2)]


def spread_rows(values, ids_ref, slots_ref, sends, experts, cap):
    length, features = values.shape
    half = cap // 2
    for e in range(experts):
        first, second = expert_hot(ids_ref, e, cap, length)
        rows = mm(jnp.where(first | second, 1.0, 0.0).astype(BF), values)
        for chain, send in enumerate(sends):
            at = slots_ref[chain * experts + e]
            send[at, :, :features] = rows[chain * half : (chain + 1) * half].astype(BF)


def upstream_body(slots_ref, values_ref, ids_ref, others_ref, send_a, send_b, *, experts, cap):
    length, features = values_ref.shape
    half = cap // 2
    spread_rows(values_ref[...], ids_ref, slots_ref, (send_a, send_b), experts, cap)
    for e in range(experts):
        first, second = expert_hot(ids_ref, e, cap, length)
        other = jnp.where(first, others_ref[0:1, :], 0.0) + jnp.where(
            second, others_ref[1:2, :], 0.0
        )
        other = jnp.sum(other, axis=1, keepdims=True)
        other = jnp.broadcast_to(other, (cap, LANES))
        for chain, send in enumerate((send_a, send_b)):
            at = slots_ref[chain * experts + e]
            send[at, :, features:] = other[chain * half : (chain + 1) * half].astype(BF)


def upstream_call(row_table, upstream, row_ids, other_ids, experts, cap):
    features = upstream.shape[1]
    return pl.pallas_call(
        functools.partial(upstream_body, experts=experts, cap=cap),
        in_specs=[smem()] + [vmem()] * 3,
        out_specs=[vmem()] * 2,
        out_shape=[jax.ShapeDtypeStruct((experts, cap // 2, features + LANES), BF)] * 2,
        compiler_params=params(8),
        name="upstream_rows",
        cost_estimate=cost(3),
    )(row_table, upstream, row_ids, other_ids)


def projection_block(halves, table_ref, n, w2, groups, pairs, depth, cuts):
    sides = []
    for refs in halves:
        parts = []
        for i in range(3):
            at = table_ref[1 + (i * groups + n) * pairs + w2]
            first = depth if refs[i].shape[1] > depth else 0
            parts.append(refs[i][at, first : first + cuts[i + 1] - cuts[i]])
        sides.append(jnp.concatenate(parts, axis=0))
    return jnp.concatenate(sides, axis=1)


def post_body(
    table_ref, slots_ref, tokens_ref, attended_ref,
    own_q, own_k, own_v, far_q, far_k, far_v, gain_ref, ids_ref,
    x1_ref, normed_ref, send_a, send_b,
    *, groups, experts, cap, cuts,
):
    length, features = tokens_ref.shape
    pairs = features // (2 * LANES)
    per_group = 2 * pairs // groups
    depth = features // groups
    halves = ((own_q, own_k, own_v), (far_q, far_k, far_v))
    core = table_ref[0]
    rows = [
        jnp.concatenate([attended_ref[n * per_group + i] for i in range(per_group)], axis=1)
        for n in range(groups)
    ]
    for w2 in range(pairs):
        total = None
        for n in range(groups):
            block = projection_block(halves, table_ref, n, w2, groups, pairs, depth, cuts)
            part = mm(rows[n], block)
            total = part if total is None else total + part
        for j in range(2):
            w = 2 * w2 + (core if j == 0 else 1 - core)
            place = pl.multiple_of(w * LANES, LANES)
            mine = total[:, j * LANES : (j + 1) * LANES]
            x1_ref[:, pl.ds(place, LANES)] = mine + tokens_ref[:, pl.ds(place, LANES)].astype(F32)
    x1 = x1_ref[...]
    factor = lax.rsqrt(jnp.mean(x1 * x1, axis=-1, keepdims=True) + NORM_EPS)
    normed = (x1 * factor * gain_ref[...]).astype(BF)
    normed_ref[...] = normed
    spread_rows(normed, ids_ref, slots_ref, (send_a, send_b), experts, cap)


def post_call(table, row_table, tokens, attended, gathered, gain, row_ids, groups, experts, cap):
    length, features = tokens.shape
    owns = [g[0] for g in gathered]
    fars = [g[1] for g in gathered]
    cuts = row_cuts(features // groups)
    return pl.pallas_call(
        functools.partial(post_body, groups=groups, experts=experts, cap=cap, cuts=cuts),
        in_specs=[smem()] * 2 + [vmem()] * 10,
        out_specs=[vmem()] * 4,
        out_shape=[
            jax.ShapeDtypeStruct((length, features), F32),
            jax.ShapeDtypeStruct((length, features), BF),
            jax.ShapeDtypeStruct((experts, cap // 2, features), BF),
            jax.ShapeDtypeStruct((experts, cap // 2, features), BF),
        ],
        compiler_params=params(12),
        name="post",
        cost_estimate=cost(3),
    )(
        table, row_table, tokens, attended, *owns, *fars, gain.reshape(1, features), row_ids
    )


def mid_body(
    table_ref, slots_ref, x1_ref, gain_ref, normed_ref, upstream_ref, back_a, back_b,
    ids_ref, choice_ref, router_ref, attended_ref,
    own_q, own_k, own_v, far_q, far_k, far_v,
    x1_grad_ref, gates_ref, gain_out_ref, router_out_ref, keep_ref, send_ref, att_grad_ref,
    *, groups, experts, cap, cuts,
):
    length, features = x1_ref.shape
    pairs = features // (2 * LANES)
    per_group = 2 * pairs // groups
    rows = features // groups
    half = cap // 2
    halves = ((own_q, own_k, own_v), (far_q, far_k, far_v))
    core = table_ref[0]
    dmoe = jnp.zeros((length, features), F32)
    dots = [jnp.zeros((length, LANES), F32)] * 2
    for e in range(experts):
        hots = expert_hot(ids_ref, e, cap, length)
        hots = [jnp.where(hot, 1.0, 0.0).astype(BF) for hot in hots]
        both = hots[0] + hots[1]
        for chain, back in enumerate((back_a, back_b)):
            at = slots_ref[chain * experts + e]
            part = slice(chain * half, (chain + 1) * half)
            got = back[at]
            dmoe = dmoe + mm(both[part], got[:, :features], TN)
            for c in range(2):
                dots[c] = dots[c] + mm(hots[c][part], got[:, features:], TN)
    normed = normed_ref[...]
    logits = mm(normed, router_ref[...])
    lane = lax.broadcasted_iota(jnp.int32, logits.shape, 1)
    picks = [lane == choice_ref[:, c : c + 1] for c in range(2)]
    picked = [jnp.sum(jnp.where(pick, logits, 0.0), axis=1, keepdims=True) for pick in picks]
    top = jnp.maximum(picked[0], picked[1])
    grown = [jnp.exp(value - top) for value in picked]
    gates = [value / (grown[0] + grown[1]) for value in grown]
    gates_ref[...] = jnp.where(lane == 0, gates[0], jnp.where(lane == 1, gates[1], 0.0))
    dgates = [dot[:, 0:1] for dot in dots]
    inner = gates[0] * dgates[0] + gates[1] * dgates[1]
    dlogits = jnp.where(picks[0], gates[0] * (dgates[0] - inner), 0.0) + jnp.where(
        picks[1], gates[1] * (dgates[1] - inner), 0.0
    )
    dlogits = dlogits.astype(BF)
    router_out_ref[...] = mm(dlogits, normed, TN)
    dmoe = dmoe + mm(dlogits, router_ref[...], NT)
    x1 = x1_ref[...]
    factor = lax.rsqrt(jnp.mean(x1 * x1, axis=-1, keepdims=True) + NORM_EPS)
    hat = x1 * factor
    gain_out_ref[...] = jnp.sum(dmoe * hat, axis=0, keepdims=True)
    scaled = dmoe * gain_ref[...]
    inner = jnp.mean(scaled * hat, axis=-1, keepdims=True)
    x1_grad_ref[...] = upstream_ref[...].astype(F32) + factor * (scaled - hat * inner)
    branches = []
    for w2 in range(pairs):
        both = []
        for j in range(2):
            w = 2 * w2 + (core if j == 0 else 1 - core)
            both.append(x1_grad_ref[:, pl.ds(pl.multiple_of(w * LANES, LANES), LANES)].astype(BF))
        branches.append(jnp.concatenate(both, axis=1))
    for n in range(groups):
        att = jnp.concatenate(
            [attended_ref[n * per_group + i] for i in range(per_group)], axis=1
        )
        total = None
        for w2 in range(pairs):
            block = mm(att, branches[w2], TN)
            for i in range(3):
                at = table_ref[1 + (i * groups + n) * pairs + w2]
                keep_ref[at, cuts[i] : cuts[i + 1]] = block[cuts[i] : cuts[i + 1], :LANES]
                send = block[cuts[i] : cuts[i + 1], LANES:].astype(BF)
                send_ref[at, cuts[i] : cuts[i + 1]] = send
            block = projection_block(halves, table_ref, n, w2, groups, pairs, rows, cuts)
            part = mm(branches[w2], block, NT)
            total = part if total is None else total + part
        for i in range(per_group):
            att_grad_ref[n * per_group + i] = total[:, i * LANES : (i + 1) * LANES].astype(BF)


def mid_call(
    table, row_table, x1, gain, normed, upstream, backs, row_ids, choices, router, attended,
    gathered, groups, experts, cap,
):
    length, features = x1.shape
    pairs = features // (2 * LANES)
    rows = features // groups
    owns = [g[0] for g in gathered]
    fars = [g[1] for g in gathered]
    return pl.pallas_call(
        functools.partial(
            mid_body, groups=groups, experts=experts, cap=cap, cuts=row_cuts(rows)
        ),
        in_specs=[smem()] * 2 + [vmem()] * 16,
        out_specs=[vmem()] * 7,
        out_shape=[
            jax.ShapeDtypeStruct((length, features), F32),
            jax.ShapeDtypeStruct((length, LANES), F32),
            jax.ShapeDtypeStruct((1, features), F32),
            jax.ShapeDtypeStruct((LANES, features), F32),
            jax.ShapeDtypeStruct((groups * pairs, rows, LANES), F32),
            jax.ShapeDtypeStruct((groups * pairs, rows, LANES), BF),
            jax.ShapeDtypeStruct((2 * pairs, length, LANES), BF),
        ],
        compiler_params=params(16),
        name="mid",
        cost_estimate=cost(7),
    )(
        table, row_table, x1, gain.reshape(1, features), normed, upstream, *backs,
        row_ids, choices, router, attended, *owns, *fars,
    )


def block_out_body(
    slots_ref, x1_ref, gates_ref, back_a, back_b, ids_ref, out_ref, *, experts, cap
):
    length, features = x1_ref.shape
    half = cap // 2
    sums = [jnp.zeros((length, features), F32)] * 2
    for e in range(experts):
        hots = [
            jnp.where(hot, 1.0, 0.0).astype(BF) for hot in expert_hot(ids_ref, e, cap, length)
        ]
        for chain, back in enumerate((back_a, back_b)):
            got = back[slots_ref[chain * experts + e]]
            part = slice(chain * half, (chain + 1) * half)
            sums = [total + mm(hot[part], got, TN) for total, hot in zip(sums, hots)]
    moe = gates_ref[:, 0:1] * sums[0] + gates_ref[:, 1:2] * sums[1]
    out_ref[...] = (x1_ref[...] + moe).astype(BF)


def block_out_call(row_table, x1, gates, backs, row_ids, experts, cap):
    return pl.pallas_call(
        functools.partial(block_out_body, experts=experts, cap=cap),
        in_specs=[smem()] + [vmem()] * 5,
        out_specs=vmem(),
        out_shape=jax.ShapeDtypeStruct(x1.shape, BF),
        compiler_params=params(8),
        name="block_out",
        cost_estimate=cost(7),
    )(row_table, x1, gates, *backs, row_ids)


def attend_back_body(
    table_ref, normed_ref, heads_ref, probs_ref, grad_ref, out_keep_ref, out_send_ref,
    keep_q, keep_k, keep_v, send_q, send_k, send_v, dheads_ref, diag_ref,
    *, groups, pairs, head_dim, cuts,
):
    length, features = normed_ref.shape
    rows = features // groups
    keeps, sends = (keep_q, keep_k, keep_v), (send_q, send_k, send_v)
    for i in range(3):
        keeps[i][:, rows:] = out_keep_ref[:, cuts[i] : cuts[i + 1]]
        sends[i][:, rows:] = out_send_ref[:, cuts[i] : cuts[i + 1]]
    masks = lane_masks(head_dim)
    scale = head_dim**-0.5

    def back(w, carry):
        q, k, v = heads_ref[0, w], heads_ref[1, w], heads_ref[2, w]
        da = grad_ref[w]
        dq = jnp.zeros((length, LANES), F32)
        dk, dv = dq, dq
        for i, mask in enumerate(masks):
            head = w * len(masks) + i
            probs = probs_ref[head]
            dp = mm(jnp.where(mask, da, jnp.zeros_like(da)), v, NT)
            spread = jnp.sum(probs * dp, axis=-1, keepdims=True)
            ds = (probs * (dp - spread)).astype(BF)
            dq = jnp.where(mask, mm(ds, k), dq)
            dk = jnp.where(mask, mm(ds, q, TN), dk)
            dv = jnp.where(mask, mm(probs.astype(BF), da, TN), dv)
            wide_ds = jnp.concatenate([ds.astype(F32), jnp.zeros((length, length), F32)], axis=1)
            diag = jnp.zeros((8, 2 * length), F32)
            for g in range(length // 8):
                diag = diag + pltpu.roll(wide_ds[8 * g : 8 * g + 8], length - 1 - 8 * g, 1)
            diag_ref[head] = diag
        dheads_ref[0, w] = (dq * scale).astype(BF)
        dheads_ref[1, w] = (dk * scale).astype(BF)
        dheads_ref[2, w] = dv.astype(BF)
        return carry

    lax.fori_loop(0, 2 * pairs, back, 0)
    core = table_ref[0]

    def weigh(w2, carry):
        for m in range(3):
            both = jnp.concatenate(
                [dheads_ref[m, 2 * w2 + core], dheads_ref[m, 2 * w2 + 1 - core]], axis=1
            )
            for n in range(groups):
                at = table_ref[1 + (m * groups + n) * pairs + w2]
                block = mm(normed_ref[:, n * rows : (n + 1) * rows], both, TN)
                keeps[m][at, :rows] = block[:, :LANES]
                sends[m][at, :rows] = block[:, LANES:].astype(BF)
        return carry

    lax.fori_loop(0, pairs, weigh, 0)


def attend_back_call(
    table, normed, heads, probs, attended_grad, out_keep, out_send, groups, head_dim
):
    length, features = normed.shape
    pairs = features // (2 * LANES)
    head_count = features // head_dim
    rows = features // groups
    cuts = row_cuts(rows)
    body = functools.partial(
        attend_back_body, groups=groups, pairs=pairs, head_dim=head_dim, cuts=cuts
    )
    shapes = [(groups * pairs, rows + b - a, LANES) for a, b in zip(cuts[:-1], cuts[1:])]
    return pl.pallas_call(
        body,
        in_specs=[smem()] + [vmem()] * 6,
        out_specs=[vmem()] * 8,
        out_shape=[jax.ShapeDtypeStruct(shape, F32) for shape in shapes]
        + [jax.ShapeDtypeStruct(shape, BF) for shape in shapes]
        + [
            jax.ShapeDtypeStruct((3, 2 * pairs, length, LANES), BF),
            jax.ShapeDtypeStruct((head_count, 8, 2 * length), F32),
        ],
        compiler_params=params(22),
        name="attend_back",
        cost_estimate=cost(12),
    )(table, normed, heads, probs, attended_grad, out_keep, out_send)


def tokens_back_body(
    table_ref, tokens_ref, gain_ref, x1_grad_ref, dheads_ref,
    own_q, own_k, own_v, far_q, far_k, far_v,
    out_ref, gain_out_ref, acc_ref,
    *, groups, pairs,
):
    length, features = tokens_ref.shape
    rows = features // groups
    core = table_ref[0]
    for n in range(groups):

        def step(w2, total):
            for m, (own, far) in enumerate(((own_q, far_q), (own_k, far_k), (own_v, far_v))):
                at = table_ref[1 + (m * groups + n) * pairs + w2]
                both = jnp.concatenate(
                    [dheads_ref[m, 2 * w2 + core], dheads_ref[m, 2 * w2 + 1 - core]], axis=1
                )
                block = jnp.concatenate([own[at, :rows], far[at, :rows]], axis=1)
                total = total + mm(both, block, NT)
            return total

        total = lax.fori_loop(0, pairs, step, jnp.zeros((length, rows), F32))
        acc_ref[:, n * rows : (n + 1) * rows] = total
    x = tokens_ref[...].astype(F32)
    factor = lax.rsqrt(jnp.mean(x * x, axis=-1, keepdims=True) + NORM_EPS)
    hat = x * factor
    grad = acc_ref[...]
    gain_out_ref[...] = jnp.sum(grad * hat, axis=0, keepdims=True)
    scaled = grad * gain_ref[...]
    inner = jnp.mean(scaled * hat, axis=-1, keepdims=True)
    out_ref[...] = (x1_grad_ref[...] + factor * (scaled - hat * inner)).astype(BF)


def tokens_back_call(table, tokens, gain, x1_grad, dheads, gathered, groups):
    length, features = tokens.shape
    pairs = features // (2 * LANES)
    owns = [g[0] for g in gathered]
    fars = [g[1] for g in gathered]
    return pl.pallas_call(
        functools.partial(tokens_back_body, groups=groups, pairs=pairs),
        in_specs=[smem()] + [vmem()] * 10,
        out_specs=[vmem()] * 2,
        out_shape=[
            jax.ShapeDtypeStruct((length, features), BF),
            jax.ShapeDtypeStruct((1, features), F32),
        ],
        scratch_shapes=[pltpu.VMEM((length, features), F32)],
        compiler_params=params(30),
        name="tokens_back",
        cost_estimate=cost(10),
    )(table, tokens, gain.reshape(1, features), x1_grad, dheads, *owns, *fars)


def expert_body(expert_ref, *refs, count, apart):
    x_refs, up_refs, refs = refs[:count], refs[count:apart], refs[apart:]
    router_ref, gate_w, up_w, down_w = refs[:4]
    y_refs, dx_refs = refs[-2 * count - 6 : -count - 6], refs[-count - 6 : -6]
    x_out, dy_ref, hidden_ref, dgate_ref, dup_ref, up_scr = refs[-6:]
    piece = pl.program_id(0)
    features = x_out.shape[1]
    for i in range(count):

        @pl.when(piece == i)
        def _(i=i):
            x_out[...] = x_refs[i][:, :features]
            up_ref = up_refs[i] if up_refs else x_refs[i].at[:, features:]
            up_scr[...] = up_ref[...]

    x, up = x_out[...], up_scr[...]
    logits = mm(x, router_ref[...])
    lane = lax.broadcasted_iota(jnp.int32, logits.shape, 1)
    other_id = up[:, features : features + 1].astype(jnp.int32)
    mine = jnp.sum(jnp.where(lane == expert_ref[0], logits, 0.0), axis=1, keepdims=True)
    other = jnp.sum(jnp.where(lane == other_id, logits, 0.0), axis=1, keepdims=True)
    top = jnp.maximum(mine, other)
    mine_e = jnp.exp(mine - top)
    gate = mine_e / (mine_e + jnp.exp(other - top))
    grad = up[:, :features].astype(F32)
    dy = (gate * grad).astype(BF)
    dy_ref[...] = dy
    step = 2 * LANES
    width = gate_w.shape[0]
    for f in range(0, width, step):
        chunk = slice(f, min(f + step, width))
        g = mm(x, gate_w[chunk, :], NT)
        u = mm(x, up_w[chunk, :], NT)
        dh = mm(dy, down_w[chunk, :], NT)
        square = g * g
        t = jnp.tanh(g * (GELU_C + (GELU_C * GELU_A) * square))
        half_t = 0.5 + 0.5 * t
        act = g * half_t
        slope = half_t + act * ((1.0 - t) * (GELU_C + (3.0 * GELU_C * GELU_A) * square))
        hidden_ref[:, chunk] = (act * u).astype(BF)
        dgate_ref[:, chunk] = (dh * u * slope).astype(BF)
        dup_ref[:, chunk] = (dh * act).astype(BF)
    y = mm(hidden_ref[...], down_w[...]).astype(BF)
    dx = mm(dgate_ref[...], gate_w[...]) + mm(dup_ref[...], up_w[...])
    dot = jnp.sum(grad * y.astype(F32), axis=1, keepdims=True)
    dx = dx.astype(BF)
    dot = jnp.broadcast_to(dot, (x.shape[0], LANES)).astype(BF)
    for i in range(count):

        @pl.when(piece == i)
        def _(i=i):
            y_refs[i][...] = y
            dx_refs[i][:, :features] = dx
            dx_refs[i][:, features:] = dot


def expert_call(expert, xs, upstreams, router, gate_w, up_w, down_w, first, total, kept):
    rows, features = xs[0].shape[0], gate_w.shape[1]
    width = gate_w.shape[0]
    count = len(xs)

    def whole(arr):
        return pl.BlockSpec(arr.shape, lambda i, e: (0, 0), pipeline_mode=pl.Buffered(1))

    def kept_spec(cols):
        return pl.BlockSpec((rows, cols), lambda i, e: (first + i, 0))

    kept_cols = (features, features, width, width, width)
    kept_in = [] if kept is None else list(kept)
    inputs = list(xs) + list(upstreams) + [router, gate_w, up_w, down_w]
    out = pl.pallas_call(
        functools.partial(expert_body, count=count, apart=count + len(upstreams)),
        grid_spec=pltpu.PrefetchScalarGridSpec(
            num_scalar_prefetch=1,
            grid=(count,),
            in_specs=[whole(arr) for arr in inputs]
            + [pl.BlockSpec(memory_space=pl.ANY)] * len(kept_in),
            out_specs=[pl.BlockSpec((rows, features), lambda i, e: (0, 0))] * count
            + [pl.BlockSpec((rows, features + LANES), lambda i, e: (0, 0))] * count
            + [kept_spec(cols) for cols in kept_cols],
            scratch_shapes=[pltpu.VMEM((rows, features + LANES), BF)],
        ),
        out_shape=[jax.ShapeDtypeStruct((rows, features), BF)] * count
        + [jax.ShapeDtypeStruct((rows, features + LANES), BF)] * count
        + [jax.ShapeDtypeStruct((total, cols), BF) for cols in kept_cols],
        input_output_aliases={
            1 + len(inputs) + i: 2 * count + i for i in range(len(kept_in))
        },
        compiler_params=params(48),
        name="expert",
        cost_estimate=cost(20 if count == 4 else 1),
    )(expert, *inputs, *kept_in)
    return out[:count], out[count : 2 * count], out[2 * count :]


def expert_grad_body(left_ref, right_ref, out_ref):
    out_ref[...] = mm(left_ref[...], right_ref[...], TN)


def expert_grad_call(left, right):
    rows, features = right.shape
    width = left.shape[1]
    size = 2 * LANES
    return pl.pallas_call(
        expert_grad_body,
        grid=(features // size,),
        in_specs=[
            pl.BlockSpec((rows, width), lambda i: (0, 0)),
            pl.BlockSpec((rows, size), lambda i: (0, i)),
        ],
        out_specs=pl.BlockSpec((width, size), lambda i: (0, i)),
        out_shape=jax.ShapeDtypeStruct((width, features), F32),
        compiler_params=params(30),
        name="expert_grad",
        cost_estimate=cost(9),
    )(left, right)


def finish_body(
    table_ref, place_ref, own_q, own_k, own_v, far_q, far_k, far_v, *refs,
    groups, pairs, cuts, update,
):
    if update:
        mine_ref, weight_ref, refs = refs[0], refs[1], refs[2:]
    qkv_ref, out_ref, rows_ref, cols_ref = refs[:4]
    new_ref = refs[4] if update else None
    acc_ref, line_ref = refs[-2:]
    features = acc_ref.shape[0]
    rows = features // groups
    core = table_ref[0]
    chunk = 32

    def fill(grads_ref, source_of, n, start, stop, cols):
        def step(c, cols):
            first = pl.multiple_of(c * chunk, chunk)
            total = jnp.zeros((chunk, LANES), F32)
            grown = []
            for index in range(2 * pairs):
                w2, j = index // 2, index % 2
                block = source_of(n, w2, j, first).astype(F32)
                w = 2 * w2 + (core if j == 0 else 1 - core)
                place = pl.multiple_of(w * LANES, LANES)
                grads_ref[pl.ds(n * rows + first, chunk), pl.ds(place, LANES)] = block
                square = block * block
                total = total + square
                grown.append(cols[index] + jnp.sum(square.reshape(-1, 8, LANES), axis=0))
            acc_ref[pl.ds(n * rows + first, chunk), :] = total
            return tuple(grown)

        return lax.fori_loop(start // chunk, stop // chunk, step, cols, unroll=2)

    def matrix(m, grads_ref, pieces):
        cols = tuple(jnp.zeros((8, LANES), F32) for _ in range(2 * pairs))
        for n in range(groups):
            for chain, start, stop, shift, own, far in pieces:

                def source_of(n, w2, j, first, chain=chain, shift=shift, own=own, far=far):
                    at = table_ref[1 + (chain * groups + n) * pairs + w2]
                    ref = own if j == 0 else far
                    return ref[at, pl.ds(pl.multiple_of(first + shift, 16), chunk), :]

                cols = fill(grads_ref, source_of, n, start, stop, cols)
        for index in range(2 * pairs):
            w = 2 * (index // 2) + (core if index % 2 == 0 else 1 - core)
            total = jnp.sum(cols[index], axis=0, keepdims=True)
            cols_ref[0, w] = total / features + STAT_EPS
        squares = acc_ref[...]
        sums = lax.dot_general(
            jnp.ones((8, LANES), F32), squares, NT,
            precision=lax.Precision.HIGHEST, preferred_element_type=F32,
        )
        rows_ref[0] = sums / features + STAT_EPS
        if update:
            line = jnp.sum(squares, axis=1, keepdims=True) / features + STAT_EPS
            line_ref[...] = jnp.broadcast_to(line, line_ref.shape)
            mean = jnp.sum(line, axis=0, keepdims=True) / features
            my_rows = line_ref[pl.ds(pl.multiple_of(place_ref[0] * rows, rows), rows), :]
            my_cols = cols_ref[0, place_ref[1]]
            step = STEP_RATE * mine_ref[0] / jnp.sqrt(my_rows * my_cols / mean)
            new_ref[0] = weight_ref[0] - step if m < 3 else step

    owns, fars = (own_q, own_k, own_v), (far_q, far_k, far_v)
    for m in range(4):

        @pl.when(pl.program_id(0) == m)
        def _(m=m):
            if m < 3:
                matrix(m, qkv_ref.at[0], [(m, 0, rows, 0, owns[m], fars[m])])
            else:
                pieces = [
                    (i, cuts[i], cuts[i + 1], rows - cuts[i], owns[i], fars[i]) for i in range(3)
                ]
                matrix(m, out_ref, pieces)


def finish_call(table, place, gathered, groups, features, mine, weights):
    pairs = features // (2 * LANES)
    rows = features // groups
    owns = [g[0] for g in gathered]
    fars = [g[1] for g in gathered]
    update = mine is not None
    extra = [mine, weights] if update else []
    block = pl.BlockSpec((1, rows, LANES), lambda m: (m, 0, 0))
    shapes = [
        jax.ShapeDtypeStruct((3, features, features), F32),
        jax.ShapeDtypeStruct((features, features), F32),
        jax.ShapeDtypeStruct((4, 8, features), F32),
        jax.ShapeDtypeStruct((4, 2 * pairs, 1, LANES), F32),
    ]
    specs = [
        pl.BlockSpec((1, features, features), lambda m: (jnp.minimum(m, 2), 0, 0)),
        pl.BlockSpec((features, features), lambda m: (0, 0)),
        pl.BlockSpec((1, 8, features), lambda m: (m, 0, 0)),
        pl.BlockSpec((1, 2 * pairs, 1, LANES), lambda m: (m, 0, 0, 0)),
    ]
    if update:
        shapes.append(jax.ShapeDtypeStruct((4, rows, LANES), F32))
        specs.append(block)

    out = pl.pallas_call(
        functools.partial(
            finish_body, groups=groups, pairs=pairs, cuts=row_cuts(rows), update=update
        ),
        grid=(4,),
        in_specs=[smem()] * 2 + [vmem()] * 6 + [block] * len(extra),
        out_specs=specs,
        out_shape=shapes,
        scratch_shapes=[pltpu.VMEM((features, LANES), F32)] * 2,
        compiler_params=params(26),
        name="finish",
        cost_estimate=cost(10),
    )(table, place, *owns, *fars, *extra)
    stats = (out[0], out[1], out[2][:, 0], out[3].reshape(4, features))
    return stats + (out[4] if update else None,)


def on_device(
    tokens,
    attn_gain,
    qkv_weights,
    out_weight,
    rel_bias,
    moe_gain,
    router,
    gate_weight,
    up_weight,
    down_weight,
    expert_ids,
    expert_slots,
    buckets,
    upstream,
):
    length, features = tokens.shape
    bucket_count, head_count = rel_bias.shape
    head_dim = features // head_count
    groups = lax.axis_size("narrow")
    wide_count = lax.axis_size("wide")
    my_narrow = lax.axis_index("narrow")
    my_wide = lax.axis_index("wide")
    my_core = my_wide % 2
    part_width = gate_weight.shape[3]
    experts = router.shape[1] * wide_count
    places = experts // groups
    split_parts = wide_count // places
    capacity = (10 * length // experts + 3) // 4
    half_cap = capacity // 2
    row_count, col_count = qkv_weights.shape[1:]
    half_wide = wide_count // 2
    core_hop = ("wide", 0)
    part_hop = ("wide", 1)
    orders = hop_orders(groups, wide_count)
    slots = [block_slots(order, groups, wide_count) for order in orders]
    direct = col_count == LANES
    pairs = features // (2 * LANES)
    if direct:
        core_entry, tables = my_core, slots
    else:
        core_entry = jnp.int32(0)
        tables = [jnp.arange(groups * pairs, dtype=jnp.int32)] * 3
    table = jnp.concatenate(
        [jnp.reshape(core_entry, (1,)).astype(jnp.int32)] + [t.reshape(-1) for t in tables]
    )
    place = jnp.stack([my_narrow, my_wide]).astype(jnp.int32)

    def as_pairs(matrix):
        blocks = from_matrix(matrix, groups, pairs)
        return blocks.reshape((groups * pairs,) + blocks.shape[2:])

    def as_halves(owns, fars):
        if direct:
            return list(zip(owns, fars))
        out = []
        for own, far, slot in zip(owns, fars, slots):
            both = as_pairs(as_matrix(own, far, slot, my_core))
            out.append((both[:, 0], both[:, 1]))
        return out

    def halves_of(keep, send, chain):
        if direct:
            return keep, send
        rows = keep.shape[1]
        both = jnp.stack([keep, send.astype(F32)], axis=1).reshape(
            groups, pairs, 2, rows, LANES
        )
        matrix = jnp.transpose(both, (0, 3, 1, 2, 4)).reshape(groups * rows, features)
        parts = from_matrix(matrix, groups, half_wide)
        placed = jnp.zeros((groups * half_wide,) + parts.shape[2:], F32)
        placed = placed.at[slots[chain].reshape(-1)].set(parts.reshape(placed.shape))
        mine = jnp.where(my_core == 0, placed[:, 0], placed[:, 1])
        theirs = jnp.where(my_core == 0, placed[:, 1], placed[:, 0])
        return mine, theirs.astype(BF)

    def split_rows(values, ends):
        return [
            lax.slice_in_dim(values, a, b, axis=1) for a, b in zip([0] + ends[:-1], ends)
        ]

    narrow_hops = [("narrow", b) for b in range(groups.bit_length() - 1)]
    place_hops = [
        ("wide", b) for b in range(split_parts.bit_length() - 1, wide_count.bit_length() - 1)
    ][::-1]
    chains = (
        narrow_hops[:1] + place_hops + narrow_hops[1:],
        place_hops + narrow_hops[1:] + narrow_hops[:1],
    )
    hop_count = len(chains[0])
    row_table = jnp.concatenate(
        [row_slots(hops, groups, places, split_parts) for hops in chains]
    )
    back_hops = (chains[0][::-1], chains[0])
    back_table = jnp.concatenate(
        [row_slots(hops[::-1], groups, places, split_parts) for hops in back_hops]
    )
    owner_slot = expert_ids % groups * places + expert_ids // groups
    row_ids = jnp.where(expert_slots >= 0, owner_slot * capacity + expert_slots, -1).T

    def flat(rows):
        return rows.reshape(-1, rows.shape[-1])

    def sends(states, step):
        return [row_send(state, hops[step]) for state, hops in zip(states, chains)]

    def joins(states, gots):
        return [row_join(state, got) for state, got in zip(states, gots)]

    def to_core(values):
        return [from_partner(value, core_hop) for value in values]

    def to_part(values):
        return [from_partner(value, part_hop) for value in values]

    def add(a, b):
        return a.astype(F32) + b.astype(F32)

    def homeward(rows):
        return rows.astype(BF).reshape(-1, 1, half_cap, rows.shape[-1])

    def homeward_start(states):
        return [(state, list(hops)) for state, hops in zip(states, chains)]

    def backs_out(states, step):
        gots = {}
        for chain in range(2):
            at = step - chain
            if 0 <= at < hop_count:
                gots[chain] = back_send(*states[chain], back_hops[chain][at])
        return gots

    def backs_join(states, gots, step):
        return [
            back_join(*state, back_hops[chain][step - chain], gots[chain])
            if chain in gots
            else state
            for chain, state in enumerate(states)
        ]

    def slots_first(states):
        return [state.reshape((-1,) + state.shape[2:]) for state, _ in states]

    router_tail = router.astype(BF).reshape(-1, col_count)
    tail_rows = router_tail.shape[0]
    out_low = jnp.concatenate(
        [
            out_weight.astype(BF),
            router_tail,
            jnp.zeros((-tail_rows % 16, col_count), BF),
        ],
        axis=0,
    )
    qkv_low = qkv_weights.astype(BF)
    upstream_a, upstream_b = upstream_call(
        row_table, upstream, row_ids, expert_ids.T[::-1].astype(F32), experts, capacity
    )
    shared = shared_hops(orders)
    stages = range(shared, len(orders[0]) - 1)
    u_state = [upstream_a[None], upstream_b[None]]
    cuts = row_cuts(row_count)
    low_cuts = cuts[:3] + [out_low.shape[0]]
    pieces, ends = [], []
    for i in range(3):
        pieces += [qkv_low[i], out_low[low_cuts[i] : low_cuts[i + 1]]]
        ends.append(sum(piece.shape[0] for piece in pieces))
    blocks = jnp.concatenate(pieces, axis=0)[None]
    for hop in orders[0][:shared]:
        blocks = grow(blocks, from_partner(blocks, hop))
    u_state, blocks = together(u_state, blocks)
    u_got = sends(u_state, 0)
    dense = split_rows(blocks, ends)
    for count, stage in enumerate(stages):
        got = [from_partner(c, order[stage]) for c, order in zip(dense, orders)]
        if count == 1:
            u_got, got = together(u_got, got)
            u_state = joins(u_state, u_got)
            u_got = sends(u_state, 1)
        dense = [grow(c, g) for c, g in zip(dense, got)]
    dense_far = to_core(dense)
    weight_parts = as_halves(dense, dense_far)
    tails = [half[:, -(out_low.shape[0] - row_count) :][:, :tail_rows] for half in (dense[2], dense_far[2])]
    full_router = jnp.transpose(
        as_matrix(*tails, slots[2], my_core)
        .reshape(groups, tail_rows, wide_count, col_count)
        .transpose(0, 2, 1, 3)
        .reshape(groups, wide_count, row_count, router.shape[1]),
        (0, 2, 1, 3),
    ).reshape(features, experts)
    router_wide = jnp.pad(full_router, ((0, 0), (0, -experts % LANES)))
    gate_low = gate_weight[0, 0].T.astype(BF)
    up_low = up_weight[0, 0].T.astype(BF)
    down_low = down_weight[0, 0].astype(BF)
    table_hot = (
        jnp.pad(buckets, (0, 1), constant_values=-1)[:, None]
        == jnp.arange(bucket_count, dtype=jnp.int32)[None, :]
    ).astype(F32)
    bias_table = jnp.dot(table_hot, rel_bias, precision=lax.Precision.HIGHEST).T
    normed_in, heads, probs, attended = attend_call(
        table, tokens, attn_gain, bias_table, weight_parts, groups, head_dim
    )
    u_got, attended = together(u_got, attended)
    for step in range(2, hop_count):
        u_state = joins(u_state, u_got)
        u_got = sends(u_state, step)
    hidden_x1, moe_input, send_a, send_b = post_call(
        table, row_table, tokens, attended, weight_parts, moe_gain, row_ids, groups, experts,
        capacity,
    )
    u_got, send_a, send_b = together(u_got, send_a, send_b)
    u_own = [flat(state) for state in joins(u_state, u_got)]
    u_core, u_part = to_core(u_own), to_part(u_own[:1])
    x_state = [send_a[None], send_b[None]]
    for step in range(hop_count):
        x_got = sends(x_state, step)
        if step == 0:
            x_got, u_core, u_part[0], router_wide = together(
                x_got, u_core, u_part[0], router_wide
            )
        else:
            x_got = together(*x_got)
        x_state = joins(x_state, x_got)
    late_parts, _ = together(weight_parts, send_a)
    projection_parts = [tuple(half[:, row_count:] for half in part) for part in late_parts]
    projection_parts, x_state = together(projection_parts, x_state)
    x_own = [flat(state) for state in x_state]
    x_core, x_part = to_core(x_own), to_part(x_own[:1])
    joined_part = from_partner(jnp.concatenate([x_own[1], u_own[1]], axis=1), part_hop)

    my_expert = (my_narrow + groups * (my_wide // split_parts)).reshape(1).astype(jnp.int32)
    row_total = 8 * x_own[0].shape[0]

    def run_expert(xs, us, first, kept):
        return expert_call(
            my_expert, xs, us, router_wide, gate_low, up_low, down_low, first, row_total, kept
        )

    y_near, dx_near, kept = run_expert(x_own + x_core, u_own + u_core, 0, None)
    x_part[0], u_part[0], dx_near = together(x_part[0], u_part[0], dx_near)
    dx_near_got = to_core(dx_near[2:])
    y_far, parts_back = [], []
    for chain in range(2):
        if chain:
            joined_part, y_far = together(joined_part, y_far)
            xs = [joined_part, from_partner(joined_part, core_hop)]
            us = []
        else:
            xs = [x_part[0], from_partner(x_part[0], core_hop)]
            us = [u_part[0], from_partner(u_part[0], core_hop)]
        y_two, dx_two, kept = run_expert(xs, us, 4 + 2 * chain, kept)
        if chain:
            y_two, dx_two, kept, parts_back[0] = together(y_two, dx_two, kept, parts_back[0])
        y_far.append(y_two)
        far_got = from_partner(dx_two[1], core_hop)
        far_sum = add(dx_two[0], far_got).astype(BF)
        if not chain:
            kept, far_sum = together(kept, far_sum)
        parts_back.append(from_partner(far_sum, part_hop))
    kept, far_sum = together(kept, far_sum)
    y_near_got = to_core(y_near[2:])
    y_far_got = to_core([two[1] for two in y_far])

    def home_sum(chain, part):
        near = add(dx_near[chain], dx_near_got[chain])
        return homeward(near + part.astype(F32))

    x_all, dy_all, hidden_all, dgate_all, dup_all = kept
    states = homeward_start([home_sum(0, parts_back[0]), None])
    for step in range(hop_count + 1):
        gots = backs_out(states, step)
        if step == 0:
            gate_local = expert_grad_call(dgate_all, x_all)
            up_local = expert_grad_call(dup_all, x_all)
            gots, part_b, gate_local, up_local, hidden_all = together(
                gots, parts_back[1], gate_local, up_local, hidden_all
            )
            states[1] = (home_sum(1, part_b), list(chains[1]))
        elif step == 1:
            down_local = expert_grad_call(hidden_all, dy_all)
            y_sums = [add(mine, got).astype(BF) for mine, got in zip(y_near[:2], y_near_got)]
            y_far_sums = [
                add(two[0], got).astype(BF) for two, got in zip(y_far, y_far_got)
            ]
            gots, down_local, y_sums, y_far_sums = together(
                gots, down_local, y_sums, y_far_sums
            )
            y_part_got = to_part(y_far_sums[:1])
        elif step == 2:
            squares = [g * g for g in (gate_local, up_local, down_local)]
            local_sums = jnp.stack([jnp.sum(q, axis=0) for q in squares], axis=0)
            part_stats = jnp.stack([jnp.mean(q, axis=1) for q in squares], axis=0) + STAT_EPS
            sums_got = from_partner(local_sums, core_hop)
            gots, local_sums, y_part_got, sums_got = together(
                gots, local_sums, y_part_got, sums_got
            )
        elif step == 3:
            sums_got, y_far_sums = together(sums_got, y_far_sums)
            local_sums = local_sums + sums_got
            sums_got = from_partner(local_sums, part_hop)
            sums_got, y_far_sums = together(sums_got, y_far_sums)
            y_part_got = y_part_got + to_part(y_far_sums[1:])
            wide_stats = (local_sums + sums_got) / (part_width * split_parts) + STAT_EPS
            gate_new = factored(
                gate_weight[0, 0].T, gate_local, part_stats[0], wide_stats[0],
                jnp.mean(wide_stats[0]),
            )
            up_new = factored(
                up_weight[0, 0].T, up_local, part_stats[1], wide_stats[1],
                jnp.mean(wide_stats[1]),
            )
            down_new = factored(
                down_weight[0, 0], down_local, part_stats[2], wide_stats[2],
                jnp.mean(wide_stats[2]),
            )
            gots, gate_new, up_new, down_new, wide_stats = together(
                gots, gate_new, up_new, down_new, wide_stats
            )
        else:
            gots = together(gots)[0]
        states = backs_join(states, gots, step)
    inputs_back = slots_first(states)
    y_home = homeward(add(y_sums[0], y_part_got[0]))
    inputs_back, y_home = together(inputs_back, y_home)
    y_states = homeward_start([y_home, None])
    y_gots = backs_out(y_states, 0)

    x1_grad, gates, moe_gain_local, router_local, out_keep, out_send, attended_grad = mid_call(
        table, back_table, hidden_x1, moe_gain, moe_input, upstream, inputs_back, row_ids,
        expert_ids, router_wide, attended, projection_parts, groups, experts, capacity,
    )
    y_part_got, y_gots, attended_grad, out_send = together(
        y_part_got, y_gots, attended_grad, out_send
    )
    y_states = backs_join(y_states, y_gots, 0)
    y_states[1] = (homeward(add(y_sums[1], y_part_got[1])), list(chains[1]))
    y_gots = backs_out(y_states, 1)

    *grads, dheads, diag = attend_back_call(
        table, normed_in, heads, probs, attended_grad, out_keep, out_send, groups, head_dim
    )
    halves = [halves_of(grads[i], grads[3 + i], i) for i in range(3)]
    addends = [[keep, from_partner(send, core_hop)] for keep, send in halves]
    ends, size = [], 0
    for value, _ in addends:
        size += value.shape[1]
        ends.append(size)
    y_step = 1
    router_local, moe_gain_local, dheads, x1_grad, diag, _ = together(
        router_local, moe_gain_local, dheads, x1_grad, diag, addends
    )

    def halve(values, hop):
        half = values[0].shape[0] // 2
        send = sum(value[half:].astype(F32) for value in values).astype(BF)
        return [value[:half] for value in values], from_partner(send, hop)

    def more_outputs():
        joined = backs_join(y_states, y_gots, y_step)
        return joined, backs_out(joined, y_step + 1), y_step + 1

    small_hops = list(orders[0])
    for count, stage in enumerate(stages[::-1]):
        halved = [halve(values, order[stage]) for values, order in zip(addends, orders)]
        gots = [got for _, got in halved]
        if count == 0:
            tokens_grad, attn_gain_local = tokens_back_call(
                table, tokens, attn_gain, x1_grad, dheads, weight_parts, groups
            )
            tail = jnp.pad(diag, ((0, 0), (0, 0), (0, 8)))
            line = sum(tail[:, i, i : i + 2 * length] for i in range(8))
            bias_local = jnp.dot(line, table_hot, precision=lax.Precision.HIGHEST)
            small = jnp.concatenate(
                [
                    attn_gain_local.reshape(-1),
                    moe_gain_local.reshape(-1),
                    bias_local.reshape(-1),
                    router_local[:experts].reshape(-1),
                ]
            ).reshape(-1, LANES)
            gots, small, y_gots = together(gots, small, y_gots)
            y_states, y_gots, y_step = more_outputs()
        else:
            small_got = from_partner(small, small_hops.pop(0))
            if y_gots:
                gots, small_got, y_gots = together(gots, small_got, y_gots)
                y_states, y_gots, y_step = more_outputs()
            else:
                gots, small_got = together(gots, small_got)
            small = small + small_got
        addends = [kept + [got] for (kept, _), got in zip(halved, gots)]
    summed = [sum(value.astype(F32) for value in values) for values in addends]
    while y_gots:
        y_states, y_gots, y_step = more_outputs()
    def small_beside(value, others):
        if not small_hops:
            return value, together(*others)
        got = from_partner(value, small_hops.pop(0))
        out = together(got, *others)
        return value + out[0], out[1:]

    total = jnp.concatenate(summed, axis=1)
    for hop in orders[0][:shared][::-1]:
        got = halve_send(total, hop)
        small, (got, y_states) = small_beside(small, (got, y_states))
        total = halve_add(total, got)
    block_out = block_out_call(
        back_table, hidden_x1, gates, slots_first(y_states), row_ids, experts, capacity
    )
    blocks = total.astype(BF)
    for hop in orders[0][:shared]:
        got = from_partner(blocks, hop)
        small, (got, total, block_out) = small_beside(small, (got, total, block_out))
        blocks = grow(blocks, got)
    pieces = split_rows(total, ends)
    dense_mine = jnp.concatenate(
        [piece[:, :row_count] for piece in pieces]
        + [jnp.concatenate([piece[:, row_count:] for piece in pieces], axis=1)],
        axis=0,
    )
    dense_weights = jnp.concatenate([qkv_weights, out_weight[None]], axis=0)
    dense = split_rows(blocks, ends)
    router_size = features * experts
    for count, stage in enumerate(stages):
        gots = [from_partner(chain, order[stage]) for chain, order in zip(dense, orders)]
        if count == 0:
            small, (gots,) = small_beside(small, (gots,))
            small, small_hops = cube_sum(small, small_hops), []
        elif count == 1:
            small, (gots, dense_mine, dense_weights) = small_beside(
                small, (gots, dense_mine, dense_weights)
            )
        else:
            gots, router_out = together(gots, router_out)
        if count == 0:
            router_total = small.reshape(-1)[-router_size:].reshape(experts, features)
            router_sq = router_total * router_total
            router_rows = jnp.mean(router_sq, axis=0) + STAT_EPS
            router_cols = jnp.mean(router_sq, axis=1) + STAT_EPS
            rows_first, cols_first = my_narrow * router.shape[0], my_wide * router.shape[1]
            router_new = factored(
                router.T,
                lax.dynamic_slice(router_total, (cols_first, rows_first), router.T.shape),
                lax.dynamic_slice_in_dim(router_cols, cols_first, router.shape[1], 0),
                lax.dynamic_slice_in_dim(router_rows, rows_first, router.shape[0], 0),
                jnp.mean(router_rows),
            )
            small_flat = small.reshape(-1)
            router_out = (
                small_flat[:features],
                small_flat[features : 2 * features],
                small_flat[2 * features : -router_size].reshape(head_count, bucket_count),
                router_total, router_new, router_rows, router_cols,
            )
        dense = [grow(chain, got) for chain, got in zip(dense, gots)]
    gain_a_total, gain_m_total, bias_total, router_total, router_new, router_rows, router_cols = (
        router_out
    )
    dense_parts = as_halves(dense, to_core(dense))
    qkv_total, out_total, rows, cols, dense_new = finish_call(
        table, place, dense_parts, groups, features, dense_mine if direct else None,
        dense_weights,
    )
    if not direct:
        rows_mine = lax.dynamic_slice_in_dim(rows, my_narrow * row_count, row_count, 1)
        cols_mine = lax.dynamic_slice_in_dim(cols, my_wide * col_count, col_count, 1)
        step = adafactor_step(dense_mine, rows_mine, cols_mine, jnp.mean(rows, axis=1))
        dense_new = jnp.concatenate([qkv_weights - step[:3], step[3:]], axis=0)
    qkv_stats = jnp.stack([rows[:3], cols[:3]], axis=0)
    out_stats = jnp.concatenate([rows[3:], cols[3:]], axis=0)
    return (
        block_out,
        tokens_grad,
        gain_a_total,
        qkv_total,
        out_total,
        bias_total.T,
        gain_m_total,
        router_total.T,
        gate_local.T[None, None],
        up_local.T[None, None],
        down_local[None, None],
        dense_new[:3],
        dense_new[3],
        router_new.T,
        gate_new.T[None, None],
        up_new.T[None, None],
        down_new[None, None],
        qkv_stats,
        out_stats,
        router_rows,
        router_cols,
        wide_stats[None, None],
        part_stats[None, None],
    )


def solution(mesh):
    in_specs = (
        P(("narrow", "wide"), None),
        P(),
        P(None, "narrow", "wide"),
        P("narrow", "wide"),
        P(),
        P(),
        P("narrow", "wide"),
        P("narrow", "wide", None, None),
        P("narrow", "wide", None, None),
        P("narrow", "wide", None, None),
        P(("narrow", "wide"), None),
        P(("narrow", "wide"), None),
        P(),
        P(("narrow", "wide"), None),
    )
    out_specs = (
        P(("narrow", "wide"), None),
        P(("narrow", "wide"), None),
        P(),
        P(),
        P(),
        P(),
        P(),
        P(),
        P("narrow", "wide", None, None),
        P("narrow", "wide", None, None),
        P("narrow", "wide", None, None),
        P(None, "narrow", "wide"),
        P("narrow", "wide"),
        P("narrow", "wide"),
        P("narrow", "wide", None, None),
        P("narrow", "wide", None, None),
        P("narrow", "wide", None, None),
        P(),
        P(),
        P(),
        P(),
        P("narrow", "wide", None, None),
        P("narrow", "wide", None, None),
    )
    return jax.shard_map(
        on_device, mesh=mesh, in_specs=in_specs, out_specs=out_specs, check_vma=False
    )
```
